32 devices in a mesh: dp: 4 (over z), ctx: 8 (over y, x, core).
Axes of the slice: x: 2, y: 2, z: 4, core: 2. Of those that a mesh axis runs over, the one named last changes fastest.
Arguments:
- features: bfloat16 [4, 1024, 4096], P('dp', 'ctx'), may hold values from -6 to 6
- short_weights: float32 [3, 3, 4096], replicated, may hold values from -3.5 to 3.5
- filters: bfloat16 [512, 256], replicated, may hold values from -0.25 to 0.25
- reach_panels: int32 [256], replicated, may hold values from 1 to 4, as said below
- cotangent: bfloat16 [4, 1024, 4096], P('dp', 'ctx'), may hold values from -6 to 6
Outputs:
- layer_out: bfloat16 [4, 1024, 4096], P('dp', 'ctx')
- input_grad: bfloat16 [4, 1024, 4096], P('dp', 'ctx')
- filter_grad: float32 [512, 256], replicated
- short_grad: float32 [3, 3, 4096], replicated
The draws below stay inside these ranges and needn't reach their ends.
Inputs may be any that keep to these rules, and one draw needn't show every extreme that they name: `reach_panels`: each group's reach counts panels of 128 positions; some group reaches 4.
All inputs are finite; a program needn't handle non-finite values.
Results may differ from the reference program's by a relative error of at most 0.0051.
Values may be sent and summed in bfloat16 or wider, within the bound.
A program may use at most 128 MiB of HBM per device.

```python
import jax
import jax.numpy as jnp
from jax import lax

C = 4096
GROUPS = 256
PANEL = 128
RMAX = 4
FILTER_LEN = 512
TOKENS = 1024
SEQS = 4


def draw_reach_panels(key, part):
    first, second = jax.random.split(jax.random.fold_in(key, 11))
    values = jax.random.randint(first, (GROUPS,), 1, RMAX + 1)
    chosen = jax.random.randint(second, (), 0, GROUPS)
    return jnp.where(jnp.arange(GROUPS) == chosen, RMAX, values).astype(jnp.int32)


def steps_of(stream_key, shape, shards, least, high):
    def one(dim, shards_of):
        steps = jax.random.uniform(jax.random.fold_in(jax.random.fold_in(stream_key, 6), dim), (shards_of,), jnp.float32, least / len(shards), high / len(shards))
        return jnp.repeat(jnp.exp(steps), shape[dim] // shards_of).reshape((-1,) + (1,) * (len(shape) - dim - 1))

    level = one(*shards[0])
    for cut in shards[1:]:
        level = level * one(*cut)
    return level


def centred(own_key, dims, deviation, most, cuts=(), kind=jnp.bfloat16):
    level = steps_of(own_key, dims, cuts, -0.22, 0.18) if cuts else 1.0
    values = jax.random.normal(own_key, dims, jnp.float32) * deviation * level
    return jnp.minimum(jnp.maximum(values, -most), most).astype(kind)


def setup_inputs(seed: int = 0) -> dict:
    seeds = jax.random.split(jax.random.key(seed), 6)
    return {
        "features": centred(seeds[0], (SEQS, TOKENS, C), 1.0, 6.0, ((0, 4), (1, 8))),
        "short_weights": centred(seeds[1], (3, 3, C), 3 ** -0.5, 3.5, (), jnp.float32),
        "filters": centred(seeds[2], (FILTER_LEN, GROUPS), FILTER_LEN ** -0.5, 0.25),
        "reach_panels": draw_reach_panels(jax.random.fold_in(seeds[5], 71), 0),
        "cotangent": centred(seeds[4], (SEQS, TOKENS, C), 1.0, 6.0, ((0, 4), (1, 8))),
    }


def short_conv(extended, tap_weights):
    length = extended.shape[1] - 2
    return (tap_weights[0] * extended[:, 2:, :] + tap_weights[1] * extended[:, 1:length + 1, :]
            + tap_weights[2] * extended[:, :length, :])


def toeplitz_block(masked_t, offset, panel_rows):
    filter_len = masked_t.shape[1]
    lag_index = (offset * panel_rows + lax.broadcasted_iota(jnp.int32, (panel_rows, panel_rows), 0)
                 - lax.broadcasted_iota(jnp.int32, (panel_rows, panel_rows), 1))
    inside = (lag_index >= 0) & (lag_index < filter_len)
    picked = jnp.take(masked_t, jnp.clip(lag_index, 0, filter_len - 1), axis=1)
    return jnp.where(inside[None, :, :], picked, jnp.zeros((), masked_t.dtype))


def lag_sums(blocks):
    groups, panel_rows = blocks.shape[0], blocks.shape[1]
    flipped = blocks[:, :, ::-1]
    padded = jnp.pad(flipped, ((0, 0), (0, 0), (0, panel_rows)))
    flattened = padded.reshape(groups, 2 * panel_rows * panel_rows)[:, :panel_rows * (2 * panel_rows - 1)]
    return jnp.sum(flattened.reshape(groups, panel_rows, 2 * panel_rows - 1), axis=1)


def reference(features, short_weights, filters, reach_panels, cotangent):
    filter_len, groups = filters.shape
    length, channels = features.shape[1], features.shape[2]
    panels = length // PANEL
    lag_pos = lax.broadcasted_iota(jnp.int32, (filter_len, groups), 0)
    keep = lag_pos < reach_panels[None, :] * PANEL
    masked = jnp.where(keep, filters, jnp.zeros((), filters.dtype))
    masked_t = masked.T
    toeplitz_all = [toeplitz_block(masked_t, offset, PANEL).astype(jnp.float32) for offset in range(RMAX)]

    def one_sequence(carry, inputs):
        accum, short_acc = carry
        seq_feat, seq_cot = inputs
        extended = jnp.pad(seq_feat.astype(jnp.float32)[None], ((0, 0), (2, 0), (0, 0)))
        queries = short_conv(extended, short_weights[0])[0]
        key_feat = short_conv(extended, short_weights[1])[0]
        value_feat = short_conv(extended, short_weights[2])[0]
        mixed = (key_feat * value_feat).astype(jnp.bfloat16)
        cot_float = seq_cot.astype(jnp.float32)
        grad_conv = (cot_float * queries).astype(jnp.bfloat16)
        mixed_split = mixed.astype(jnp.float32).reshape(panels, PANEL, groups, 16)
        grad_split = grad_conv.astype(jnp.float32).reshape(panels, PANEL, groups, 16)
        total = jnp.zeros(mixed_split.shape, jnp.float32)
        back = jnp.zeros(mixed_split.shape, jnp.float32)
        for offset in range(RMAX):
            earlier = jnp.pad(mixed_split, ((offset, 0), (0, 0), (0, 0), (0, 0)))[:panels]
            later = jnp.pad(grad_split, ((0, offset), (0, 0), (0, 0), (0, 0)))[offset:]
            total = total + jnp.einsum('gts,nsgc->ntgc', toeplitz_all[offset], earlier)
            back = back + jnp.einsum('gts,ntgc->nsgc', toeplitz_all[offset], later)
            products = jnp.einsum('ntgc,nsgc->gts', grad_split, earlier)
            accum = accum.at[:, offset * PANEL + 1:offset * PANEL + 2 * PANEL].add(lag_sums(products))
        conv_out = total.reshape(length, channels)
        out_seq = (queries * conv_out).astype(jnp.bfloat16)
        grad_query = cot_float * conv_out
        grad_mixed = back.reshape(length, channels)
        stacked = jnp.stack([grad_query, grad_mixed * value_feat, grad_mixed * key_feat])
        after = jnp.pad(stacked, ((0, 0), (0, 2), (0, 0)))
        grad_in = jnp.zeros((length, channels), jnp.float32)
        for stream in range(3):
            for tap in range(3):
                grad_in = grad_in + short_weights[stream, tap] * after[stream, tap:tap + length]
        short_part = jnp.stack([jnp.stack([jnp.sum(stacked[stream] * extended[0, 2 - tap:2 - tap + length], axis=0)
                                           for tap in range(3)]) for stream in range(3)])
        return (accum, short_acc + short_part), (out_seq, grad_in.astype(jnp.bfloat16))

    start = (jnp.zeros((groups, filter_len + 2 * PANEL), jnp.float32), jnp.zeros((3, 3, channels), jnp.float32))
    (accum, short_grad), (layer_out, input_grad) = lax.scan(one_sequence, start, (features, cotangent))
    filter_grad = jnp.where(keep, accum[:, PANEL:PANEL + filter_len].T, jnp.zeros((), jnp.float32))
    return layer_out, input_grad, filter_grad, short_grad
```

```python
import functools

import jax
import jax.numpy as jnp
from jax import lax
from jax.experimental import pallas as pl
from jax.experimental.pallas import tpu as pltpu
from jax.sharding import PartitionSpec as P

PANEL = 128
UNIT = 16
TILE = 128
TAPS = 3
UNROLL = 4
MESH = pl.DeviceIdType.MESH


def rows_down(x, rows):
    return jnp.concatenate([jnp.zeros((rows, x.shape[1]), x.dtype), x[:-rows]], axis=0)


def rows_up(x, rows):
    return jnp.concatenate([x[rows:], jnp.zeros((rows, x.shape[1]), x.dtype)], axis=0)


def causal():
    shape = (PANEL, PANEL)
    return lax.broadcasted_iota(jnp.int32, shape, 1) >= lax.broadcasted_iota(jnp.int32, shape, 0)


def toeplitz(taps):
    width = taps.shape[1]
    x = jnp.broadcast_to(taps, (8, width))
    row = lax.broadcasted_iota(jnp.int32, (8, width), 0)
    for bit in (1, 2, 4):
        x = jnp.where((row & bit) != 0, pltpu.roll(x, bit, 1), x)
    rows = 8
    while rows < PANEL:
        x = jnp.concatenate([x, pltpu.roll(x, rows, 1)], axis=0)
        rows *= 2
    first = jnp.where(causal(), x[:, :PANEL], 0.0)
    return jnp.concatenate([first, x[:, PANEL:]], axis=1).astype(jnp.bfloat16)


def lag_sums(products):
    width = products.shape[1]
    first = jnp.where(causal(), products[:, :PANEL], 0.0)
    x = jnp.concatenate([first, products[:, PANEL:]], axis=1)
    rows = PANEL // 2
    while rows >= 8:
        x = x[:rows] + pltpu.roll(x[rows:], width - rows, 1)
        rows //= 2
    for step in (4, 2, 1):
        x = x + pltpu.roll(pltpu.roll(x, 8 - step, 0), width - step, 1)
    return x[0:1]


def tile_terms(reach, panels, ft, ct, wt, spreads, out_t, in_t, fg, sg_t):
    rows = panels * UNIT

    def group(g, carry):
        first = pl.multiple_of(g * UNIT, UNIT)
        lane = lax.broadcasted_iota(jnp.int32, (rows, PANEL), 1)
        chan = pl.ds(first, UNIT)
        feat = ft[:, chan, :].reshape(rows, PANEL)
        cot = ct[:, chan, :].reshape(rows, PANEL)
        w_all = wt[chan, :]

        def weigh(k, x):
            w = jnp.broadcast_to(w_all[:, k : k + 1], (UNIT, PANEL))
            return (x.reshape(panels, UNIT, PANEL) * w[None]).reshape(rows, PANEL)

        feats = [feat]
        for tap in range(1, TAPS):
            turned = pltpu.roll(feat, tap, 1)
            feats.append(jnp.where(lane < tap, rows_down(turned, UNIT), turned))
        streams = []
        for m in range(3):
            total = weigh(m * TAPS, feats[0])
            for tap in range(1, TAPS):
                total = total + weigh(m * TAPS + tap, feats[tap])
            streams.append(total)
        query, key, value = streams
        mixed = (key * value).astype(jnp.bfloat16)
        grad_conv = (cot * query).astype(jnp.bfloat16)
        earlier = jnp.concatenate(
            [mixed] + [rows_down(mixed, o * UNIT) for o in range(1, reach)], axis=1
        )
        later = jnp.concatenate(
            [grad_conv] + [rows_up(grad_conv, o * UNIT) for o in range(1, reach)], axis=1
        )
        spread = spreads[g]
        stacked = jnp.concatenate(
            [spread[:, o * PANEL : (o + 1) * PANEL] for o in range(reach)], axis=0
        )
        conv = jnp.dot(earlier, stacked, preferred_element_type=jnp.float32)
        back = lax.dot_general(
            later, spread, (((1,), (1,)), ((), ())), preferred_element_type=jnp.float32
        )
        products = lax.dot_general(
            mixed, later, (((0,), (0,)), ((), ())), preferred_element_type=jnp.float32
        )
        fg[pl.ds(g, 1), :] = lag_sums(products)
        out_t[:, chan, :] = (query * conv).reshape(panels, UNIT, PANEL)
        grads = (cot * conv, back * value, back * key)
        grad_in = None
        for tap in range(TAPS):
            part = weigh(tap, grads[0]) + weigh(TAPS + tap, grads[1]) + weigh(2 * TAPS + tap, grads[2])
            if tap:
                turned = pltpu.roll(part, PANEL - tap, 1)
                part = jnp.where(lane >= PANEL - tap, rows_up(turned, UNIT), turned)
            grad_in = part if grad_in is None else grad_in + part
        in_t[:, chan, :] = grad_in.reshape(panels, UNIT, PANEL)
        small_lane = lax.broadcasted_iota(jnp.int32, (UNIT, PANEL), 1)
        sums = jnp.zeros((UNIT, PANEL), jnp.float32)
        for m in range(3):
            for tap in range(TAPS):
                part = jnp.sum((grads[m] * feats[tap]).reshape(panels, UNIT, PANEL), axis=0)
                sums = jnp.where(small_lane == m * TAPS + tap, jnp.sum(part, axis=1, keepdims=True), sums)
        sg_t[chan, :] = sums
        return carry

    lax.fori_loop(0, TILE // UNIT, group, 0, unroll=UNROLL)


def layer_kernel(
    reach, ndp, nctx, f_hbm, c_hbm, sw_hbm, fl_hbm, rp_hbm, out_hbm, in_hbm, all_hbm,
    sw, fl, rp, wrow, wt, taps, small_sem, arrived, leaving, spreads, ft, ct, out_t, in_t, fg, sg_t, pay, parts, sums,
    own_sem, in_send, in_recv, out_send, out_recv, keep_sem,
    rs_send, rs_recv, gd_send, gd_recv, gd_own, gc_send, gc_recv,
):
    dp, me = lax.axis_index("dp"), lax.axis_index("ctx")
    width = arrived.shape[3]
    tiles = width // TILE
    chunk = sums.shape[1]
    ins, outs = (f_hbm, c_hbm), (out_hbm, in_hbm)

    def ctx_peer(k):
        return lax.rem(me + k, nctx)

    def dp_peer(k):
        return lax.rem(dp + k, ndp)

    def lanes(j):
        return pl.ds(pl.multiple_of(j * TILE, TILE), TILE)

    def cols(owner, j):
        return pl.ds(pl.multiple_of(owner * width + j * TILE, TILE), TILE)

    def copy(src, dst, send, recv, device):
        return pltpu.make_async_remote_copy(
            src_ref=src, dst_ref=dst, send_sem=send, recv_sem=recv, device_id=device, device_id_type=MESH
        )

    def in_copy(a, j, k, slot):
        return copy(
            ins[a].at[:, cols(ctx_peer(k), j)],
            arrived.at[a, slot, :, lanes(j)],
            in_send.at[a, j, k],
            in_recv.at[a, j, k],
            (dp, ctx_peer(k)),
        )

    def in_own(a, j):
        return pltpu.make_async_copy(
            ins[a].at[:, cols(me, j)], arrived.at[a, me, :, lanes(j)], own_sem.at[a, j]
        )

    def out_copy(a, j, k, slot):
        return copy(
            leaving.at[a, ctx_peer(k), :, lanes(j)],
            outs[a].at[:, cols(slot, j)],
            out_send.at[a, j, k],
            out_recv.at[a, j, k],
            (dp, ctx_peer(k)),
        )

    def out_own(a, j):
        return pltpu.make_async_copy(
            leaving.at[a, me, :, lanes(j)], outs[a].at[:, cols(me, j)], keep_sem.at[a, j]
        )

    def rs_copy(j, k):
        return copy(
            pay.at[j, dp_peer(k)], parts.at[j, k], rs_send.at[j, k], rs_recv.at[j, k], (dp_peer(k), me)
        )

    def gc_copy(j, k, slot):
        return copy(
            sums.at[j], all_hbm.at[j, dp, slot], gc_send.at[j, k], gc_recv.at[j, k], (dp, ctx_peer(k))
        )

    def gc_keep(j):
        return pltpu.make_async_copy(sums.at[j], all_hbm.at[j, dp, me], gd_own.at[j])

    def gd_copy(j, k, slot):
        return copy(
            all_hbm.at[j, dp], all_hbm.at[j, slot], gd_send.at[j, k], gd_recv.at[j, k], (dp_peer(k), me)
        )

    def each(count, body, unroll=1):
        def step(i, carry):
            body(i)
            return carry

        lax.fori_loop(0, count, step, 0, unroll=unroll)

    small = [
        pltpu.make_async_copy(src, dst, small_sem.at[i])
        for i, (src, dst) in enumerate(((sw_hbm, sw), (fl_hbm, fl), (rp_hbm, rp)))
    ]
    for one in small:
        one.start()
    barrier = pltpu.get_barrier_semaphore()
    for k in range(1, nctx):
        pl.semaphore_signal(barrier, inc=1, device_id=(dp, ctx_peer(k)), device_id_type=MESH)
    for k in range(1, ndp):
        pl.semaphore_signal(barrier, inc=1, device_id=(dp_peer(k), me), device_id_type=MESH)
    for a in range(2):
        each(tiles, lambda j: in_own(a, j).start())
    pl.semaphore_wait(barrier, nctx + ndp - 2)

    def send_in(j):
        for a in range(2):
            each(nctx - 1, lambda i: in_copy(a, j, i + 1, me).start())

    ahead = min(2, tiles)
    each(ahead, send_in)
    for one in small:
        one.wait()
    units = taps.shape[0]
    group = me * units
    block = pl.ds(pl.multiple_of(group // PANEL * PANEL, PANEL), PANEL)
    lag_pos = lax.broadcasted_iota(jnp.int32, (fl.shape[0], PANEL), 0)
    masked = jnp.where(lag_pos < rp[:, block] * PANEL, fl[:, block].astype(jnp.float32), 0.0)
    masked = pltpu.roll(masked, lax.rem(PANEL - lax.rem(group, PANEL), PANEL), 1)
    for o in range(reach):
        taps[:, o * PANEL : (o + 1) * PANEL] = masked[o * PANEL : (o + 1) * PANEL].T[:units]
    wrow[...] = jnp.zeros_like(wrow)

    def turn_weights(j):
        for m in range(3):
            wrow[m * TAPS : (m + 1) * TAPS] = sw[m, :, cols(me, j)]
        wt[lanes(j), :] = wrow[...].T

    each(tiles, turn_weights)

    def build(g):
        spreads[g] = toeplitz(taps[pl.ds(g, 1), :])

    each(taps.shape[0], build, UNROLL)

    def spread_ctx(j):
        each(ndp - 1, lambda i: rs_copy(j, i + 1).wait_recv())
        total = pay[j, dp]
        for k in range(1, ndp):
            total = total + parts[j, k]
        sums[j] = total.astype(jnp.bfloat16)
        gc_keep(j).start()
        each(nctx - 1, lambda i: gc_copy(j, i + 1, me).start())

    def spread_dp(j):
        gc_keep(j).wait()
        each(nctx - 1, lambda i: gc_copy(j, i + 1, lax.rem(me + nctx - i - 1, nctx)).wait_recv())
        each(ndp - 1, lambda i: gd_copy(j, i + 1, dp).start())

    def one_tile(j):
        for a in range(2):
            in_own(a, j).wait()
            each(
                nctx - 1,
                lambda i: in_copy(a, j, i + 1, lax.rem(me + nctx - i - 1, nctx)).wait_recv(),
            )

        @pl.when(j + ahead < tiles)
        def _():
            send_in(j + ahead)

        def turn_in(n):
            ft[n] = arrived[0, n, :, lanes(j)].astype(jnp.float32).T
            ct[n] = arrived[1, n, :, lanes(j)].astype(jnp.float32).T

        each(nctx, turn_in, UNROLL)
        units = TILE // UNIT
        tile_terms(
            reach, nctx, ft, ct, wt.at[lanes(j), :],
            spreads.at[pl.ds(j * units, units)], out_t, in_t, fg, sg_t,
        )

        def turn_out(n):
            leaving[0, n, :, lanes(j)] = out_t[n].T.astype(jnp.bfloat16)
            leaving[1, n, :, lanes(j)] = in_t[n].T.astype(jnp.bfloat16)

        each(nctx, turn_out, UNROLL)
        rows = [fg[:, o * PANEL : (o + 1) * PANEL] for o in range(reach)] + [sg_t[...].T[:UNIT]]
        filled = reach * units + UNIT
        if filled < ndp * chunk:
            rows.append(jnp.zeros((ndp * chunk - filled, PANEL), jnp.float32))
        pay[j] = jnp.concatenate(rows, axis=0).reshape(ndp, chunk, PANEL)
        each(ndp - 1, lambda i: rs_copy(j, i + 1).start())
        for a in range(2):
            out_own(a, j).start()
            each(nctx - 1, lambda i: out_copy(a, j, i + 1, me).start())

        @pl.when(j >= 1)
        def _():
            spread_ctx(j - 1)

        @pl.when(j >= 2)
        def _():
            spread_dp(j - 2)

    each(tiles, one_tile)
    if tiles >= 2:
        spread_dp(tiles - 2)
    spread_ctx(tiles - 1)
    spread_dp(tiles - 1)

    def finish(j):
        for a in range(2):
            each(nctx - 1, lambda i: in_copy(a, j, i + 1, me).wait_send())
            out_own(a, j).wait()
            each(nctx - 1, lambda i: out_copy(a, j, i + 1, me).wait_send())
            each(
                nctx - 1,
                lambda i: out_copy(a, j, i + 1, lax.rem(me + nctx - i - 1, nctx)).wait_recv(),
            )
        each(ndp - 1, lambda i: rs_copy(j, i + 1).wait_send())
        each(nctx - 1, lambda i: gc_copy(j, i + 1, me).wait_send())
        each(ndp - 1, lambda i: gd_copy(j, i + 1, dp).wait_send())
        each(ndp - 1, lambda i: gd_copy(j, i + 1, lax.rem(dp + ndp - i - 1, ndp)).wait_recv())

    each(tiles, finish)


def finish_kernel(reach, ndp, nctx, out_in, grad_in, every, rp, out_out, grad_out, fg, sg, sem):
    moves = [
        pltpu.make_async_copy(src, dst, sem.at[i])
        for i, (src, dst) in enumerate(((out_in, out_out), (grad_in, grad_out)))
    ]
    for one in moves:
        one.start()
    tiles = every.shape[0]
    units = TILE // UNIT
    lag_rows = [[] for _ in range(reach)]
    for n in range(nctx):
        for j in range(tiles):
            terms = every[j, :, n].astype(jnp.float32).reshape(-1, PANEL)
            for o in range(reach):
                lag_rows[o].append(terms[o * units : (o + 1) * units])
            first = (n * tiles + j) * TILE
            for m in range(3):
                row = reach * units + m * TAPS
                sg[m, :, first : first + TILE] = terms[row : row + TAPS]
    lag_pos = lax.broadcasted_iota(jnp.int32, (PANEL, fg.shape[1]), 0)
    for o in range(reach):
        sums = jnp.concatenate(lag_rows[o], axis=0).T
        fg[o * PANEL : (o + 1) * PANEL] = jnp.where(lag_pos + o * PANEL < rp[...] * PANEL, sums, 0.0)
    for one in moves:
        one.wait()


def shards(ndp, nctx, features, short_weights, filters, reach_panels, cotangent):
    filter_len, groups = filters.shape
    channels = features.shape[2]
    reach = filter_len // PANEL
    rows = features.shape[1]
    assert rows == PANEL and features.shape[0] == 1
    width = channels // nctx
    tiles = width // TILE
    units = width // UNIT
    tile_units = TILE // UNIT
    reach_row = reach_panels.reshape(1, groups)
    filled = reach * tile_units + UNIT
    chunk = -(-filled // (UNIT * ndp)) * UNIT
    hbm = pl.BlockSpec(memory_space=pltpu.HBM)
    vmem = pl.BlockSpec(memory_space=pltpu.VMEM)
    dma = pltpu.SemaphoreType.DMA
    turned = pltpu.VMEM((nctx, TILE, PANEL), jnp.float32)
    layer_out, input_grad, every = pl.pallas_call(
        functools.partial(layer_kernel, reach, ndp, nctx),
        in_specs=[hbm] * 5,
        out_specs=[hbm, hbm, hbm],
        out_shape=[
            jax.ShapeDtypeStruct((rows, channels), jnp.bfloat16),
            jax.ShapeDtypeStruct((rows, channels), jnp.bfloat16),
            jax.ShapeDtypeStruct((tiles, ndp, nctx, chunk, PANEL), jnp.bfloat16),
        ],
        scratch_shapes=[
            pltpu.VMEM((3, TAPS, channels), jnp.float32),
            pltpu.VMEM((filter_len, groups), jnp.bfloat16),
            pltpu.VMEM((1, groups), jnp.int32),
            pltpu.VMEM((UNIT, PANEL), jnp.float32),
            pltpu.VMEM((width, UNIT), jnp.float32),
            pltpu.VMEM((units, filter_len), jnp.float32),
            dma((3,)),
            pltpu.VMEM((2, nctx, PANEL, width), jnp.bfloat16),
            pltpu.VMEM((2, nctx, PANEL, width), jnp.bfloat16),
            pltpu.VMEM((units, PANEL, filter_len), jnp.bfloat16),
            turned,
            turned,
            turned,
            turned,
            pltpu.VMEM((tile_units, filter_len), jnp.float32),
            pltpu.VMEM((TILE, PANEL), jnp.float32),
            pltpu.VMEM((tiles, ndp, chunk, PANEL), jnp.float32),
            pltpu.VMEM((tiles, ndp, chunk, PANEL), jnp.float32),
            pltpu.VMEM((tiles, chunk, PANEL), jnp.bfloat16),
            dma((2, tiles)),
            dma((2, tiles, nctx)),
            dma((2, tiles, nctx)),
            dma((2, tiles, nctx)),
            dma((2, tiles, nctx)),
            dma((2, tiles)),
            dma((tiles, ndp)),
            dma((tiles, ndp)),
            dma((tiles, ndp)),
            dma((tiles, ndp)),
            dma((tiles,)),
            dma((tiles, nctx)),
            dma((tiles, nctx)),
        ],
        compiler_params=pltpu.CompilerParams(
            collective_id=0, has_side_effects=True, vmem_limit_bytes=58 * 2**20
        ),
    )(features[0], cotangent[0], short_weights, filters, reach_row)
    layer_out, input_grad, filter_grad, short_grad = pl.pallas_call(
        functools.partial(finish_kernel, reach, ndp, nctx),
        in_specs=[hbm, hbm, vmem, vmem],
        out_specs=[hbm, hbm, vmem, vmem],
        out_shape=[
            jax.ShapeDtypeStruct((rows, channels), jnp.bfloat16),
            jax.ShapeDtypeStruct((rows, channels), jnp.bfloat16),
            jax.ShapeDtypeStruct((filter_len, groups), jnp.float32),
            jax.ShapeDtypeStruct((3, TAPS, channels), jnp.float32),
        ],
        scratch_shapes=[dma((2,))],
    )(layer_out, input_grad, every, reach_row)
    return (layer_out[None], input_grad[None], filter_grad, short_grad)


def solution(mesh):
    return jax.shard_map(
        functools.partial(shards, mesh.shape["dp"], mesh.shape["ctx"]),
        mesh=mesh,
        in_specs=(P("dp", "ctx", None), P(), P(), P(), P("dp", "ctx", None)),
        out_specs=(P("dp", "ctx", None), P("dp", "ctx", None), P(), P()),
        check_vma=False,
    )
```

```python
import functools

import jax
import jax.numpy as jnp
from jax import lax
from jax.experimental import pallas as pl
from jax.experimental.pallas import tpu as pltpu
from jax.sharding import PartitionSpec as P

PANEL = 128
UNIT = 16
TILE = 128
TAPS = 3
UNROLL = 4
STRIPS = 4
AROUND = 8
MESH = pl.DeviceIdType.MESH


def rows_down(x, rows):
    return jnp.concatenate([jnp.zeros((rows, x.shape[1]), x.dtype), x[:-rows]], axis=0)


def rows_up(x, rows):
    return jnp.concatenate([x[rows:], jnp.zeros((rows, x.shape[1]), x.dtype)], axis=0)


def turn(place, count):
    return jnp.where(place >= count, place - count, place)


def causal():
    shape = (PANEL, PANEL)
    return lax.broadcasted_iota(jnp.int32, shape, 1) >= lax.broadcasted_iota(jnp.int32, shape, 0)


def toeplitz(taps):
    width = taps.shape[1]
    x = jnp.broadcast_to(taps, (8, width))
    row = lax.broadcasted_iota(jnp.int32, (8, width), 0)
    for bit in (1, 2, 4):
        x = jnp.where((row & bit) != 0, pltpu.roll(x, bit, 1), x)
    rows = 8
    while rows < PANEL:
        x = jnp.concatenate([x, pltpu.roll(x, rows, 1)], axis=0)
        rows *= 2
    first = jnp.where(causal(), x[:, :PANEL], 0.0)
    return jnp.concatenate([first, x[:, PANEL:]], axis=1).astype(jnp.bfloat16)


def lag_sums(products):
    width = products.shape[1]
    first = jnp.where(causal(), products[:, :PANEL], 0.0)
    x = jnp.concatenate([first, products[:, PANEL:]], axis=1)
    rows = PANEL // 2
    while rows >= 8:
        x = x[:rows] + pltpu.roll(x[rows:], width - rows, 1)
        rows //= 2
    for step in (4, 2, 1):
        x = x + pltpu.roll(pltpu.roll(x, 8 - step, 0), width - step, 1)
    return x[0:1]


def tile_terms(reach, panels, ft, ct, wt, spreads, out_t, in_t, fg, sg_t):
    rows = panels * UNIT

    def group(g, carry):
        first = pl.multiple_of(g * UNIT, UNIT)
        lane = lax.broadcasted_iota(jnp.int32, (rows, PANEL), 1)
        chan = pl.ds(first, UNIT)
        feat = ft[:, chan, :].reshape(rows, PANEL)
        cot = ct[:, chan, :].reshape(rows, PANEL)
        w_all = wt[chan, :]

        def weigh(k, x):
            w = jnp.broadcast_to(w_all[:, k : k + 1], (UNIT, PANEL))
            return (x.reshape(panels, UNIT, PANEL) * w[None]).reshape(rows, PANEL)

        feats = [feat]
        for tap in range(1, TAPS):
            turned = pltpu.roll(feat, tap, 1)
            feats.append(jnp.where(lane < tap, rows_down(turned, UNIT), turned))
        streams = []
        for m in range(3):
            total = weigh(m * TAPS, feats[0])
            for tap in range(1, TAPS):
                total = total + weigh(m * TAPS + tap, feats[tap])
            streams.append(total)
        query, key, value = streams
        mixed = (key * value).astype(jnp.bfloat16)
        grad_conv = (cot * query).astype(jnp.bfloat16)
        earlier = jnp.concatenate(
            [mixed] + [rows_down(mixed, o * UNIT) for o in range(1, reach)], axis=1
        )
        later = jnp.concatenate(
            [grad_conv] + [rows_up(grad_conv, o * UNIT) for o in range(1, reach)], axis=1
        )
        spread = spreads[g]
        stacked = jnp.concatenate(
            [spread[:, o * PANEL : (o + 1) * PANEL] for o in range(reach)], axis=0
        )
        conv = jnp.dot(earlier, stacked, preferred_element_type=jnp.float32)
        back = lax.dot_general(
            later, spread, (((1,), (1,)), ((), ())), preferred_element_type=jnp.float32
        )
        products = lax.dot_general(
            mixed, later, (((0,), (0,)), ((), ())), preferred_element_type=jnp.float32
        )
        fg[pl.ds(g, 1), :] = lag_sums(products)
        out_t[:, chan, :] = (query * conv).reshape(panels, UNIT, PANEL)
        grads = (cot * conv, back * value, back * key)
        grad_in = None
        for tap in range(TAPS):
            part = weigh(tap, grads[0]) + weigh(TAPS + tap, grads[1]) + weigh(2 * TAPS + tap, grads[2])
            if tap:
                turned = pltpu.roll(part, PANEL - tap, 1)
                part = jnp.where(lane >= PANEL - tap, rows_up(turned, UNIT), turned)
            grad_in = part if grad_in is None else grad_in + part
        in_t[:, chan, :] = grad_in.reshape(panels, UNIT, PANEL)
        small_lane = lax.broadcasted_iota(jnp.int32, (UNIT, PANEL), 1)
        sums = jnp.zeros((UNIT, PANEL), jnp.float32)
        for m in range(3):
            for tap in range(TAPS):
                part = jnp.sum((grads[m] * feats[tap]).reshape(panels, UNIT, PANEL), axis=0)
                sums = jnp.where(small_lane == m * TAPS + tap, jnp.sum(part, axis=1, keepdims=True), sums)
        sg_t[chan, :] = sums
        return carry

    lax.fori_loop(0, TILE // UNIT, group, 0, unroll=UNROLL)


def layer_kernel(
    reach, ndp, nctx, f_hbm, c_hbm, sw_hbm, fl_hbm, rp_hbm, out_hbm, in_hbm, fg_hbm, sg_hbm,
    every, fg_all, sg_all, last_sem, sw, fl, rp, wrow, wt, taps, small_sem, arrived, leaving, spreads, ft, ct, out_t, in_t, fg, sg_t, pay, parts, sums,
    own_sem, in_send, in_recv, out_send, out_recv, keep_sem,
    rs_send, rs_recv, gd_send, gd_recv, gd_own, gc_send, gc_recv,
):
    dp, me = lax.axis_index("dp"), lax.axis_index("ctx")
    width = arrived.shape[3]
    tiles = width // TILE
    chunk = sums.shape[1]
    ins, outs = (f_hbm, c_hbm), (out_hbm, in_hbm)

    def ctx_peer(k):
        return turn(me + k, nctx)

    def ctx_from(k):
        return turn(me + nctx - k, nctx)

    def dp_peer(k):
        return turn(dp + k, ndp)

    def dp_from(k):
        return turn(dp + ndp - k, ndp)

    def lanes(j):
        return pl.ds(pl.multiple_of(j * TILE, TILE), TILE)

    def cols(owner, j):
        return pl.ds(pl.multiple_of(owner * width + j * TILE, TILE), TILE)

    def copy(src, dst, send, recv, device):
        return pltpu.make_async_remote_copy(
            src_ref=src, dst_ref=dst, send_sem=send, recv_sem=recv, device_id=device, device_id_type=MESH
        )

    def in_copy(a, j, k, slot):
        return copy(
            ins[a].at[:, cols(ctx_peer(k), j)],
            arrived.at[a, slot, :, lanes(j)],
            in_send.at[a, j, k],
            in_recv.at[a, j, k],
            (dp, ctx_peer(k)),
        )

    def in_own(a, j):
        return pltpu.make_async_copy(
            ins[a].at[:, cols(me, j)], arrived.at[a, me, :, lanes(j)], own_sem.at[a, j]
        )

    def out_copy(a, j, k, slot):
        return copy(
            leaving.at[a, ctx_peer(k), :, lanes(j)],
            outs[a].at[:, cols(slot, j)],
            out_send.at[a, j, k],
            out_recv.at[a, j, k],
            (dp, ctx_peer(k)),
        )

    def out_own(a, j):
        return pltpu.make_async_copy(
            leaving.at[a, me, :, lanes(j)], outs[a].at[:, cols(me, j)], keep_sem.at[a, j]
        )

    def rs_copy(j, k):
        return copy(
            pay.at[j, dp_peer(k)], parts.at[j, k], rs_send.at[j, k], rs_recv.at[j, k], (dp_peer(k), me)
        )

    def gc_copy(j, k, slot):
        return copy(
            sums.at[j], every.at[j, dp, slot], gc_send.at[j, k], gc_recv.at[j, k], (dp, ctx_peer(k))
        )

    def gc_keep(j):
        return pltpu.make_async_copy(sums.at[j], every.at[j, dp, me], gd_own.at[j])

    def gd_copy(j, k, slot):
        return copy(
            every.at[j, dp], every.at[j, slot], gd_send.at[j, k], gd_recv.at[j, k], (dp_peer(k), me)
        )

    def each(count, body, unroll=1):
        unroll = max(1, min(unroll, count))

        def step(i, carry):
            body(i)
            return carry

        lax.fori_loop(0, count, step, 0, unroll=unroll)

    small = [
        pltpu.make_async_copy(src, dst, small_sem.at[i])
        for i, (src, dst) in enumerate(((sw_hbm, sw), (fl_hbm, fl), (rp_hbm, rp)))
    ]
    for one in small:
        one.start()
    barrier = pltpu.get_barrier_semaphore()
    for k in range(1, nctx):
        pl.semaphore_signal(barrier, inc=1, device_id=(dp, ctx_peer(k)), device_id_type=MESH)
    for k in range(1, ndp):
        pl.semaphore_signal(barrier, inc=1, device_id=(dp_peer(k), me), device_id_type=MESH)
    for a in range(2):
        each(tiles, lambda j: in_own(a, j).start())
    pl.semaphore_wait(barrier, nctx + ndp - 2)

    def send_in(j):
        for a in range(2):
            each(nctx - 1, unroll=AROUND, body=lambda i: in_copy(a, j, i + 1, me).start())

    ahead = min(2, tiles)
    each(ahead, send_in)
    for one in small:
        one.wait()
    units = taps.shape[0]
    group = me * units
    block = pl.ds(pl.multiple_of(group // PANEL * PANEL, PANEL), PANEL)
    lag_pos = lax.broadcasted_iota(jnp.int32, (fl.shape[0], PANEL), 0)
    masked = jnp.where(lag_pos < rp[:, block] * PANEL, fl[:, block].astype(jnp.float32), 0.0)
    masked = pltpu.roll(masked, lax.rem(PANEL - lax.rem(group, PANEL), PANEL), 1)
    for o in range(reach):
        taps[:, o * PANEL : (o + 1) * PANEL] = masked[o * PANEL : (o + 1) * PANEL].T[:units]
    wrow[...] = jnp.zeros_like(wrow)

    def turn_weights(j):
        for m in range(3):
            wrow[m * TAPS : (m + 1) * TAPS] = sw[m, :, cols(me, j)]
        wt[lanes(j), :] = wrow[...].T

    each(tiles, turn_weights)

    def build(g):
        spreads[g] = toeplitz(taps[pl.ds(g, 1), :])

    each(taps.shape[0], build, UNROLL)

    def spread_ctx(j):
        each(ndp - 1, unroll=AROUND, body=lambda i: rs_copy(j, i + 1).wait_recv())
        total = pay[j, dp]
        for k in range(1, ndp):
            total = total + parts[j, k]
        sums[j] = total.astype(jnp.bfloat16)
        gc_keep(j).start()
        each(nctx - 1, unroll=AROUND, body=lambda i: gc_copy(j, i + 1, me).start())

    def spread_dp(j):
        gc_keep(j).wait()
        each(nctx - 1, unroll=AROUND, body=lambda i: gc_copy(j, i + 1, ctx_from(i + 1)).wait_recv())
        each(ndp - 1, unroll=AROUND, body=lambda i: gd_copy(j, i + 1, dp).start())

    def send_out(a, j):
        out_own(a, j).start()
        each(nctx - 1, unroll=AROUND, body=lambda i: out_copy(a, j, i + 1, me).start())

    def one_tile(j):
        for a in range(2):
            in_own(a, j).wait()
            each(
                nctx - 1,
                unroll=AROUND,
                body=lambda i: in_copy(a, j, i + 1, ctx_from(i + 1)).wait_recv(),
            )

        @pl.when(j + ahead < tiles)
        def _():
            send_in(j + ahead)

        def turn_in(n):
            ft[n] = arrived[0, n, :, lanes(j)].astype(jnp.float32).T
            ct[n] = arrived[1, n, :, lanes(j)].astype(jnp.float32).T

        each(nctx, turn_in, UNROLL)
        units = TILE // UNIT
        tile_terms(
            reach, nctx, ft, ct, wt.at[lanes(j), :],
            spreads.at[pl.ds(j * units, units)], out_t, in_t, fg, sg_t,
        )

        def turn_out(n):
            leaving[0, n, :, lanes(j)] = out_t[n].T.astype(jnp.bfloat16)
            leaving[1, n, :, lanes(j)] = in_t[n].T.astype(jnp.bfloat16)

        each(nctx, turn_out, UNROLL)
        rows = [fg[:, o * PANEL : (o + 1) * PANEL] for o in range(reach)] + [sg_t[...].T[:UNIT]]
        filled = reach * units + UNIT
        if filled < ndp * chunk:
            rows.append(jnp.zeros((ndp * chunk - filled, PANEL), jnp.float32))
        pay[j] = jnp.concatenate(rows, axis=0).reshape(ndp, chunk, PANEL)
        each(ndp - 1, unroll=AROUND, body=lambda i: rs_copy(j, i + 1).start())

        @pl.when(j >= 1)
        def _():
            spread_ctx(j - 1)

        @pl.when(j >= 2)
        def _():
            spread_dp(j - 2)

        @pl.when(j < tiles - 1)
        def _():
            send_out(0, j)
            send_out(1, j)

        @pl.when(j == tiles - 1)
        def _():
            spread_ctx(j)
            send_out(0, j)
            if tiles >= 2:
                spread_dp(j - 1)
            spread_dp(j)
            send_out(1, j)

    each(tiles, one_tile)

    def sums_in(j):
        each(ndp - 1, unroll=AROUND, body=lambda i: gd_copy(j, i + 1, dp_from(i + 1)).wait_recv())

    each(tiles, sums_in)
    lag_rows = [[] for _ in range(reach)]
    width_units = TILE // UNIT
    for n in range(nctx):
        for j in range(tiles):
            terms = every[j, :, n].astype(jnp.float32).reshape(-1, PANEL)
            for o in range(reach):
                lag_rows[o].append(terms[o * width_units : (o + 1) * width_units])
            first = (n * tiles + j) * TILE
            for m in range(3):
                row = reach * width_units + m * TAPS
                sg_all[m, :, first : first + TILE] = terms[row : row + TAPS]
    lag_pos = lax.broadcasted_iota(jnp.int32, (PANEL, fg_all.shape[1]), 0)
    for o in range(reach):
        lags = jnp.concatenate(lag_rows[o], axis=0).T
        fg_all[o * PANEL : (o + 1) * PANEL] = jnp.where(lag_pos + o * PANEL < rp[...] * PANEL, lags, 0.0)
    last = [
        pltpu.make_async_copy(src, dst, last_sem.at[i])
        for i, (src, dst) in enumerate(((fg_all, fg_hbm), (sg_all, sg_hbm)))
    ]
    for one in last:
        one.start()

    def finish(j):
        for a in range(2):
            each(nctx - 1, unroll=AROUND, body=lambda i: in_copy(a, j, i + 1, me).wait_send())
            out_own(a, j).wait()
            each(nctx - 1, unroll=AROUND, body=lambda i: out_copy(a, j, i + 1, me).wait_send())
            each(
                nctx - 1,
                unroll=AROUND,
                body=lambda i: out_copy(a, j, i + 1, ctx_from(i + 1)).wait_recv(),
            )
        each(ndp - 1, unroll=AROUND, body=lambda i: rs_copy(j, i + 1).wait_send())
        each(nctx - 1, unroll=AROUND, body=lambda i: gc_copy(j, i + 1, me).wait_send())
        each(ndp - 1, unroll=AROUND, body=lambda i: gd_copy(j, i + 1, dp).wait_send())

    each(tiles, finish)
    for one in last:
        one.wait()


def finish_kernel(*refs):
    sources, targets, holds, (get_sem, put_sem) = refs[:4], refs[4:8], refs[8:12], refs[12:]
    fetches, moves = [], []
    for i in range(STRIPS):
        for a, (src, hold, dst) in enumerate(zip(sources, holds, targets)):
            if len(src.shape) == 2:
                strip = src.shape[0] // STRIPS
                part = pl.ds(i * strip, strip)
            elif i < src.shape[0]:
                part = i
            else:
                continue
            fetches.append(pltpu.make_async_copy(src.at[part], hold.at[part], get_sem.at[a, i]))
            moves.append(pltpu.make_async_copy(hold.at[part], dst.at[part], put_sem.at[a, i]))
    for one in fetches:
        one.start()
    for fetch, move in zip(fetches, moves):
        fetch.wait()
        move.start()
    for one in moves:
        one.wait()


def shards(ndp, nctx, features, short_weights, filters, reach_panels, cotangent):
    filter_len, groups = filters.shape
    channels = features.shape[2]
    reach = filter_len // PANEL
    rows = features.shape[1]
    assert rows == PANEL and features.shape[0] == 1
    width = channels // nctx
    tiles = width // TILE
    units = width // UNIT
    tile_units = TILE // UNIT
    reach_row = reach_panels.reshape(1, groups)
    filled = reach * tile_units + UNIT
    chunk = -(-filled // (UNIT * ndp)) * UNIT
    hbm = pl.BlockSpec(memory_space=pltpu.HBM)
    dma = pltpu.SemaphoreType.DMA
    turned = pltpu.VMEM((nctx, TILE, PANEL), jnp.float32)
    results = [
        jax.ShapeDtypeStruct((rows, channels), jnp.bfloat16),
        jax.ShapeDtypeStruct((rows, channels), jnp.bfloat16),
        jax.ShapeDtypeStruct((filter_len, groups), jnp.float32),
        jax.ShapeDtypeStruct((3, TAPS, channels), jnp.float32),
    ]
    held = pl.pallas_call(
        functools.partial(layer_kernel, reach, ndp, nctx),
        in_specs=[hbm] * 5,
        out_specs=[hbm] * 4,
        out_shape=results,
        scratch_shapes=[
            pltpu.VMEM((tiles, ndp, nctx, chunk, PANEL), jnp.bfloat16),
            pltpu.VMEM((filter_len, groups), jnp.float32),
            pltpu.VMEM((3, TAPS, channels), jnp.float32),
            dma((2,)),
            pltpu.VMEM((3, TAPS, channels), jnp.float32),
            pltpu.VMEM((filter_len, groups), jnp.bfloat16),
            pltpu.VMEM((1, groups), jnp.int32),
            pltpu.VMEM((UNIT, PANEL), jnp.float32),
            pltpu.VMEM((width, UNIT), jnp.float32),
            pltpu.VMEM((units, filter_len), jnp.float32),
            dma((3,)),
            pltpu.VMEM((2, nctx, PANEL, width), jnp.bfloat16),
            pltpu.VMEM((2, nctx, PANEL, width), jnp.bfloat16),
            pltpu.VMEM((units, PANEL, filter_len), jnp.bfloat16),
            turned,
            turned,
            turned,
            turned,
            pltpu.VMEM((tile_units, filter_len), jnp.float32),
            pltpu.VMEM((TILE, PANEL), jnp.float32),
            pltpu.VMEM((tiles, ndp, chunk, PANEL), jnp.float32),
            pltpu.VMEM((tiles, ndp, chunk, PANEL), jnp.float32),
            pltpu.VMEM((tiles, chunk, PANEL), jnp.bfloat16),
            dma((2, tiles)),
            dma((2, tiles, nctx)),
            dma((2, tiles, nctx)),
            dma((2, tiles, nctx)),
            dma((2, tiles, nctx)),
            dma((2, tiles)),
            dma((tiles, ndp)),
            dma((tiles, ndp)),
            dma((tiles, ndp)),
            dma((tiles, ndp)),
            dma((tiles,)),
            dma((tiles, nctx)),
            dma((tiles, nctx)),
        ],
        compiler_params=pltpu.CompilerParams(
            collective_id=0, has_side_effects=True, vmem_limit_bytes=58 * 2**20
        ),
    )(features[0], cotangent[0], short_weights, filters, reach_row)
    layer_out, input_grad, filter_grad, short_grad = pl.pallas_call(
        finish_kernel,
        in_specs=[hbm] * 4,
        out_specs=[hbm] * 4,
        out_shape=results,
        scratch_shapes=[pltpu.VMEM(one.shape, one.dtype) for one in results] + [dma((4, STRIPS))] * 2,
    )(*held)
    return (layer_out[None], input_grad[None], filter_grad, short_grad)


def solution(mesh):
    return jax.shard_map(
        functools.partial(shards, mesh.shape["dp"], mesh.shape["ctx"]),
        mesh=mesh,
        in_specs=(P("dp", "ctx", None), P(), P(), P(), P("dp", "ctx", None)),
        out_specs=(P("dp", "ctx", None), P("dp", "ctx", None), P(), P()),
        check_vma=False,
    )
```

```python
import functools

import jax
import jax.numpy as jnp
from jax import lax
from jax.experimental import pallas as pl
from jax.experimental.pallas import tpu as pltpu
from jax.sharding import PartitionSpec as P

PANEL = 128
UNIT = 16
TILE = 128
TAPS = 3
UNROLL = 4
STRIPS = 4
AROUND = 8
MESH = pl.DeviceIdType.MESH


def rows_down(x, rows):
    return jnp.concatenate([jnp.zeros((rows, x.shape[1]), x.dtype), x[:-rows]], axis=0)


def rows_up(x, rows):
    return jnp.concatenate([x[rows:], jnp.zeros((rows, x.shape[1]), x.dtype)], axis=0)


def turn(place, count):
    return jnp.where(place >= count, place - count, place)


def causal():
    shape = (PANEL, PANEL)
    return lax.broadcasted_iota(jnp.int32, shape, 1) >= lax.broadcasted_iota(jnp.int32, shape, 0)


def toeplitz(taps):
    width = taps.shape[1]
    x = jnp.broadcast_to(taps, (8, width))
    row = lax.broadcasted_iota(jnp.int32, (8, width), 0)
    for bit in (1, 2, 4):
        x = jnp.where((row & bit) != 0, pltpu.roll(x, bit, 1), x)
    rows = 8
    while rows < PANEL:
        x = jnp.concatenate([x, pltpu.roll(x, rows, 1)], axis=0)
        rows *= 2
    first = jnp.where(causal(), x[:, :PANEL], 0.0)
    return jnp.concatenate([first, x[:, PANEL:]], axis=1).astype(jnp.bfloat16)


def lag_sums(products):
    width = products.shape[1]
    first = jnp.where(causal(), products[:, :PANEL], 0.0)
    x = jnp.concatenate([first, products[:, PANEL:]], axis=1)
    rows = PANEL // 2
    while rows >= 8:
        x = x[:rows] + pltpu.roll(x[rows:], width - rows, 1)
        rows //= 2
    for step in (4, 2, 1):
        x = x + pltpu.roll(pltpu.roll(x, 8 - step, 0), width - step, 1)
    return x[0:1]


def tile_terms(reach, panels, ft, ct, wt, spreads, out_t, in_t, fg, sg_t):
    rows = panels * UNIT

    def group(g, carry):
        first = pl.multiple_of(g * UNIT, UNIT)
        lane = lax.broadcasted_iota(jnp.int32, (rows, PANEL), 1)
        chan = pl.ds(first, UNIT)
        feat = ft[:, chan, :].reshape(rows, PANEL)
        cot = ct[:, chan, :].reshape(rows, PANEL)
        w_all = wt[chan, :]

        def weigh(k, x):
            w = jnp.broadcast_to(w_all[:, k : k + 1], (UNIT, PANEL))
            return (x.reshape(panels, UNIT, PANEL) * w[None]).reshape(rows, PANEL)

        feats = [feat]
        for tap in range(1, TAPS):
            turned = pltpu.roll(feat, tap, 1)
            feats.append(jnp.where(lane < tap, rows_down(turned, UNIT), turned))
        streams = []
        for m in range(3):
            total = weigh(m * TAPS, feats[0])
            for tap in range(1, TAPS):
                total = total + weigh(m * TAPS + tap, feats[tap])
            streams.append(total)
        query, key, value = streams
        mixed = (key * value).astype(jnp.bfloat16)
        grad_conv = (cot * query).astype(jnp.bfloat16)
        earlier = jnp.concatenate(
            [mixed] + [rows_down(mixed, o * UNIT) for o in range(1, reach)], axis=1
        )
        later = jnp.concatenate(
            [grad_conv] + [rows_up(grad_conv, o * UNIT) for o in range(1, reach)], axis=1
        )
        spread = spreads[g]
        stacked = jnp.concatenate(
            [spread[:, o * PANEL : (o + 1) * PANEL] for o in range(reach)], axis=0
        )
        conv = jnp.dot(earlier, stacked, preferred_element_type=jnp.float32)
        back = lax.dot_general(
            later, spread, (((1,), (1,)), ((), ())), preferred_element_type=jnp.float32
        )
        products = lax.dot_general(
            mixed, later, (((0,), (0,)), ((), ())), preferred_element_type=jnp.float32
        )
        fg[pl.ds(g, 1), :] = lag_sums(products)
        out_t[:, chan, :] = (query * conv).reshape(panels, UNIT, PANEL)
        grads = (cot * conv, back * value, back * key)
        grad_in = None
        for tap in range(TAPS):
            part = weigh(tap, grads[0]) + weigh(TAPS + tap, grads[1]) + weigh(2 * TAPS + tap, grads[2])
            if tap:
                turned = pltpu.roll(part, PANEL - tap, 1)
                part = jnp.where(lane >= PANEL - tap, rows_up(turned, UNIT), turned)
            grad_in = part if grad_in is None else grad_in + part
        in_t[:, chan, :] = grad_in.reshape(panels, UNIT, PANEL)
        small_lane = lax.broadcasted_iota(jnp.int32, (UNIT, PANEL), 1)
        sums = jnp.zeros((UNIT, PANEL), jnp.float32)
        for m in range(3):
            for tap in range(TAPS):
                part = jnp.sum((grads[m] * feats[tap]).reshape(panels, UNIT, PANEL), axis=0)
                sums = jnp.where(small_lane == m * TAPS + tap, jnp.sum(part, axis=1, keepdims=True), sums)
        sg_t[chan, :] = sums
        return carry

    lax.fori_loop(0, TILE // UNIT, group, 0, unroll=UNROLL)


def layer_kernel(
    reach, ndp, nctx, f_hbm, c_hbm, sw_hbm, fl_hbm, rp_hbm, out_hbm, in_hbm, fg_hbm, sg_hbm,
    near, far, halves, tail, tail_all, zx_send, zx_recv, gl_send, gl_recv,
    every, fg_all, sg_all, last_sem, sw, fl, rp, wrow, wt, taps, small_sem, arrived, leaving, spreads, ft, ct, out_t, in_t, fg, sg_t, pay, parts, sums,
    own_sem, in_send, in_recv, out_send, out_recv, keep_sem,
    rs_send, rs_recv, gd_send, gd_recv, gd_own, gc_send, gc_recv,
):
    dp, me = lax.axis_index("dp"), lax.axis_index("ctx")
    width = arrived.shape[3]
    tiles = width // TILE
    chunk = sums.shape[1]
    filled = tail.shape[0]
    ins, outs = (f_hbm, c_hbm), (out_hbm, in_hbm)

    def ctx_peer(k):
        return turn(me + k, nctx)

    def ctx_from(k):
        return turn(me + nctx - k, nctx)

    def dp_peer(k):
        return turn(dp + k, ndp)

    def dp_from(k):
        return turn(dp + ndp - k, ndp)

    def lanes(j):
        return pl.ds(pl.multiple_of(j * TILE, TILE), TILE)

    def cols(owner, j):
        return pl.ds(pl.multiple_of(owner * width + j * TILE, TILE), TILE)

    def copy(src, dst, send, recv, device):
        return pltpu.make_async_remote_copy(
            src_ref=src, dst_ref=dst, send_sem=send, recv_sem=recv, device_id=device, device_id_type=MESH
        )

    def in_copy(a, j, k, slot):
        return copy(
            ins[a].at[:, cols(ctx_peer(k), j)],
            arrived.at[a, slot, :, lanes(j)],
            in_send.at[a, j, k],
            in_recv.at[a, j, k],
            (dp, ctx_peer(k)),
        )

    def in_own(a, j):
        return pltpu.make_async_copy(
            ins[a].at[:, cols(me, j)], arrived.at[a, me, :, lanes(j)], own_sem.at[a, j]
        )

    def out_copy(a, j, k, slot):
        return copy(
            leaving.at[a, ctx_peer(k), :, lanes(j)],
            outs[a].at[:, cols(slot, j)],
            out_send.at[a, j, k],
            out_recv.at[a, j, k],
            (dp, ctx_peer(k)),
        )

    def out_own(a, j):
        return pltpu.make_async_copy(
            leaving.at[a, me, :, lanes(j)], outs[a].at[:, cols(me, j)], keep_sem.at[a, j]
        )

    def rs_copy(j, k):
        return copy(
            pay.at[j, dp_peer(k)], parts.at[j, k], rs_send.at[j, k], rs_recv.at[j, k], (dp_peer(k), me)
        )

    def gc_copy(j, k, slot):
        return copy(
            sums.at[j], every.at[j, dp, slot], gc_send.at[j, k], gc_recv.at[j, k], (dp, ctx_peer(k))
        )

    def gc_keep(j):
        return pltpu.make_async_copy(sums.at[j], every.at[j, dp, me], gd_own.at[j])

    def gd_copy(j, k, slot):
        return copy(
            every.at[j, dp], every.at[j, slot], gd_send.at[j, k], gd_recv.at[j, k], (dp_peer(k), me)
        )

    def zx_copy(k, slot):
        return copy(halves.at[dp], halves.at[slot], zx_send.at[k], zx_recv.at[k], (dp_peer(k), me))

    def gl_copy(k, slot):
        return copy(tail, tail_all.at[slot], gl_send.at[k], gl_recv.at[k], (dp, ctx_peer(k)))

    def each(count, body, unroll=1):
        if count < 1:
            return
        unroll = max(1, min(unroll, count))

        def step(i, carry):
            body(i)
            return carry

        lax.fori_loop(0, count, step, 0, unroll=unroll)

    small = [
        pltpu.make_async_copy(src, dst, small_sem.at[i])
        for i, (src, dst) in enumerate(((sw_hbm, sw), (fl_hbm, fl), (rp_hbm, rp)))
    ]
    for one in small:
        one.start()
    barrier = pltpu.get_barrier_semaphore()
    others = [ctx_peer(k) for k in range(1, nctx)]
    for other in others:

        @pl.when(other != 0)
        def _():
            pl.semaphore_signal(barrier, inc=1, device_id=(dp, other), device_id_type=MESH)

    for a in range(2):
        each(tiles, lambda j: in_own(a, j).start())

    @pl.when(me != 0)
    def _():
        pl.semaphore_wait(barrier, nctx - 1)
        pl.semaphore_signal(near, inc=1, device_id=(dp, 0), device_id_type=MESH)

    @pl.when(me == 0)
    def _():
        pl.semaphore_wait(near, nctx - 1)
        for k in range(1, ndp):
            pl.semaphore_signal(barrier, inc=1, device_id=(dp_peer(k), 0), device_id_type=MESH)

    def send_in(j):
        for a in range(2):
            each(nctx - 1, unroll=AROUND, body=lambda i: in_copy(a, j, i + 1, me).start())

    ahead = min(2, tiles)
    each(ahead, send_in)
    for one in small:
        one.wait()
    units = taps.shape[0]
    group = me * units
    block = pl.ds(pl.multiple_of(group // PANEL * PANEL, PANEL), PANEL)
    lag_pos = lax.broadcasted_iota(jnp.int32, (fl.shape[0], PANEL), 0)
    masked = jnp.where(lag_pos < rp[:, block] * PANEL, fl[:, block].astype(jnp.float32), 0.0)
    masked = pltpu.roll(masked, lax.rem(PANEL - lax.rem(group, PANEL), PANEL), 1)
    for o in range(reach):
        taps[:, o * PANEL : (o + 1) * PANEL] = masked[o * PANEL : (o + 1) * PANEL].T[:units]
    wrow[...] = jnp.zeros_like(wrow)

    def turn_weights(j):
        for m in range(3):
            wrow[m * TAPS : (m + 1) * TAPS] = sw[m, :, cols(me, j)]
        wt[lanes(j), :] = wrow[...].T

    each(tiles, turn_weights)

    def build(g):
        spreads[g] = toeplitz(taps[pl.ds(g, 1), :])

    each(taps.shape[0], build, UNROLL)

    @pl.when(me == 0)
    def _():
        pl.semaphore_wait(barrier, ndp - 1)
        for other in others:
            pl.semaphore_signal(far, inc=1, device_id=(dp, other), device_id_type=MESH)

    @pl.when(me != 0)
    def _():
        pl.semaphore_wait(far, 1)

    def spread_ctx(j):
        each(ndp - 1, unroll=AROUND, body=lambda i: rs_copy(j, i + 1).wait_recv())
        total = pay[j, dp]
        for k in range(1, ndp):
            total = total + parts[j, k]
        sums[j] = total.astype(jnp.bfloat16)
        gc_keep(j).start()
        each(nctx - 1, unroll=AROUND, body=lambda i: gc_copy(j, i + 1, me).start())

    def spread_dp(j):
        gc_keep(j).wait()
        each(nctx - 1, unroll=AROUND, body=lambda i: gc_copy(j, i + 1, ctx_from(i + 1)).wait_recv())
        each(ndp - 1, unroll=AROUND, body=lambda i: gd_copy(j, i + 1, dp).start())

    def send_out(a, j):
        out_own(a, j).start()
        each(nctx - 1, unroll=AROUND, body=lambda i: out_copy(a, j, i + 1, me).start())

    def one_tile(j):
        for a in range(2):
            in_own(a, j).wait()
            each(
                nctx - 1,
                unroll=AROUND,
                body=lambda i: in_copy(a, j, i + 1, ctx_from(i + 1)).wait_recv(),
            )

        @pl.when(j + ahead < tiles)
        def _():
            send_in(j + ahead)

        def turn_in(n):
            ft[n] = arrived[0, n, :, lanes(j)].astype(jnp.float32).T
            ct[n] = arrived[1, n, :, lanes(j)].astype(jnp.float32).T

        each(nctx, turn_in, UNROLL)
        units = TILE // UNIT
        tile_terms(
            reach, nctx, ft, ct, wt.at[lanes(j), :],
            spreads.at[pl.ds(j * units, units)], out_t, in_t, fg, sg_t,
        )

        def turn_out(n):
            leaving[0, n, :, lanes(j)] = out_t[n].T.astype(jnp.bfloat16)
            leaving[1, n, :, lanes(j)] = in_t[n].T.astype(jnp.bfloat16)

        each(nctx, turn_out, UNROLL)
        rows = [fg[:, o * PANEL : (o + 1) * PANEL] for o in range(reach)] + [sg_t[...].T[:UNIT]]
        terms = jnp.concatenate(rows, axis=0)

        @pl.when(j < tiles - 1)
        def _():
            padded = [terms]
            if filled < ndp * chunk:
                padded.append(jnp.zeros((ndp * chunk - filled, PANEL), jnp.float32))
            pay[j] = jnp.concatenate(padded, axis=0).reshape(ndp, chunk, PANEL)
            each(ndp - 1, unroll=AROUND, body=lambda i: rs_copy(j, i + 1).start())

        @pl.when(j == tiles - 1)
        def _():
            halves[dp] = terms.astype(jnp.bfloat16)
            each(ndp - 1, unroll=AROUND, body=lambda i: zx_copy(i + 1, dp).start())

        @pl.when(j >= 1)
        def _():
            spread_ctx(j - 1)

        @pl.when(j >= 2)
        def _():
            spread_dp(j - 2)

        @pl.when(j < tiles - 1)
        def _():
            send_out(0, j)
            send_out(1, j)

        @pl.when(j == tiles - 1)
        def _():
            each(ndp - 1, unroll=AROUND, body=lambda i: zx_copy(i + 1, dp_from(i + 1)).wait_recv())
            total = halves[0].astype(jnp.float32)
            for k in range(1, ndp):
                total = total + halves[k].astype(jnp.float32)
            tail[...] = total.astype(jnp.bfloat16)
            tail_all[me] = tail[...]
            each(nctx - 1, unroll=AROUND, body=lambda i: gl_copy(i + 1, me).start())
            send_out(0, j)
            if tiles >= 2:
                spread_dp(j - 1)
            send_out(1, j)

    each(tiles, one_tile)

    def sums_in(j):
        each(ndp - 1, unroll=AROUND, body=lambda i: gd_copy(j, i + 1, dp_from(i + 1)).wait_recv())

    each(tiles - 1, sums_in)
    each(nctx - 1, unroll=AROUND, body=lambda i: gl_copy(i + 1, ctx_from(i + 1)).wait_recv())
    lag_rows = [[] for _ in range(reach)]
    width_units = TILE // UNIT
    for n in range(nctx):
        for j in range(tiles):
            if j < tiles - 1:
                terms = every[j, :, n].astype(jnp.float32).reshape(-1, PANEL)
            else:
                terms = tail_all[n].astype(jnp.float32)
            for o in range(reach):
                lag_rows[o].append(terms[o * width_units : (o + 1) * width_units])
            first = (n * tiles + j) * TILE
            for m in range(3):
                row = reach * width_units + m * TAPS
                sg_all[m, :, first : first + TILE] = terms[row : row + TAPS]
    lag_pos = lax.broadcasted_iota(jnp.int32, (PANEL, fg_all.shape[1]), 0)
    for o in range(reach):
        lags = jnp.concatenate(lag_rows[o], axis=0).T
        fg_all[o * PANEL : (o + 1) * PANEL] = jnp.where(lag_pos + o * PANEL < rp[...] * PANEL, lags, 0.0)
    last = [
        pltpu.make_async_copy(src, dst, last_sem.at[i])
        for i, (src, dst) in enumerate(((fg_all, fg_hbm), (sg_all, sg_hbm)))
    ]
    for one in last:
        one.start()

    def finish(j):
        for a in range(2):
            each(nctx - 1, unroll=AROUND, body=lambda i: in_copy(a, j, i + 1, me).wait_send())
            out_own(a, j).wait()
            each(nctx - 1, unroll=AROUND, body=lambda i: out_copy(a, j, i + 1, me).wait_send())
            each(
                nctx - 1,
                unroll=AROUND,
                body=lambda i: out_copy(a, j, i + 1, ctx_from(i + 1)).wait_recv(),
            )

    def finish_sums(j):
        each(ndp - 1, unroll=AROUND, body=lambda i: rs_copy(j, i + 1).wait_send())
        each(nctx - 1, unroll=AROUND, body=lambda i: gc_copy(j, i + 1, me).wait_send())
        each(ndp - 1, unroll=AROUND, body=lambda i: gd_copy(j, i + 1, dp).wait_send())

    each(tiles - 1, finish_sums)
    each(ndp - 1, unroll=AROUND, body=lambda i: zx_copy(i + 1, dp).wait_send())
    each(nctx - 1, unroll=AROUND, body=lambda i: gl_copy(i + 1, me).wait_send())
    each(tiles, finish)
    for one in last:
        one.wait()


def finish_kernel(*refs):
    sources, targets, holds, (get_sem, put_sem) = refs[:4], refs[4:8], refs[8:12], refs[12:]
    fetches, moves = [], []
    for i in range(STRIPS):
        for a, (src, hold, dst) in enumerate(zip(sources, holds, targets)):
            if len(src.shape) == 2:
                strip = src.shape[0] // STRIPS
                part = pl.ds(i * strip, strip)
            elif i < src.shape[0]:
                part = i
            else:
                continue
            fetches.append(pltpu.make_async_copy(src.at[part], hold.at[part], get_sem.at[a, i]))
            moves.append(pltpu.make_async_copy(hold.at[part], dst.at[part], put_sem.at[a, i]))
    for one in fetches:
        one.start()
    for fetch, move in zip(fetches, moves):
        fetch.wait()
        move.start()
    for one in moves:
        one.wait()


def shards(ndp, nctx, features, short_weights, filters, reach_panels, cotangent):
    filter_len, groups = filters.shape
    channels = features.shape[2]
    reach = filter_len // PANEL
    rows = features.shape[1]
    assert rows == PANEL and features.shape[0] == 1
    width = channels // nctx
    tiles = width // TILE
    units = width // UNIT
    tile_units = TILE // UNIT
    reach_row = reach_panels.reshape(1, groups)
    filled = reach * tile_units + UNIT
    chunk = -(-filled // (UNIT * ndp)) * UNIT
    hbm = pl.BlockSpec(memory_space=pltpu.HBM)
    dma = pltpu.SemaphoreType.DMA
    turned = pltpu.VMEM((nctx, TILE, PANEL), jnp.float32)
    results = [
        jax.ShapeDtypeStruct((rows, channels), jnp.bfloat16),
        jax.ShapeDtypeStruct((rows, channels), jnp.bfloat16),
        jax.ShapeDtypeStruct((filter_len, groups), jnp.float32),
        jax.ShapeDtypeStruct((3, TAPS, channels), jnp.float32),
    ]
    held = pl.pallas_call(
        functools.partial(layer_kernel, reach, ndp, nctx),
        in_specs=[hbm] * 5,
        out_specs=[hbm] * 4,
        out_shape=results,
        scratch_shapes=[
            pltpu.SemaphoreType.REGULAR,
            pltpu.SemaphoreType.REGULAR,
            pltpu.VMEM((ndp, filled, PANEL), jnp.bfloat16),
            pltpu.VMEM((filled, PANEL), jnp.bfloat16),
            pltpu.VMEM((nctx, filled, PANEL), jnp.bfloat16),
            dma((ndp,)),
            dma((ndp,)),
            dma((nctx,)),
            dma((nctx,)),
            pltpu.VMEM((tiles, ndp, nctx, chunk, PANEL), jnp.bfloat16),
            pltpu.VMEM((filter_len, groups), jnp.float32),
            pltpu.VMEM((3, TAPS, channels), jnp.float32),
            dma((2,)),
            pltpu.VMEM((3, TAPS, channels), jnp.float32),
            pltpu.VMEM((filter_len, groups), jnp.bfloat16),
            pltpu.VMEM((1, groups), jnp.int32),
            pltpu.VMEM((UNIT, PANEL), jnp.float32),
            pltpu.VMEM((width, UNIT), jnp.float32),
            pltpu.VMEM((units, filter_len), jnp.float32),
            dma((3,)),
            pltpu.VMEM((2, nctx, PANEL, width), jnp.bfloat16),
            pltpu.VMEM((2, nctx, PANEL, width), jnp.bfloat16),
            pltpu.VMEM((units, PANEL, filter_len), jnp.bfloat16),
            turned,
            turned,
            turned,
            turned,
            pltpu.VMEM((tile_units, filter_len), jnp.float32),
            pltpu.VMEM((TILE, PANEL), jnp.float32),
            pltpu.VMEM((tiles, ndp, chunk, PANEL), jnp.float32),
            pltpu.VMEM((tiles, ndp, chunk, PANEL), jnp.float32),
            pltpu.VMEM((tiles, chunk, PANEL), jnp.bfloat16),
            dma((2, tiles)),
            dma((2, tiles, nctx)),
            dma((2, tiles, nctx)),
            dma((2, tiles, nctx)),
            dma((2, tiles, nctx)),
            dma((2, tiles)),
            dma((tiles, ndp)),
            dma((tiles, ndp)),
            dma((tiles, ndp)),
            dma((tiles, ndp)),
            dma((tiles,)),
            dma((tiles, nctx)),
            dma((tiles, nctx)),
        ],
        compiler_params=pltpu.CompilerParams(
            collective_id=0, has_side_effects=True, vmem_limit_bytes=58 * 2**20
        ),
    )(features[0], cotangent[0], short_weights, filters, reach_row)
    layer_out, input_grad, filter_grad, short_grad = pl.pallas_call(
        finish_kernel,
        in_specs=[hbm] * 4,
        out_specs=[hbm] * 4,
        out_shape=results,
        scratch_shapes=[pltpu.VMEM(one.shape, one.dtype) for one in results] + [dma((4, STRIPS))] * 2,
    )(*held)
    return (layer_out[None], input_grad[None], filter_grad, short_grad)


def solution(mesh):
    return jax.shard_map(
        functools.partial(shards, mesh.shape["dp"], mesh.shape["ctx"]),
        mesh=mesh,
        in_specs=(P("dp", "ctx", None), P(), P(), P(), P("dp", "ctx", None)),
        out_specs=(P("dp", "ctx", None), P("dp", "ctx", None), P(), P()),
        check_vma=False,
    )
```

```python
import functools

import jax
import jax.numpy as jnp
from jax import lax
from jax.experimental import pallas as pl
from jax.experimental.pallas import tpu as pltpu
from jax.sharding import PartitionSpec as P

PANEL = 128
UNIT = 16
TILE = 128
TAPS = 3
UNROLL = 4
STRIPS = 4
AROUND = 8
MESH = pl.DeviceIdType.MESH


def rows_down(x, rows):
    return jnp.concatenate([jnp.zeros((rows, x.shape[1]), x.dtype), x[:-rows]], axis=0)


def rows_up(x, rows):
    return jnp.concatenate([x[rows:], jnp.zeros((rows, x.shape[1]), x.dtype)], axis=0)


def turn(place, count):
    return jnp.where(place >= count, place - count, place)


def causal():
    shape = (PANEL, PANEL)
    return lax.broadcasted_iota(jnp.int32, shape, 1) >= lax.broadcasted_iota(jnp.int32, shape, 0)


def toeplitz(taps):
    width = taps.shape[1]
    x = jnp.broadcast_to(taps, (8, width))
    row = lax.broadcasted_iota(jnp.int32, (8, width), 0)
    for bit in (1, 2, 4):
        x = jnp.where((row & bit) != 0, pltpu.roll(x, bit, 1), x)
    rows = 8
    while rows < PANEL:
        x = jnp.concatenate([x, pltpu.roll(x, rows, 1)], axis=0)
        rows *= 2
    first = jnp.where(causal(), x[:, :PANEL], 0.0)
    return jnp.concatenate([first, x[:, PANEL:]], axis=1).astype(jnp.bfloat16)


def lag_sums(products):
    width = products.shape[1]
    first = jnp.where(causal(), products[:, :PANEL], 0.0)
    x = jnp.concatenate([first, products[:, PANEL:]], axis=1)
    rows = PANEL // 2
    while rows >= 8:
        x = x[:rows] + pltpu.roll(x[rows:], width - rows, 1)
        rows //= 2
    for step in (4, 2, 1):
        x = x + pltpu.roll(pltpu.roll(x, 8 - step, 0), width - step, 1)
    return x[0:1]


def tile_terms(reach, panels, ft, ct, wt, spreads, out_t, in_t, fg, sg_t):
    rows = panels * UNIT

    def group(g, carry):
        first = pl.multiple_of(g * UNIT, UNIT)
        lane = lax.broadcasted_iota(jnp.int32, (rows, PANEL), 1)
        chan = pl.ds(first, UNIT)
        feat = ft[:, chan, :].reshape(rows, PANEL)
        cot = ct[:, chan, :].reshape(rows, PANEL)
        w_all = wt[chan, :]

        def weigh(k, x):
            w = jnp.broadcast_to(w_all[:, k : k + 1], (UNIT, PANEL))
            return (x.reshape(panels, UNIT, PANEL) * w[None]).reshape(rows, PANEL)

        feats = [feat]
        for tap in range(1, TAPS):
            turned = pltpu.roll(feat, tap, 1)
            feats.append(jnp.where(lane < tap, rows_down(turned, UNIT), turned))
        streams = []
        for m in range(3):
            total = weigh(m * TAPS, feats[0])
            for tap in range(1, TAPS):
                total = total + weigh(m * TAPS + tap, feats[tap])
            streams.append(total)
        query, key, value = streams
        mixed = (key * value).astype(jnp.bfloat16)
        grad_conv = (cot * query).astype(jnp.bfloat16)
        earlier = jnp.concatenate(
            [mixed] + [rows_down(mixed, o * UNIT) for o in range(1, reach)], axis=1
        )
        later = jnp.concatenate(
            [grad_conv] + [rows_up(grad_conv, o * UNIT) for o in range(1, reach)], axis=1
        )
        spread = spreads[g]
        stacked = jnp.concatenate(
            [spread[:, o * PANEL : (o + 1) * PANEL] for o in range(reach)], axis=0
        )
        conv = jnp.dot(earlier, stacked, preferred_element_type=jnp.float32)
        back = lax.dot_general(
            later, spread, (((1,), (1,)), ((), ())), preferred_element_type=jnp.float32
        )
        products = lax.dot_general(
            mixed, later, (((0,), (0,)), ((), ())), preferred_element_type=jnp.float32
        )
        fg[pl.ds(g, 1), :] = lag_sums(products)
        out_t[:, chan, :] = (query * conv).reshape(panels, UNIT, PANEL)
        grads = (cot * conv, back * value, back * key)
        grad_in = None
        for tap in range(TAPS):
            part = weigh(tap, grads[0]) + weigh(TAPS + tap, grads[1]) + weigh(2 * TAPS + tap, grads[2])
            if tap:
                turned = pltpu.roll(part, PANEL - tap, 1)
                part = jnp.where(lane >= PANEL - tap, rows_up(turned, UNIT), turned)
            grad_in = part if grad_in is None else grad_in + part
        in_t[:, chan, :] = grad_in.reshape(panels, UNIT, PANEL)
        small_lane = lax.broadcasted_iota(jnp.int32, (UNIT, PANEL), 1)
        sums = jnp.zeros((UNIT, PANEL), jnp.float32)
        for m in range(3):
            for tap in range(TAPS):
                part = jnp.sum((grads[m] * feats[tap]).reshape(panels, UNIT, PANEL), axis=0)
                sums = jnp.where(small_lane == m * TAPS + tap, jnp.sum(part, axis=1, keepdims=True), sums)
        sg_t[chan, :] = sums
        return carry

    lax.fori_loop(0, TILE // UNIT, group, 0, unroll=UNROLL)


def layer_kernel(
    reach, ndp, nctx, f_hbm, c_hbm, sw_hbm, fl_hbm, rp_hbm, out_hbm, in_hbm, fg_hbm, sg_hbm,
    near, far, halves, tail, tail_all, zx_send, zx_recv, gl_send, gl_recv,
    every, fg_all, sg_all, last_sem, sw, fl, rp, wrow, wt, taps, small_sem, arrived, leaving, spreads, ft, ct, out_t, in_t, fg, sg_t, pay, parts, sums,
    own_sem, in_send, in_recv, out_send, out_recv, keep_sem,
    rs_send, rs_recv, gd_send, gd_recv, gc_send, gc_recv, pair_send, pair_recv,
):
    dp, me = lax.axis_index("dp"), lax.axis_index("ctx")
    width = arrived.shape[3]
    tiles = width // TILE
    chunk, filled = sums.shape[0], tail.shape[0]
    core, chip, chips = lax.rem(me, 2), me // 2, nctx // 2
    lag_count = reach * (TILE // UNIT)
    early = tiles - 1
    ins, outs = (f_hbm, c_hbm), (out_hbm, in_hbm)

    def ctx_peer(k):
        return turn(me + k, nctx)

    def ctx_from(k):
        return turn(me + nctx - k, nctx)

    def dp_peer(k):
        return turn(dp + k, ndp)

    def dp_from(k):
        return turn(dp + ndp - k, ndp)

    def lanes(j):
        return pl.ds(pl.multiple_of(j * TILE, TILE), TILE)

    def cols(owner, j):
        return pl.ds(pl.multiple_of(owner * width + j * TILE, TILE), TILE)

    def copy(src, dst, send, recv, device):
        return pltpu.make_async_remote_copy(
            src_ref=src, dst_ref=dst, send_sem=send, recv_sem=recv, device_id=device, device_id_type=MESH
        )

    def in_copy(a, j, k, slot):
        return copy(
            ins[a].at[:, cols(ctx_peer(k), j)],
            arrived.at[a, slot, :, lanes(j)],
            in_send.at[a, j, k],
            in_recv.at[a, j, k],
            (dp, ctx_peer(k)),
        )

    def in_own(a, j):
        return pltpu.make_async_copy(
            ins[a].at[:, cols(me, j)], arrived.at[a, me, :, lanes(j)], own_sem.at[a, j]
        )

    def out_copy(a, j, k, slot):
        return copy(
            leaving.at[a, ctx_peer(k), :, lanes(j)],
            outs[a].at[:, cols(slot, j)],
            out_send.at[a, j, k],
            out_recv.at[a, j, k],
            (dp, ctx_peer(k)),
        )

    def out_own(a, j):
        return pltpu.make_async_copy(
            leaving.at[a, me, :, lanes(j)], outs[a].at[:, cols(me, j)], keep_sem.at[a, j]
        )

    def rs_copy(k):
        part = pl.ds(pl.multiple_of(dp_peer(k) * chunk, chunk), chunk)
        return copy(pay.at[part], parts.at[k], rs_send.at[k], rs_recv.at[k], (dp_peer(k), me))

    def gc_copy(k, slot):
        return copy(sums, every.at[core, dp, slot], gc_send.at[k], gc_recv.at[k], (dp, ctx_peer(2 * k)))

    def gd_copy(k, slot):
        return copy(
            every.at[core, dp], every.at[core, slot], gd_send.at[k], gd_recv.at[k], (dp_peer(k), me)
        )

    def zx_copy(k, slot):
        return copy(halves.at[dp], halves.at[slot], zx_send.at[k], zx_recv.at[k], (dp_peer(k), me))

    def gl_copy(k, slot):
        return copy(tail, tail_all.at[core, slot], gl_send.at[k], gl_recv.at[k], (dp, ctx_peer(2 * k)))

    def pair_copy(i, which):
        ref = (every, tail_all)[i]
        return copy(
            ref.at[which], ref.at[which], pair_send.at[i], pair_recv.at[i], (dp, me + 1 - 2 * core)
        )

    def each(count, body, unroll=1):
        if count < 1:
            return
        unroll = max(1, min(unroll, count))

        def step(i, carry):
            body(i)
            return carry

        lax.fori_loop(0, count, step, 0, unroll=unroll)

    small = [
        pltpu.make_async_copy(src, dst, small_sem.at[i])
        for i, (src, dst) in enumerate(((sw_hbm, sw), (fl_hbm, fl), (rp_hbm, rp)))
    ]
    for one in small:
        one.start()
    barrier = pltpu.get_barrier_semaphore()
    others = [ctx_peer(k) for k in range(1, nctx)]
    for other in others:

        @pl.when(other != 0)
        def _():
            pl.semaphore_signal(barrier, inc=1, device_id=(dp, other), device_id_type=MESH)

    for a in range(2):
        each(tiles, lambda j: in_own(a, j).start())

    @pl.when(me != 0)
    def _():
        pl.semaphore_wait(barrier, nctx - 1)
        pl.semaphore_signal(near, inc=1, device_id=(dp, 0), device_id_type=MESH)

    @pl.when(me == 0)
    def _():
        pl.semaphore_wait(near, nctx - 1)
        for k in range(1, ndp):
            pl.semaphore_signal(barrier, inc=1, device_id=(dp_peer(k), 0), device_id_type=MESH)

    def send_in(j):
        for a in range(2):
            each(nctx - 1, unroll=AROUND, body=lambda i: in_copy(a, j, i + 1, me).start())

    ahead = min(2, tiles)
    each(ahead, send_in)
    for one in small:
        one.wait()
    units = taps.shape[0]
    group = me * units
    block = pl.ds(pl.multiple_of(group // PANEL * PANEL, PANEL), PANEL)
    lag_pos = lax.broadcasted_iota(jnp.int32, (fl.shape[0], PANEL), 0)
    masked = jnp.where(lag_pos < rp[:, block] * PANEL, fl[:, block].astype(jnp.float32), 0.0)
    masked = pltpu.roll(masked, lax.rem(PANEL - lax.rem(group, PANEL), PANEL), 1)
    for o in range(reach):
        taps[:, o * PANEL : (o + 1) * PANEL] = masked[o * PANEL : (o + 1) * PANEL].T[:units]
    wrow[...] = jnp.zeros_like(wrow)

    def turn_weights(j):
        for m in range(3):
            wrow[m * TAPS : (m + 1) * TAPS] = sw[m, :, cols(me, j)]
        wt[lanes(j), :] = wrow[...].T

    each(tiles, turn_weights)

    def build(g):
        spreads[g] = toeplitz(taps[pl.ds(g, 1), :])

    each(taps.shape[0], build, UNROLL)

    @pl.when(me == 0)
    def _():
        pl.semaphore_wait(barrier, ndp - 1)
        for other in others:
            pl.semaphore_signal(far, inc=1, device_id=(dp, other), device_id_type=MESH)

    @pl.when(me != 0)
    def _():
        pl.semaphore_wait(far, 1)

    def spread_ctx():
        each(ndp - 1, unroll=AROUND, body=lambda i: rs_copy(i + 1).wait_recv())
        total = pay[pl.ds(pl.multiple_of(dp * chunk, chunk), chunk)]
        for k in range(1, ndp):
            total = total + parts[k]
        sums[...] = total.astype(jnp.bfloat16)
        every[core, dp, chip] = sums[...]
        each(chips - 1, unroll=AROUND, body=lambda i: gc_copy(i + 1, chip).start())

    def spread_dp():
        each(chips - 1, unroll=AROUND, body=lambda i: gc_copy(i + 1, ctx_from(2 * i + 2) // 2).wait_recv())
        each(ndp - 1, unroll=AROUND, body=lambda i: gd_copy(i + 1, dp).start())

    def send_out(a, j):
        out_own(a, j).start()
        each(nctx - 1, unroll=AROUND, body=lambda i: out_copy(a, j, i + 1, me).start())

    def one_tile(j):
        for a in range(2):
            in_own(a, j).wait()
            each(
                nctx - 1,
                unroll=AROUND,
                body=lambda i: in_copy(a, j, i + 1, ctx_from(i + 1)).wait_recv(),
            )

        @pl.when(j + ahead < tiles)
        def _():
            send_in(j + ahead)

        def turn_in(n):
            ft[n] = arrived[0, n, :, lanes(j)].astype(jnp.float32).T
            ct[n] = arrived[1, n, :, lanes(j)].astype(jnp.float32).T

        each(nctx, turn_in, UNROLL)
        units = TILE // UNIT
        tile_terms(
            reach, nctx, ft, ct, wt.at[lanes(j), :],
            spreads.at[pl.ds(j * units, units)], out_t, in_t, fg, sg_t,
        )

        def turn_out(n):
            leaving[0, n, :, lanes(j)] = out_t[n].T.astype(jnp.bfloat16)
            leaving[1, n, :, lanes(j)] = in_t[n].T.astype(jnp.bfloat16)

        each(nctx, turn_out, UNROLL)
        lags = jnp.concatenate([fg[:, o * PANEL : (o + 1) * PANEL] for o in range(reach)], axis=0)
        shorts = sg_t[...].T[:UNIT]

        @pl.when(j < early)
        def _():
            pay[pl.ds(pl.multiple_of(j * lag_count, lag_count), lag_count)] = lags

        for place in range(early):

            @pl.when(j == place)
            def _():
                first = early * lag_count + place * 3 * TAPS
                pay[first : first + 3 * TAPS] = shorts[: 3 * TAPS]

        @pl.when(j == early - 1)
        def _():
            each(ndp - 1, unroll=AROUND, body=lambda i: rs_copy(i + 1).start())

        @pl.when(j == early)
        def _():
            halves[dp] = jnp.concatenate([lags, shorts], axis=0).astype(jnp.bfloat16)
            each(ndp - 1, unroll=AROUND, body=lambda i: zx_copy(i + 1, dp).start())

        @pl.when(j < early)
        def _():
            send_out(0, j)
            send_out(1, j)

        @pl.when(j == early)
        def _():
            if early:
                spread_ctx()
            each(ndp - 1, unroll=AROUND, body=lambda i: zx_copy(i + 1, dp_from(i + 1)).wait_recv())
            total = halves[0].astype(jnp.float32)
            for k in range(1, ndp):
                total = total + halves[k].astype(jnp.float32)
            tail[...] = total.astype(jnp.bfloat16)
            tail_all[core, chip] = tail[...]
            each(chips - 1, unroll=AROUND, body=lambda i: gl_copy(i + 1, chip).start())
            send_out(0, j)
            if early:
                spread_dp()
            each(
                chips - 1,
                unroll=AROUND,
                body=lambda i: gl_copy(i + 1, ctx_from(2 * i + 2) // 2).wait_recv(),
            )
            pair_copy(1, core).start()
            send_out(1, j)

    if early:
        pay[early * (lag_count + 3 * TAPS) :] = jnp.zeros(
            (pay.shape[0] - early * (lag_count + 3 * TAPS), PANEL), jnp.float32
        )
    each(tiles, one_tile)
    if early:
        each(ndp - 1, unroll=AROUND, body=lambda i: gd_copy(i + 1, dp_from(i + 1)).wait_recv())
        pair_copy(0, core).start()
    pair_copy(1, 1 - core).wait_recv()
    if early:
        pair_copy(0, 1 - core).wait_recv()
    lag_rows = [[] for _ in range(reach)]
    width_units = TILE // UNIT
    for n in range(nctx):
        if early:
            before = every[n % 2, :, n // 2].astype(jnp.float32).reshape(-1, PANEL)
        for j in range(tiles):
            if j < early:
                lags = before[j * lag_count : (j + 1) * lag_count]
                row = early * lag_count + j * 3 * TAPS
                shorts = before[row : row + 3 * TAPS]
            else:
                terms = tail_all[n % 2, n // 2].astype(jnp.float32)
                lags, shorts = terms[:lag_count], terms[lag_count : lag_count + 3 * TAPS]
            for o in range(reach):
                lag_rows[o].append(lags[o * width_units : (o + 1) * width_units])
            first = (n * tiles + j) * TILE
            for m in range(3):
                sg_all[m, :, first : first + TILE] = shorts[m * TAPS : (m + 1) * TAPS]
    lag_pos = lax.broadcasted_iota(jnp.int32, (PANEL, fg_all.shape[1]), 0)
    for o in range(reach):
        lags = jnp.concatenate(lag_rows[o], axis=0).T
        fg_all[o * PANEL : (o + 1) * PANEL] = jnp.where(lag_pos + o * PANEL < rp[...] * PANEL, lags, 0.0)
    last = [
        pltpu.make_async_copy(src, dst, last_sem.at[i])
        for i, (src, dst) in enumerate(((fg_all, fg_hbm), (sg_all, sg_hbm)))
    ]
    for one in last:
        one.start()

    def finish(j):
        for a in range(2):
            each(nctx - 1, unroll=AROUND, body=lambda i: in_copy(a, j, i + 1, me).wait_send())
            out_own(a, j).wait()
            each(nctx - 1, unroll=AROUND, body=lambda i: out_copy(a, j, i + 1, me).wait_send())
            each(
                nctx - 1,
                unroll=AROUND,
                body=lambda i: out_copy(a, j, i + 1, ctx_from(i + 1)).wait_recv(),
            )

    if early:
        each(ndp - 1, unroll=AROUND, body=lambda i: rs_copy(i + 1).wait_send())
        each(chips - 1, unroll=AROUND, body=lambda i: gc_copy(i + 1, chip).wait_send())
        each(ndp - 1, unroll=AROUND, body=lambda i: gd_copy(i + 1, dp).wait_send())
        pair_copy(0, core).wait_send()
    each(ndp - 1, unroll=AROUND, body=lambda i: zx_copy(i + 1, dp).wait_send())
    each(chips - 1, unroll=AROUND, body=lambda i: gl_copy(i + 1, chip).wait_send())
    pair_copy(1, core).wait_send()
    each(tiles, finish)
    for one in last:
        one.wait()


def finish_kernel(*refs):
    sources, targets, holds, (get_sem, put_sem) = refs[:4], refs[4:8], refs[8:12], refs[12:]
    fetches, moves = [], []
    for i in range(STRIPS):
        for a, (src, hold, dst) in enumerate(zip(sources, holds, targets)):
            if len(src.shape) == 2:
                strip = src.shape[0] // STRIPS
                part = pl.ds(i * strip, strip)
            elif i < src.shape[0]:
                part = i
            else:
                continue
            fetches.append(pltpu.make_async_copy(src.at[part], hold.at[part], get_sem.at[a, i]))
            moves.append(pltpu.make_async_copy(hold.at[part], dst.at[part], put_sem.at[a, i]))
    for one in fetches:
        one.start()
    for fetch, move in zip(fetches, moves):
        fetch.wait()
        move.start()
    for one in moves:
        one.wait()


def shards(ndp, nctx, features, short_weights, filters, reach_panels, cotangent):
    filter_len, groups = filters.shape
    channels = features.shape[2]
    reach = filter_len // PANEL
    rows = features.shape[1]
    assert rows == PANEL and features.shape[0] == 1
    width = channels // nctx
    tiles = width // TILE
    units = width // UNIT
    tile_units = TILE // UNIT
    reach_row = reach_panels.reshape(1, groups)
    filled = reach * tile_units + UNIT
    early_rows = max(tiles - 1, 1) * (reach * tile_units + 3 * TAPS)
    chunk = -(-early_rows // (UNIT * ndp)) * UNIT
    assert nctx % 2 == 0
    hbm = pl.BlockSpec(memory_space=pltpu.HBM)
    dma = pltpu.SemaphoreType.DMA
    turned = pltpu.VMEM((nctx, TILE, PANEL), jnp.float32)
    results = [
        jax.ShapeDtypeStruct((rows, channels), jnp.bfloat16),
        jax.ShapeDtypeStruct((rows, channels), jnp.bfloat16),
        jax.ShapeDtypeStruct((filter_len, groups), jnp.float32),
        jax.ShapeDtypeStruct((3, TAPS, channels), jnp.float32),
    ]
    held = pl.pallas_call(
        functools.partial(layer_kernel, reach, ndp, nctx),
        in_specs=[hbm] * 5,
        out_specs=[hbm] * 4,
        out_shape=results,
        scratch_shapes=[
            pltpu.SemaphoreType.REGULAR,
            pltpu.SemaphoreType.REGULAR,
            pltpu.VMEM((ndp, filled, PANEL), jnp.bfloat16),
            pltpu.VMEM((filled, PANEL), jnp.bfloat16),
            pltpu.VMEM((2, nctx // 2, filled, PANEL), jnp.bfloat16),
            dma((ndp,)),
            dma((ndp,)),
            dma((nctx // 2,)),
            dma((nctx // 2,)),
            pltpu.VMEM((2, ndp, nctx // 2, chunk, PANEL), jnp.bfloat16),
            pltpu.VMEM((filter_len, groups), jnp.float32),
            pltpu.VMEM((3, TAPS, channels), jnp.float32),
            dma((2,)),
            pltpu.VMEM((3, TAPS, channels), jnp.float32),
            pltpu.VMEM((filter_len, groups), jnp.bfloat16),
            pltpu.VMEM((1, groups), jnp.int32),
            pltpu.VMEM((UNIT, PANEL), jnp.float32),
            pltpu.VMEM((width, UNIT), jnp.float32),
            pltpu.VMEM((units, filter_len), jnp.float32),
            dma((3,)),
            pltpu.VMEM((2, nctx, PANEL, width), jnp.bfloat16),
            pltpu.VMEM((2, nctx, PANEL, width), jnp.bfloat16),
            pltpu.VMEM((units, PANEL, filter_len), jnp.bfloat16),
            turned,
            turned,
            turned,
            turned,
            pltpu.VMEM((tile_units, filter_len), jnp.float32),
            pltpu.VMEM((TILE, PANEL), jnp.float32),
            pltpu.VMEM((ndp * chunk, PANEL), jnp.float32),
            pltpu.VMEM((ndp, chunk, PANEL), jnp.float32),
            pltpu.VMEM((chunk, PANEL), jnp.bfloat16),
            dma((2, tiles)),
            dma((2, tiles, nctx)),
            dma((2, tiles, nctx)),
            dma((2, tiles, nctx)),
            dma((2, tiles, nctx)),
            dma((2, tiles)),
            dma((ndp,)),
            dma((ndp,)),
            dma((ndp,)),
            dma((ndp,)),
            dma((nctx // 2,)),
            dma((nctx // 2,)),
            dma((2,)),
            dma((2,)),
        ],
        compiler_params=pltpu.CompilerParams(
            collective_id=0, has_side_effects=True, vmem_limit_bytes=58 * 2**20
        ),
    )(features[0], cotangent[0], short_weights, filters, reach_row)
    layer_out, input_grad, filter_grad, short_grad = pl.pallas_call(
        finish_kernel,
        in_specs=[hbm] * 4,
        out_specs=[hbm] * 4,
        out_shape=results,
        scratch_shapes=[pltpu.VMEM(one.shape, one.dtype) for one in results] + [dma((4, STRIPS))] * 2,
    )(*held)
    return (layer_out[None], input_grad[None], filter_grad, short_grad)


def solution(mesh):
    return jax.shard_map(
        functools.partial(shards, mesh.shape["dp"], mesh.shape["ctx"]),
        mesh=mesh,
        in_specs=(P("dp", "ctx", None), P(), P(), P(), P("dp", "ctx", None)),
        out_specs=(P("dp", "ctx", None), P("dp", "ctx", None), P(), P()),
        check_vma=False,
    )
```

```python
import functools

import jax
import jax.numpy as jnp
from jax import lax
from jax.experimental import pallas as pl
from jax.experimental.pallas import tpu as pltpu
from jax.sharding import PartitionSpec as P

PANEL = 128
UNIT = 16
TILE = 128
TAPS = 3
UNROLL = 4
STRIPS = 4
AROUND = 8
MESH = pl.DeviceIdType.MESH


def rows_down(x, rows):
    return jnp.concatenate([jnp.zeros((rows, x.shape[1]), x.dtype), x[:-rows]], axis=0)


def rows_up(x, rows):
    return jnp.concatenate([x[rows:], jnp.zeros((rows, x.shape[1]), x.dtype)], axis=0)


def turn(place, count):
    return jnp.where(place >= count, place - count, place)


def causal():
    shape = (PANEL, PANEL)
    return lax.broadcasted_iota(jnp.int32, shape, 1) >= lax.broadcasted_iota(jnp.int32, shape, 0)


def toeplitz(taps):
    width = taps.shape[1]
    x = jnp.broadcast_to(taps, (8, width))
    row = lax.broadcasted_iota(jnp.int32, (8, width), 0)
    for bit in (1, 2, 4):
        x = jnp.where((row & bit) != 0, pltpu.roll(x, bit, 1), x)
    rows = 8
    while rows < PANEL:
        x = jnp.concatenate([x, pltpu.roll(x, rows, 1)], axis=0)
        rows *= 2
    first = jnp.where(causal(), x[:, :PANEL], 0.0)
    return jnp.concatenate([first, x[:, PANEL:]], axis=1).astype(jnp.bfloat16)


def lag_sums(products):
    width = products.shape[1]
    first = jnp.where(causal(), products[:, :PANEL], 0.0)
    x = jnp.concatenate([first, products[:, PANEL:]], axis=1)
    rows = PANEL // 2
    while rows >= 8:
        x = x[:rows] + pltpu.roll(x[rows:], width - rows, 1)
        rows //= 2
    for step in (4, 2, 1):
        x = x + pltpu.roll(pltpu.roll(x, 8 - step, 0), width - step, 1)
    return x[0:1]


def tile_terms(reach, panels, ft, ct, wt, spreads, out_t, in_t, fg, sg_t):
    rows = panels * UNIT

    def group(g, carry):
        first = pl.multiple_of(g * UNIT, UNIT)
        lane = lax.broadcasted_iota(jnp.int32, (rows, PANEL), 1)
        chan = pl.ds(first, UNIT)
        feat = ft[:, chan, :].reshape(rows, PANEL)
        cot = ct[:, chan, :].reshape(rows, PANEL)
        w_all = wt[chan, :]

        def weigh(k, x):
            w = jnp.broadcast_to(w_all[:, k : k + 1], (UNIT, PANEL))
            return (x.reshape(panels, UNIT, PANEL) * w[None]).reshape(rows, PANEL)

        feats = [feat]
        for tap in range(1, TAPS):
            turned = pltpu.roll(feat, tap, 1)
            feats.append(jnp.where(lane < tap, rows_down(turned, UNIT), turned))
        streams = []
        for m in range(3):
            total = weigh(m * TAPS, feats[0])
            for tap in range(1, TAPS):
                total = total + weigh(m * TAPS + tap, feats[tap])
            streams.append(total)
        query, key, value = streams
        mixed = (key * value).astype(jnp.bfloat16)
        grad_conv = (cot * query).astype(jnp.bfloat16)
        earlier = jnp.concatenate(
            [mixed] + [rows_down(mixed, o * UNIT) for o in range(1, reach)], axis=1
        )
        later = jnp.concatenate(
            [grad_conv] + [rows_up(grad_conv, o * UNIT) for o in range(1, reach)], axis=1
        )
        spread = spreads[g]
        stacked = jnp.concatenate(
            [spread[:, o * PANEL : (o + 1) * PANEL] for o in range(reach)], axis=0
        )
        conv = jnp.dot(earlier, stacked, preferred_element_type=jnp.float32)
        back = lax.dot_general(
            later, spread, (((1,), (1,)), ((), ())), preferred_element_type=jnp.float32
        )
        products = lax.dot_general(
            mixed, later, (((0,), (0,)), ((), ())), preferred_element_type=jnp.float32
        )
        fg[pl.ds(g, 1), :] = lag_sums(products)
        out_t[:, chan, :] = (query * conv).reshape(panels, UNIT, PANEL)
        grads = (cot * conv, back * value, back * key)
        grad_in = None
        for tap in range(TAPS):
            part = weigh(tap, grads[0]) + weigh(TAPS + tap, grads[1]) + weigh(2 * TAPS + tap, grads[2])
            if tap:
                turned = pltpu.roll(part, PANEL - tap, 1)
                part = jnp.where(lane >= PANEL - tap, rows_up(turned, UNIT), turned)
            grad_in = part if grad_in is None else grad_in + part
        in_t[:, chan, :] = grad_in.reshape(panels, UNIT, PANEL)
        small_lane = lax.broadcasted_iota(jnp.int32, (UNIT, PANEL), 1)
        sums = jnp.zeros((UNIT, PANEL), jnp.float32)
        for m in range(3):
            for tap in range(TAPS):
                part = jnp.sum((grads[m] * feats[tap]).reshape(panels, UNIT, PANEL), axis=0)
                sums = jnp.where(small_lane == m * TAPS + tap, jnp.sum(part, axis=1, keepdims=True), sums)
        sg_t[chan, :] = sums
        return carry

    lax.fori_loop(0, TILE // UNIT, group, 0, unroll=UNROLL)


def layer_kernel(
    reach, ndp, nctx, f_hbm, c_hbm, sw_hbm, fl_hbm, rp_hbm, out_hbm, in_hbm, fg_hbm, sg_hbm,
    near, far, halves, tail, tail_all, zx_send, zx_recv, gl_send, gl_recv,
    every, fg_all, sg_all, last_sem, sw, fl, rp, wrow, wt, taps, small_sem, arrived, leaving, spreads, ft, ct, out_t, in_t, fg, sg_t, pay, parts, sums,
    own_sem, in_send, in_recv, out_send, out_recv, keep_sem,
    rs_send, rs_recv, gd_send, gd_recv, gc_send, gc_recv, pair_send, pair_recv,
):
    dp, me = lax.axis_index("dp"), lax.axis_index("ctx")
    width = arrived.shape[3]
    tiles = width // TILE
    chunk, filled = sums.shape[0], tail.shape[0]
    core, chip, chips = lax.rem(me, 2), me // 2, nctx // 2
    lag_count = reach * (TILE // UNIT)
    early = tiles - 1
    ins, outs = (f_hbm, c_hbm), (out_hbm, in_hbm)

    def ctx_peer(k):
        return turn(me + k, nctx)

    def ctx_from(k):
        return turn(me + nctx - k, nctx)

    def dp_peer(k):
        return turn(dp + k, ndp)

    def dp_from(k):
        return turn(dp + ndp - k, ndp)

    def lanes(j):
        return pl.ds(pl.multiple_of(j * TILE, TILE), TILE)

    def cols(owner, j):
        return pl.ds(pl.multiple_of(owner * width + j * TILE, TILE), TILE)

    def copy(src, dst, send, recv, device):
        return pltpu.make_async_remote_copy(
            src_ref=src, dst_ref=dst, send_sem=send, recv_sem=recv, device_id=device, device_id_type=MESH
        )

    def in_copy(a, j, k, slot):
        return copy(
            ins[a].at[:, cols(ctx_peer(k), j)],
            arrived.at[a, slot, :, lanes(j)],
            in_send.at[a, j, k],
            in_recv.at[a, j, k],
            (dp, ctx_peer(k)),
        )

    def in_own(a, j):
        return pltpu.make_async_copy(
            ins[a].at[:, cols(me, j)], arrived.at[a, me, :, lanes(j)], own_sem.at[a, j]
        )

    def out_copy(a, j, k, slot):
        return copy(
            leaving.at[a, ctx_peer(k), :, lanes(j)],
            outs[a].at[:, cols(slot, j)],
            out_send.at[a, j, k],
            out_recv.at[a, j, k],
            (dp, ctx_peer(k)),
        )

    def out_own(a, j):
        return pltpu.make_async_copy(
            leaving.at[a, me, :, lanes(j)], outs[a].at[:, cols(me, j)], keep_sem.at[a, j]
        )

    def rs_copy(k):
        part = pl.ds(pl.multiple_of(dp_peer(k) * chunk, chunk), chunk)
        return copy(pay.at[part], parts.at[k], rs_send.at[k], rs_recv.at[k], (dp_peer(k), me))

    def gc_copy(k, slot):
        return copy(sums, every.at[core, dp, slot], gc_send.at[k], gc_recv.at[k], (dp, ctx_peer(2 * k)))

    def gd_copy(k, slot):
        return copy(
            every.at[core, dp], every.at[core, slot], gd_send.at[k], gd_recv.at[k], (dp_peer(k), me)
        )

    def zx_copy(k, slot):
        return copy(halves.at[dp], halves.at[slot], zx_send.at[k], zx_recv.at[k], (dp_peer(k), me))

    def gl_copy(k, slot):
        return copy(tail, tail_all.at[core, slot], gl_send.at[k], gl_recv.at[k], (dp, ctx_peer(2 * k)))

    def pair_copy(i, which):
        ref = (every, tail_all)[i]
        return copy(
            ref.at[which], ref.at[which], pair_send.at[i], pair_recv.at[i], (dp, me + 1 - 2 * core)
        )

    def each(count, body, unroll=1):
        if count < 1:
            return
        unroll = max(1, min(unroll, count))

        def step(i, carry):
            body(i)
            return carry

        lax.fori_loop(0, count, step, 0, unroll=unroll)

    small = [
        pltpu.make_async_copy(src, dst, small_sem.at[i])
        for i, (src, dst) in enumerate(((sw_hbm, sw), (fl_hbm, fl), (rp_hbm, rp)))
    ]
    for one in small:
        one.start()
    barrier = pltpu.get_barrier_semaphore()
    others = [ctx_peer(k) for k in range(1, nctx)]
    for other in others:

        @pl.when(other != 0)
        def _():
            pl.semaphore_signal(barrier, inc=1, device_id=(dp, other), device_id_type=MESH)

    for a in range(2):
        each(tiles, lambda j: in_own(a, j).start())

    @pl.when(me != 0)
    def _():
        pl.semaphore_wait(barrier, nctx - 1)
        pl.semaphore_signal(near, inc=1, device_id=(dp, 0), device_id_type=MESH)

    @pl.when(me == 0)
    def _():
        pl.semaphore_wait(near, nctx - 1)
        for k in range(1, ndp):
            pl.semaphore_signal(barrier, inc=1, device_id=(dp_peer(k), 0), device_id_type=MESH)

    def send_in(j):
        for a in range(2):
            each(nctx - 1, unroll=AROUND, body=lambda i: in_copy(a, j, i + 1, me).start())

    ahead = min(2, tiles)
    each(ahead, send_in)
    for one in small:
        one.wait()
    units = taps.shape[0]
    group = me * units
    block = pl.ds(pl.multiple_of(group // PANEL * PANEL, PANEL), PANEL)
    lag_pos = lax.broadcasted_iota(jnp.int32, (fl.shape[0], PANEL), 0)
    masked = jnp.where(lag_pos < rp[:, block] * PANEL, fl[:, block].astype(jnp.float32), 0.0)
    masked = pltpu.roll(masked, lax.rem(PANEL - lax.rem(group, PANEL), PANEL), 1)
    for o in range(reach):
        taps[:, o * PANEL : (o + 1) * PANEL] = masked[o * PANEL : (o + 1) * PANEL].T[:units]
    wrow[...] = jnp.zeros_like(wrow)

    def turn_weights(j):
        for m in range(3):
            wrow[m * TAPS : (m + 1) * TAPS] = sw[m, :, cols(me, j)]
        wt[lanes(j), :] = wrow[...].T

    each(tiles, turn_weights)

    def build(g):
        spreads[g] = toeplitz(taps[pl.ds(g, 1), :])

    each(taps.shape[0], build, UNROLL)

    @pl.when(me == 0)
    def _():
        pl.semaphore_wait(barrier, ndp - 1)
        for other in others:
            pl.semaphore_signal(far, inc=1, device_id=(dp, other), device_id_type=MESH)

    @pl.when(me != 0)
    def _():
        pl.semaphore_wait(far, 1)

    def spread_ctx():
        each(ndp - 1, unroll=AROUND, body=lambda i: rs_copy(i + 1).wait_recv())
        total = pay[pl.ds(pl.multiple_of(dp * chunk, chunk), chunk)]
        for k in range(1, ndp):
            total = total + parts[k]
        sums[...] = total.astype(jnp.bfloat16)
        every[core, dp, chip] = sums[...]
        each(chips - 1, unroll=AROUND, body=lambda i: gc_copy(i + 1, chip).start())

    def spread_dp():
        each(chips - 1, unroll=AROUND, body=lambda i: gc_copy(i + 1, ctx_from(2 * i + 2) // 2).wait_recv())
        each(ndp - 1, unroll=AROUND, body=lambda i: gd_copy(i + 1, dp).start())

    def send_out(a, j):
        out_own(a, j).start()
        each(nctx - 1, unroll=AROUND, body=lambda i: out_copy(a, j, i + 1, me).start())

    def one_tile(j):
        for a in range(2):
            in_own(a, j).wait()
            each(
                nctx - 1,
                unroll=AROUND,
                body=lambda i: in_copy(a, j, i + 1, ctx_from(i + 1)).wait_recv(),
            )

        @pl.when(j + ahead < tiles)
        def _():
            send_in(j + ahead)

        def turn_in(n):
            ft[n] = arrived[0, n, :, lanes(j)].astype(jnp.float32).T
            ct[n] = arrived[1, n, :, lanes(j)].astype(jnp.float32).T

        each(nctx, turn_in, UNROLL)
        units = TILE // UNIT
        tile_terms(
            reach, nctx, ft, ct, wt.at[lanes(j), :],
            spreads.at[pl.ds(j * units, units)], out_t, in_t, fg, sg_t,
        )

        def turn_out(n):
            leaving[0, n, :, lanes(j)] = out_t[n].T.astype(jnp.bfloat16)
            leaving[1, n, :, lanes(j)] = in_t[n].T.astype(jnp.bfloat16)

        each(nctx, turn_out, UNROLL)
        lags = jnp.concatenate([fg[:, o * PANEL : (o + 1) * PANEL] for o in range(reach)], axis=0)
        shorts = sg_t[...].T[:UNIT]

        @pl.when(j < early)
        def _():
            pay[pl.ds(pl.multiple_of(j * lag_count, lag_count), lag_count)] = lags

        for place in range(early):

            @pl.when(j == place)
            def _():
                first = early * lag_count + place * 3 * TAPS
                pay[first : first + 3 * TAPS] = shorts[: 3 * TAPS]

        @pl.when(j == early - 1)
        def _():
            each(ndp - 1, unroll=AROUND, body=lambda i: rs_copy(i + 1).start())

        @pl.when(j == early)
        def _():
            halves[dp] = jnp.concatenate([lags, shorts], axis=0).astype(jnp.bfloat16)
            each(ndp - 1, unroll=AROUND, body=lambda i: zx_copy(i + 1, dp).start())

        @pl.when(j < early)
        def _():
            send_out(0, j)

        @pl.when(j < early - 1)
        def _():
            send_out(1, j)

        @pl.when(j == early)
        def _():
            if early:
                spread_ctx()
                send_out(1, j - 1)
            each(ndp - 1, unroll=AROUND, body=lambda i: zx_copy(i + 1, dp_from(i + 1)).wait_recv())
            total = halves[0].astype(jnp.float32)
            for k in range(1, ndp):
                total = total + halves[k].astype(jnp.float32)
            tail[...] = total.astype(jnp.bfloat16)
            tail_all[core, chip] = tail[...]
            each(chips - 1, unroll=AROUND, body=lambda i: gl_copy(i + 1, chip).start())
            send_out(0, j)
            if early:
                spread_dp()
            send_out(1, j)
            each(
                chips - 1,
                unroll=AROUND,
                body=lambda i: gl_copy(i + 1, ctx_from(2 * i + 2) // 2).wait_recv(),
            )
            pair_copy(1, core).start()

    if early:
        pay[early * (lag_count + 3 * TAPS) :] = jnp.zeros(
            (pay.shape[0] - early * (lag_count + 3 * TAPS), PANEL), jnp.float32
        )
    each(tiles, one_tile)
    if early:
        each(ndp - 1, unroll=AROUND, body=lambda i: gd_copy(i + 1, dp_from(i + 1)).wait_recv())
        pair_copy(0, core).start()
    pair_copy(1, 1 - core).wait_recv()
    if early:
        pair_copy(0, 1 - core).wait_recv()
    lag_rows = [[] for _ in range(reach)]
    width_units = TILE // UNIT
    for n in range(nctx):
        if early:
            before = every[n % 2, :, n // 2].astype(jnp.float32).reshape(-1, PANEL)
        for j in range(tiles):
            if j < early:
                lags = before[j * lag_count : (j + 1) * lag_count]
                row = early * lag_count + j * 3 * TAPS
                shorts = before[row : row + 3 * TAPS]
            else:
                terms = tail_all[n % 2, n // 2].astype(jnp.float32)
                lags, shorts = terms[:lag_count], terms[lag_count : lag_count + 3 * TAPS]
            for o in range(reach):
                lag_rows[o].append(lags[o * width_units : (o + 1) * width_units])
            first = (n * tiles + j) * TILE
            for m in range(3):
                sg_all[m, :, first : first + TILE] = shorts[m * TAPS : (m + 1) * TAPS]
    lag_pos = lax.broadcasted_iota(jnp.int32, (PANEL, fg_all.shape[1]), 0)
    for o in range(reach):
        lags = jnp.concatenate(lag_rows[o], axis=0).T
        fg_all[o * PANEL : (o + 1) * PANEL] = jnp.where(lag_pos + o * PANEL < rp[...] * PANEL, lags, 0.0)
    last = [
        pltpu.make_async_copy(src, dst, last_sem.at[i])
        for i, (src, dst) in enumerate(((fg_all, fg_hbm), (sg_all, sg_hbm)))
    ]
    for one in last:
        one.start()

    def finish(j):
        for a in range(2):
            each(nctx - 1, unroll=AROUND, body=lambda i: in_copy(a, j, i + 1, me).wait_send())
            out_own(a, j).wait()
            each(nctx - 1, unroll=AROUND, body=lambda i: out_copy(a, j, i + 1, me).wait_send())
            each(
                nctx - 1,
                unroll=AROUND,
                body=lambda i: out_copy(a, j, i + 1, ctx_from(i + 1)).wait_recv(),
            )

    if early:
        each(ndp - 1, unroll=AROUND, body=lambda i: rs_copy(i + 1).wait_send())
        each(chips - 1, unroll=AROUND, body=lambda i: gc_copy(i + 1, chip).wait_send())
        each(ndp - 1, unroll=AROUND, body=lambda i: gd_copy(i + 1, dp).wait_send())
        pair_copy(0, core).wait_send()
    each(ndp - 1, unroll=AROUND, body=lambda i: zx_copy(i + 1, dp).wait_send())
    each(chips - 1, unroll=AROUND, body=lambda i: gl_copy(i + 1, chip).wait_send())
    pair_copy(1, core).wait_send()
    each(tiles, finish)
    for one in last:
        one.wait()


def finish_kernel(*refs):
    sources, targets, holds, (get_sem, put_sem) = refs[:4], refs[4:8], refs[8:12], refs[12:]
    fetches, moves = [], []
    for i in range(STRIPS):
        for a, (src, hold, dst) in enumerate(zip(sources, holds, targets)):
            if len(src.shape) == 2:
                strip = src.shape[0] // STRIPS
                part = pl.ds(i * strip, strip)
            elif i < src.shape[0]:
                part = i
            else:
                continue
            fetches.append(pltpu.make_async_copy(src.at[part], hold.at[part], get_sem.at[a, i]))
            moves.append(pltpu.make_async_copy(hold.at[part], dst.at[part], put_sem.at[a, i]))
    for one in fetches:
        one.start()
    for fetch, move in zip(fetches, moves):
        fetch.wait()
        move.start()
    for one in moves:
        one.wait()


def shards(ndp, nctx, features, short_weights, filters, reach_panels, cotangent):
    filter_len, groups = filters.shape
    channels = features.shape[2]
    reach = filter_len // PANEL
    rows = features.shape[1]
    assert rows == PANEL and features.shape[0] == 1
    width = channels // nctx
    tiles = width // TILE
    units = width // UNIT
    tile_units = TILE // UNIT
    reach_row = reach_panels.reshape(1, groups)
    filled = reach * tile_units + UNIT
    early_rows = max(tiles - 1, 1) * (reach * tile_units + 3 * TAPS)
    chunk = -(-early_rows // (UNIT * ndp)) * UNIT
    assert nctx % 2 == 0
    hbm = pl.BlockSpec(memory_space=pltpu.HBM)
    dma = pltpu.SemaphoreType.DMA
    turned = pltpu.VMEM((nctx, TILE, PANEL), jnp.float32)
    results = [
        jax.ShapeDtypeStruct((rows, channels), jnp.bfloat16),
        jax.ShapeDtypeStruct((rows, channels), jnp.bfloat16),
        jax.ShapeDtypeStruct((filter_len, groups), jnp.float32),
        jax.ShapeDtypeStruct((3, TAPS, channels), jnp.float32),
    ]
    held = pl.pallas_call(
        functools.partial(layer_kernel, reach, ndp, nctx),
        in_specs=[hbm] * 5,
        out_specs=[hbm] * 4,
        out_shape=results,
        scratch_shapes=[
            pltpu.SemaphoreType.REGULAR,
            pltpu.SemaphoreType.REGULAR,
            pltpu.VMEM((ndp, filled, PANEL), jnp.bfloat16),
            pltpu.VMEM((filled, PANEL), jnp.bfloat16),
            pltpu.VMEM((2, nctx // 2, filled, PANEL), jnp.bfloat16),
            dma((ndp,)),
            dma((ndp,)),
            dma((nctx // 2,)),
            dma((nctx // 2,)),
            pltpu.VMEM((2, ndp, nctx // 2, chunk, PANEL), jnp.bfloat16),
            pltpu.VMEM((filter_len, groups), jnp.float32),
            pltpu.VMEM((3, TAPS, channels), jnp.float32),
            dma((2,)),
            pltpu.VMEM((3, TAPS, channels), jnp.float32),
            pltpu.VMEM((filter_len, groups), jnp.bfloat16),
            pltpu.VMEM((1, groups), jnp.int32),
            pltpu.VMEM((UNIT, PANEL), jnp.float32),
            pltpu.VMEM((width, UNIT), jnp.float32),
            pltpu.VMEM((units, filter_len), jnp.float32),
            dma((3,)),
            pltpu.VMEM((2, nctx, PANEL, width), jnp.bfloat16),
            pltpu.VMEM((2, nctx, PANEL, width), jnp.bfloat16),
            pltpu.VMEM((units, PANEL, filter_len), jnp.bfloat16),
            turned,
            turned,
            turned,
            turned,
            pltpu.VMEM((tile_units, filter_len), jnp.float32),
            pltpu.VMEM((TILE, PANEL), jnp.float32),
            pltpu.VMEM((ndp * chunk, PANEL), jnp.float32),
            pltpu.VMEM((ndp, chunk, PANEL), jnp.float32),
            pltpu.VMEM((chunk, PANEL), jnp.bfloat16),
            dma((2, tiles)),
            dma((2, tiles, nctx)),
            dma((2, tiles, nctx)),
            dma((2, tiles, nctx)),
            dma((2, tiles, nctx)),
            dma((2, tiles)),
            dma((ndp,)),
            dma((ndp,)),
            dma((ndp,)),
            dma((ndp,)),
            dma((nctx // 2,)),
            dma((nctx // 2,)),
            dma((2,)),
            dma((2,)),
        ],
        compiler_params=pltpu.CompilerParams(
            collective_id=0, has_side_effects=True, vmem_limit_bytes=58 * 2**20
        ),
    )(features[0], cotangent[0], short_weights, filters, reach_row)
    layer_out, input_grad, filter_grad, short_grad = pl.pallas_call(
        finish_kernel,
        in_specs=[hbm] * 4,
        out_specs=[hbm] * 4,
        out_shape=results,
        scratch_shapes=[pltpu.VMEM(one.shape, one.dtype) for one in results] + [dma((4, STRIPS))] * 2,
    )(*held)
    return (layer_out[None], input_grad[None], filter_grad, short_grad)


def solution(mesh):
    return jax.shard_map(
        functools.partial(shards, mesh.shape["dp"], mesh.shape["ctx"]),
        mesh=mesh,
        in_specs=(P("dp", "ctx", None), P(), P(), P(), P("dp", "ctx", None)),
        out_specs=(P("dp", "ctx", None), P("dp", "ctx", None), P(), P()),
        check_vma=False,
    )
```

```python
import functools

import jax
import jax.numpy as jnp
from jax import lax
from jax.experimental import pallas as pl
from jax.experimental.pallas import tpu as pltpu
from jax.sharding import PartitionSpec as P

PANEL = 128
UNIT = 16
TILE = 128
TAPS = 3
UNROLL = 4
AROUND = 8
MESH = pl.DeviceIdType.MESH


def rows_down(x, rows):
    return jnp.concatenate([jnp.zeros((rows, x.shape[1]), x.dtype), x[:-rows]], axis=0)


def rows_up(x, rows):
    return jnp.concatenate([x[rows:], jnp.zeros((rows, x.shape[1]), x.dtype)], axis=0)


def turn(place, count):
    return jnp.where(place >= count, place - count, place)


def causal():
    shape = (PANEL, PANEL)
    return lax.broadcasted_iota(jnp.int32, shape, 1) >= lax.broadcasted_iota(jnp.int32, shape, 0)


def toeplitz(taps):
    width = taps.shape[1]
    x = jnp.broadcast_to(taps, (8, width))
    row = lax.broadcasted_iota(jnp.int32, (8, width), 0)
    for bit in (1, 2, 4):
        x = jnp.where((row & bit) != 0, pltpu.roll(x, bit, 1), x)
    rows = 8
    while rows < PANEL:
        x = jnp.concatenate([x, pltpu.roll(x, rows, 1)], axis=0)
        rows *= 2
    first = jnp.where(causal(), x[:, :PANEL], 0.0)
    return jnp.concatenate([first, x[:, PANEL:]], axis=1).astype(jnp.bfloat16)


def lag_sums(products):
    width = products.shape[1]
    first = jnp.where(causal(), products[:, :PANEL], 0.0)
    x = jnp.concatenate([first, products[:, PANEL:]], axis=1)
    rows = PANEL // 2
    while rows >= 8:
        x = x[:rows] + pltpu.roll(x[rows:], width - rows, 1)
        rows //= 2
    for step in (4, 2, 1):
        x = x + pltpu.roll(pltpu.roll(x, 8 - step, 0), width - step, 1)
    return x[0:1]


def tile_terms(reach, panels, ft, ct, wt, spreads, out_t, in_t, fg, sg_t):
    rows = panels * UNIT

    def group(g, carry):
        first = pl.multiple_of(g * UNIT, UNIT)
        lane = lax.broadcasted_iota(jnp.int32, (rows, PANEL), 1)
        chan = pl.ds(first, UNIT)
        feat = ft[:, chan, :].reshape(rows, PANEL)
        cot = ct[:, chan, :].reshape(rows, PANEL)
        w_all = wt[chan, :]

        def weigh(k, x):
            w = jnp.broadcast_to(w_all[:, k : k + 1], (UNIT, PANEL))
            return (x.reshape(panels, UNIT, PANEL) * w[None]).reshape(rows, PANEL)

        feats = [feat]
        for tap in range(1, TAPS):
            turned = pltpu.roll(feat, tap, 1)
            feats.append(jnp.where(lane < tap, rows_down(turned, UNIT), turned))
        streams = []
        for m in range(3):
            total = weigh(m * TAPS, feats[0])
            for tap in range(1, TAPS):
                total = total + weigh(m * TAPS + tap, feats[tap])
            streams.append(total)
        query, key, value = streams
        mixed = (key * value).astype(jnp.bfloat16)
        grad_conv = (cot * query).astype(jnp.bfloat16)
        earlier = jnp.concatenate(
            [mixed] + [rows_down(mixed, o * UNIT) for o in range(1, reach)], axis=1
        )
        later = jnp.concatenate(
            [grad_conv] + [rows_up(grad_conv, o * UNIT) for o in range(1, reach)], axis=1
        )
        spread = spreads[g]
        stacked = jnp.concatenate(
            [spread[:, o * PANEL : (o + 1) * PANEL] for o in range(reach)], axis=0
        )
        conv = jnp.dot(earlier, stacked, preferred_element_type=jnp.float32)
        back = lax.dot_general(
            later, spread, (((1,), (1,)), ((), ())), preferred_element_type=jnp.float32
        )
        products = lax.dot_general(
            mixed, later, (((0,), (0,)), ((), ())), preferred_element_type=jnp.float32
        )
        fg[pl.ds(g, 1), :] = lag_sums(products)
        out_t[:, chan, :] = (query * conv).reshape(panels, UNIT, PANEL)
        grads = (cot * conv, back * value, back * key)
        grad_in = None
        for tap in range(TAPS):
            part = weigh(tap, grads[0]) + weigh(TAPS + tap, grads[1]) + weigh(2 * TAPS + tap, grads[2])
            if tap:
                turned = pltpu.roll(part, PANEL - tap, 1)
                part = jnp.where(lane >= PANEL - tap, rows_up(turned, UNIT), turned)
            grad_in = part if grad_in is None else grad_in + part
        in_t[:, chan, :] = grad_in.reshape(panels, UNIT, PANEL)
        small_lane = lax.broadcasted_iota(jnp.int32, (UNIT, PANEL), 1)
        sums = jnp.zeros((UNIT, PANEL), jnp.float32)
        for m in range(3):
            for tap in range(TAPS):
                part = jnp.sum((grads[m] * feats[tap]).reshape(panels, UNIT, PANEL), axis=0)
                sums = jnp.where(small_lane == m * TAPS + tap, jnp.sum(part, axis=1, keepdims=True), sums)
        sg_t[chan, :] = sums
        return carry

    lax.fori_loop(0, TILE // UNIT, group, 0, unroll=UNROLL)


def layer_kernel(
    reach, ndp, nctx, f_hbm, c_hbm, sw_hbm, fl_hbm, rp_hbm, out_hbm, in_hbm, fg_hbm, sg_hbm,
    near, far, halves, tail, tail_all, zx_send, zx_recv, gl_send, gl_recv,
    every, fg_all, sg_all, last_sem, sw, fl, rp, wrow, wt, taps, small_sem, arrived, leaving, spreads, ft, ct, out_t, in_t, fg, sg_t, pay, parts, sums,
    own_sem, in_send, in_recv, out_send, out_recv, keep_sem,
    rs_send, rs_recv, gd_send, gd_recv, gc_send, gc_recv, pair_send, pair_recv,
):
    dp, me = lax.axis_index("dp"), lax.axis_index("ctx")
    width = arrived.shape[3]
    tiles = width // TILE
    chunk, filled = sums.shape[0], tail.shape[0]
    core, chip, chips = lax.rem(me, 2), me // 2, nctx // 2
    lag_count = reach * (TILE // UNIT)
    early = tiles - 1
    ins, outs = (f_hbm, c_hbm), (out_hbm, in_hbm)

    def ctx_peer(k):
        return turn(me + k, nctx)

    def ctx_from(k):
        return turn(me + nctx - k, nctx)

    def dp_peer(k):
        return turn(dp + k, ndp)

    def dp_from(k):
        return turn(dp + ndp - k, ndp)

    def lanes(j):
        return pl.ds(pl.multiple_of(j * TILE, TILE), TILE)

    def cols(owner, j):
        return pl.ds(pl.multiple_of(owner * width + j * TILE, TILE), TILE)

    def copy(src, dst, send, recv, device):
        return pltpu.make_async_remote_copy(
            src_ref=src, dst_ref=dst, send_sem=send, recv_sem=recv, device_id=device, device_id_type=MESH
        )

    def in_copy(a, j, k, slot):
        return copy(
            ins[a].at[:, cols(ctx_peer(k), j)],
            arrived.at[a, slot, :, lanes(j)],
            in_send.at[a, j, k],
            in_recv.at[a, j, k],
            (dp, ctx_peer(k)),
        )

    def in_own(a, j):
        return pltpu.make_async_copy(
            ins[a].at[:, cols(me, j)], arrived.at[a, me, :, lanes(j)], own_sem.at[a, j]
        )

    def out_copy(a, j, k, slot):
        return copy(
            leaving.at[a, ctx_peer(k), :, lanes(j)],
            outs[a].at[:, cols(slot, j)],
            out_send.at[a, j, k],
            out_recv.at[a, j, k],
            (dp, ctx_peer(k)),
        )

    def out_own(a, j):
        return pltpu.make_async_copy(
            leaving.at[a, me, :, lanes(j)], outs[a].at[:, cols(me, j)], keep_sem.at[a, j]
        )

    def rs_copy(k):
        part = pl.ds(pl.multiple_of(dp_peer(k) * chunk, chunk), chunk)
        return copy(pay.at[part], parts.at[k], rs_send.at[k], rs_recv.at[k], (dp_peer(k), me))

    def gc_copy(k, slot):
        return copy(sums, every.at[core, dp, slot], gc_send.at[k], gc_recv.at[k], (dp, ctx_peer(2 * k)))

    def gd_copy(k, slot):
        return copy(
            every.at[core, dp], every.at[core, slot], gd_send.at[k], gd_recv.at[k], (dp_peer(k), me)
        )

    def zx_copy(k, slot):
        return copy(halves.at[dp], halves.at[slot], zx_send.at[k], zx_recv.at[k], (dp_peer(k), me))

    def gl_copy(k, slot):
        return copy(tail, tail_all.at[core, slot], gl_send.at[k], gl_recv.at[k], (dp, ctx_peer(2 * k)))

    def pair_copy(i, which):
        ref = (every, tail_all)[i]
        return copy(
            ref.at[which], ref.at[which], pair_send.at[i], pair_recv.at[i], (dp, me + 1 - 2 * core)
        )

    def each(count, body, unroll=1):
        if count < 1:
            return
        unroll = max(1, min(unroll, count))

        def step(i, carry):
            body(i)
            return carry

        lax.fori_loop(0, count, step, 0, unroll=unroll)

    small = [
        pltpu.make_async_copy(src, dst, small_sem.at[i])
        for i, (src, dst) in enumerate(((sw_hbm, sw), (fl_hbm, fl), (rp_hbm, rp)))
    ]
    for one in small:
        one.start()
    barrier = pltpu.get_barrier_semaphore()
    others = [ctx_peer(k) for k in range(1, nctx)]
    for other in others:

        @pl.when(other != 0)
        def _():
            pl.semaphore_signal(barrier, inc=1, device_id=(dp, other), device_id_type=MESH)

    for a in range(2):
        each(tiles, lambda j: in_own(a, j).start())

    @pl.when(me != 0)
    def _():
        pl.semaphore_wait(barrier, nctx - 1)
        pl.semaphore_signal(near, inc=1, device_id=(dp, 0), device_id_type=MESH)

    @pl.when(me == 0)
    def _():
        pl.semaphore_wait(near, nctx - 1)
        for k in range(1, ndp):
            pl.semaphore_signal(barrier, inc=1, device_id=(dp_peer(k), 0), device_id_type=MESH)

    def send_in(j):
        for a in range(2):
            each(nctx - 1, unroll=AROUND, body=lambda i: in_copy(a, j, i + 1, me).start())

    ahead = min(2, tiles)
    each(ahead, send_in)
    for one in small:
        one.wait()
    units = taps.shape[0]
    group = me * units
    block = pl.ds(pl.multiple_of(group // PANEL * PANEL, PANEL), PANEL)
    lag_pos = lax.broadcasted_iota(jnp.int32, (fl.shape[0], PANEL), 0)
    masked = jnp.where(lag_pos < rp[:, block] * PANEL, fl[:, block].astype(jnp.float32), 0.0)
    masked = pltpu.roll(masked, lax.rem(PANEL - lax.rem(group, PANEL), PANEL), 1)
    for o in range(reach):
        taps[:, o * PANEL : (o + 1) * PANEL] = masked[o * PANEL : (o + 1) * PANEL].T[:units]
    wrow[...] = jnp.zeros_like(wrow)

    def turn_weights(j):
        for m in range(3):
            wrow[m * TAPS : (m + 1) * TAPS] = sw[m, :, cols(me, j)]
        wt[lanes(j), :] = wrow[...].T

    each(tiles, turn_weights)

    def build(g):
        spreads[g] = toeplitz(taps[pl.ds(g, 1), :])

    each(taps.shape[0], build, UNROLL)

    @pl.when(me == 0)
    def _():
        pl.semaphore_wait(barrier, ndp - 1)
        for other in others:
            pl.semaphore_signal(far, inc=1, device_id=(dp, other), device_id_type=MESH)

    @pl.when(me != 0)
    def _():
        pl.semaphore_wait(far, 1)

    def spread_ctx():
        each(ndp - 1, unroll=AROUND, body=lambda i: rs_copy(i + 1).wait_recv())
        total = pay[pl.ds(pl.multiple_of(dp * chunk, chunk), chunk)]
        for k in range(1, ndp):
            total = total + parts[k]
        sums[...] = total.astype(jnp.bfloat16)
        every[core, dp, chip] = sums[...]
        each(chips - 1, unroll=AROUND, body=lambda i: gc_copy(i + 1, chip).start())

    def spread_dp():
        each(chips - 1, unroll=AROUND, body=lambda i: gc_copy(i + 1, ctx_from(2 * i + 2) // 2).wait_recv())
        each(ndp - 1, unroll=AROUND, body=lambda i: gd_copy(i + 1, dp).start())

    def send_out(a, j):
        out_own(a, j).start()
        each(nctx - 1, unroll=AROUND, body=lambda i: out_copy(a, j, i + 1, me).start())

    def one_tile(j):
        for a in range(2):
            in_own(a, j).wait()
            each(
                nctx - 1,
                unroll=AROUND,
                body=lambda i: in_copy(a, j, i + 1, ctx_from(i + 1)).wait_recv(),
            )

        @pl.when(j + ahead < tiles)
        def _():
            send_in(j + ahead)

        def turn_in(n):
            ft[n] = arrived[0, n, :, lanes(j)].astype(jnp.float32).T
            ct[n] = arrived[1, n, :, lanes(j)].astype(jnp.float32).T

        each(nctx, turn_in, UNROLL)
        units = TILE // UNIT
        tile_terms(
            reach, nctx, ft, ct, wt.at[lanes(j), :],
            spreads.at[pl.ds(j * units, units)], out_t, in_t, fg, sg_t,
        )

        def turn_out(n):
            leaving[0, n, :, lanes(j)] = out_t[n].T.astype(jnp.bfloat16)
            leaving[1, n, :, lanes(j)] = in_t[n].T.astype(jnp.bfloat16)

        each(nctx, turn_out, UNROLL)
        lags = jnp.concatenate([fg[:, o * PANEL : (o + 1) * PANEL] for o in range(reach)], axis=0)
        shorts = sg_t[...].T[:UNIT]

        @pl.when(j < early)
        def _():
            pay[pl.ds(pl.multiple_of(j * lag_count, lag_count), lag_count)] = lags

        for place in range(early):

            @pl.when(j == place)
            def _():
                first = early * lag_count + place * 3 * TAPS
                pay[first : first + 3 * TAPS] = shorts[: 3 * TAPS]

        @pl.when(j == early - 1)
        def _():
            each(ndp - 1, unroll=AROUND, body=lambda i: rs_copy(i + 1).start())

        @pl.when(j == early)
        def _():
            halves[dp] = jnp.concatenate([lags, shorts], axis=0).astype(jnp.bfloat16)
            each(ndp - 1, unroll=AROUND, body=lambda i: zx_copy(i + 1, dp).start())

        @pl.when(j < early)
        def _():
            send_out(0, j)

        @pl.when(j < early - 1)
        def _():
            send_out(1, j)

        @pl.when(j == early)
        def _():
            if early:
                spread_ctx()
                send_out(1, j - 1)
            each(ndp - 1, unroll=AROUND, body=lambda i: zx_copy(i + 1, dp_from(i + 1)).wait_recv())
            total = halves[0].astype(jnp.float32)
            for k in range(1, ndp):
                total = total + halves[k].astype(jnp.float32)
            tail[...] = total.astype(jnp.bfloat16)
            tail_all[core, chip] = tail[...]
            each(chips - 1, unroll=AROUND, body=lambda i: gl_copy(i + 1, chip).start())
            send_out(0, j)
            if early:
                spread_dp()
            send_out(1, j)
            each(
                chips - 1,
                unroll=AROUND,
                body=lambda i: gl_copy(i + 1, ctx_from(2 * i + 2) // 2).wait_recv(),
            )
            pair_copy(1, core).start()

    if early:
        pay[early * (lag_count + 3 * TAPS) :] = jnp.zeros(
            (pay.shape[0] - early * (lag_count + 3 * TAPS), PANEL), jnp.float32
        )
    each(tiles, one_tile)
    if early:
        each(ndp - 1, unroll=AROUND, body=lambda i: gd_copy(i + 1, dp_from(i + 1)).wait_recv())
        pair_copy(0, core).start()
    pair_copy(1, 1 - core).wait_recv()
    if early:
        pair_copy(0, 1 - core).wait_recv()
    lag_rows = [[] for _ in range(reach)]
    width_units = TILE // UNIT
    for n in range(nctx):
        if early:
            before = every[n % 2, :, n // 2].astype(jnp.float32).reshape(-1, PANEL)
        for j in range(tiles):
            if j < early:
                lags = before[j * lag_count : (j + 1) * lag_count]
                row = early * lag_count + j * 3 * TAPS
                shorts = before[row : row + 3 * TAPS]
            else:
                terms = tail_all[n % 2, n // 2].astype(jnp.float32)
                lags, shorts = terms[:lag_count], terms[lag_count : lag_count + 3 * TAPS]
            for o in range(reach):
                lag_rows[o].append(lags[o * width_units : (o + 1) * width_units])
            first = (n * tiles + j) * TILE
            for m in range(3):
                sg_all[m, :, first : first + TILE] = shorts[m * TAPS : (m + 1) * TAPS]
    lag_pos = lax.broadcasted_iota(jnp.int32, (PANEL, fg_all.shape[1]), 0)
    for o in range(reach):
        lags = jnp.concatenate(lag_rows[o], axis=0).T
        fg_all[o * PANEL : (o + 1) * PANEL] = jnp.where(lag_pos + o * PANEL < rp[...] * PANEL, lags, 0.0)
    last = [
        pltpu.make_async_copy(src, dst, last_sem.at[i])
        for i, (src, dst) in enumerate(((fg_all, fg_hbm), (sg_all, sg_hbm)))
    ]
    for one in last:
        one.start()

    def finish(j):
        for a in range(2):
            each(nctx - 1, unroll=AROUND, body=lambda i: in_copy(a, j, i + 1, me).wait_send())
            out_own(a, j).wait()
            each(nctx - 1, unroll=AROUND, body=lambda i: out_copy(a, j, i + 1, me).wait_send())
            each(
                nctx - 1,
                unroll=AROUND,
                body=lambda i: out_copy(a, j, i + 1, ctx_from(i + 1)).wait_recv(),
            )

    if early:
        each(ndp - 1, unroll=AROUND, body=lambda i: rs_copy(i + 1).wait_send())
        each(chips - 1, unroll=AROUND, body=lambda i: gc_copy(i + 1, chip).wait_send())
        each(ndp - 1, unroll=AROUND, body=lambda i: gd_copy(i + 1, dp).wait_send())
        pair_copy(0, core).wait_send()
    each(ndp - 1, unroll=AROUND, body=lambda i: zx_copy(i + 1, dp).wait_send())
    each(chips - 1, unroll=AROUND, body=lambda i: gl_copy(i + 1, chip).wait_send())
    pair_copy(1, core).wait_send()
    each(tiles, finish)
    for one in last:
        one.wait()


def finish_kernel(*refs):
    sem = refs[-1]
    moves = [
        pltpu.make_async_copy(src, dst, sem.at[i]) for i, (src, dst) in enumerate(zip(refs[:4], refs[4:8]))
    ]
    for one in moves:
        one.start()
    for one in moves:
        one.wait()


def shards(ndp, nctx, features, short_weights, filters, reach_panels, cotangent):
    filter_len, groups = filters.shape
    channels = features.shape[2]
    reach = filter_len // PANEL
    rows = features.shape[1]
    assert rows == PANEL and features.shape[0] == 1
    width = channels // nctx
    tiles = width // TILE
    units = width // UNIT
    tile_units = TILE // UNIT
    reach_row = reach_panels.reshape(1, groups)
    filled = reach * tile_units + UNIT
    early_rows = max(tiles - 1, 1) * (reach * tile_units + 3 * TAPS)
    chunk = -(-early_rows // (UNIT * ndp)) * UNIT
    assert nctx % 2 == 0
    hbm = pl.BlockSpec(memory_space=pltpu.HBM)
    dma = pltpu.SemaphoreType.DMA
    turned = pltpu.VMEM((nctx, TILE, PANEL), jnp.float32)
    results = [
        jax.ShapeDtypeStruct((rows, channels), jnp.bfloat16),
        jax.ShapeDtypeStruct((rows, channels), jnp.bfloat16),
        jax.ShapeDtypeStruct((filter_len, groups), jnp.float32),
        jax.ShapeDtypeStruct((3, TAPS, channels), jnp.float32),
    ]
    held = pl.pallas_call(
        functools.partial(layer_kernel, reach, ndp, nctx),
        in_specs=[hbm] * 5,
        out_specs=[hbm] * 4,
        out_shape=results,
        scratch_shapes=[
            pltpu.SemaphoreType.REGULAR,
            pltpu.SemaphoreType.REGULAR,
            pltpu.VMEM((ndp, filled, PANEL), jnp.bfloat16),
            pltpu.VMEM((filled, PANEL), jnp.bfloat16),
            pltpu.VMEM((2, nctx // 2, filled, PANEL), jnp.bfloat16),
            dma((ndp,)),
            dma((ndp,)),
            dma((nctx // 2,)),
            dma((nctx // 2,)),
            pltpu.VMEM((2, ndp, nctx // 2, chunk, PANEL), jnp.bfloat16),
            pltpu.VMEM((filter_len, groups), jnp.float32),
            pltpu.VMEM((3, TAPS, channels), jnp.float32),
            dma((2,)),
            pltpu.VMEM((3, TAPS, channels), jnp.float32),
            pltpu.VMEM((filter_len, groups), jnp.bfloat16),
            pltpu.VMEM((1, groups), jnp.int32),
            pltpu.VMEM((UNIT, PANEL), jnp.float32),
            pltpu.VMEM((width, UNIT), jnp.float32),
            pltpu.VMEM((units, filter_len), jnp.float32),
            dma((3,)),
            pltpu.VMEM((2, nctx, PANEL, width), jnp.bfloat16),
            pltpu.VMEM((2, nctx, PANEL, width), jnp.bfloat16),
            pltpu.VMEM((units, PANEL, filter_len), jnp.bfloat16),
            turned,
            turned,
            turned,
            turned,
            pltpu.VMEM((tile_units, filter_len), jnp.float32),
            pltpu.VMEM((TILE, PANEL), jnp.float32),
            pltpu.VMEM((ndp * chunk, PANEL), jnp.float32),
            pltpu.VMEM((ndp, chunk, PANEL), jnp.float32),
            pltpu.VMEM((chunk, PANEL), jnp.bfloat16),
            dma((2, tiles)),
            dma((2, tiles, nctx)),
            dma((2, tiles, nctx)),
            dma((2, tiles, nctx)),
            dma((2, tiles, nctx)),
            dma((2, tiles)),
            dma((ndp,)),
            dma((ndp,)),
            dma((ndp,)),
            dma((ndp,)),
            dma((nctx // 2,)),
            dma((nctx // 2,)),
            dma((2,)),
            dma((2,)),
        ],
        compiler_params=pltpu.CompilerParams(
            collective_id=0, has_side_effects=True, vmem_limit_bytes=50 * 2**20
        ),
    )(*(pltpu.with_memory_space_constraint(one, pltpu.HBM) for one in (features[0], cotangent[0], short_weights, filters, reach_row)))
    layer_out, input_grad, filter_grad, short_grad = pl.pallas_call(
        finish_kernel,
        in_specs=[pl.BlockSpec(memory_space=pltpu.VMEM)] * 4,
        out_specs=[hbm] * 4,
        out_shape=results,
        scratch_shapes=[dma((4,))],
        compiler_params=pltpu.CompilerParams(vmem_limit_bytes=8 * 2**20),
    )(*held)
    return (layer_out[None], input_grad[None], filter_grad, short_grad)


def solution(mesh):
    return jax.shard_map(
        functools.partial(shards, mesh.shape["dp"], mesh.shape["ctx"]),
        mesh=mesh,
        in_specs=(P("dp", "ctx", None), P(), P(), P(), P("dp", "ctx", None)),
        out_specs=(P("dp", "ctx", None), P("dp", "ctx", None), P(), P()),
        check_vma=False,
    )
```

```python
import functools

import jax
import jax.numpy as jnp
from jax import lax
from jax.experimental import pallas as pl
from jax.experimental.pallas import tpu as pltpu
from jax.sharding import PartitionSpec as P

PANEL = 128
UNIT = 16
TILE = 128
TAPS = 3
UNROLL = 4
AROUND = 8
IN_SIZES = (1,)
OUT_SIZES = (1,)
MESH = pl.DeviceIdType.MESH


def rows_down(x, rows):
    return jnp.concatenate([jnp.zeros((rows, x.shape[1]), x.dtype), x[:-rows]], axis=0)


def rows_up(x, rows):
    return jnp.concatenate([x[rows:], jnp.zeros((rows, x.shape[1]), x.dtype)], axis=0)


def turn(place, count):
    return jnp.where(place >= count, place - count, place)


def spans(tiles, sizes):
    found, first = [], 0
    while first < tiles:
        count = min(sizes[min(len(found), len(sizes) - 1)], tiles - first)
        found.append((first, count))
        first += count
    return found


def causal():
    shape = (PANEL, PANEL)
    return lax.broadcasted_iota(jnp.int32, shape, 1) >= lax.broadcasted_iota(jnp.int32, shape, 0)


def toeplitz(taps):
    width = taps.shape[1]
    x = jnp.broadcast_to(taps, (8, width))
    row = lax.broadcasted_iota(jnp.int32, (8, width), 0)
    for bit in (1, 2, 4):
        x = jnp.where((row & bit) != 0, pltpu.roll(x, bit, 1), x)
    rows = 8
    while rows < PANEL:
        x = jnp.concatenate([x, pltpu.roll(x, rows, 1)], axis=0)
        rows *= 2
    first = jnp.where(causal(), x[:, :PANEL], 0.0)
    return jnp.concatenate([first, x[:, PANEL:]], axis=1).astype(jnp.bfloat16)


def lag_sums(products):
    width = products.shape[1]
    first = jnp.where(causal(), products[:, :PANEL], 0.0)
    x = jnp.concatenate([first, products[:, PANEL:]], axis=1)
    rows = PANEL // 2
    while rows >= 8:
        x = x[:rows] + pltpu.roll(x[rows:], width - rows, 1)
        rows //= 2
    return x


def row_sums(partial):
    reach = partial.shape[0]
    total = None
    for row in range(8):
        picked = pl.ds(row, TILE // UNIT, stride=8)
        x = jnp.concatenate([partial.at[o][picked, :] for o in range(reach)], axis=1)
        total = x if total is None else total + pltpu.roll(x, reach * PANEL - row, 1)
    return total


def tile_terms(reach, panels, ft, ct, wt, spreads, out_t, in_t, fg, sg_t):
    rows = panels * UNIT

    def group(g, carry):
        first = pl.multiple_of(g * UNIT, UNIT)
        lane = lax.broadcasted_iota(jnp.int32, (rows, PANEL), 1)
        chan = pl.ds(first, UNIT)
        feat = ft[:, chan, :].reshape(rows, PANEL)
        cot = ct[:, chan, :].reshape(rows, PANEL)
        w_all = wt[chan, :]

        def weigh(k, x):
            w = jnp.broadcast_to(w_all[:, k : k + 1], (UNIT, PANEL))
            return (x.reshape(panels, UNIT, PANEL) * w[None]).reshape(rows, PANEL)

        feats = [feat]
        for tap in range(1, TAPS):
            turned = pltpu.roll(feat, tap, 1)
            feats.append(jnp.where(lane < tap, rows_down(turned, UNIT), turned))
        streams = []
        for m in range(3):
            total = weigh(m * TAPS, feats[0])
            for tap in range(1, TAPS):
                total = total + weigh(m * TAPS + tap, feats[tap])
            streams.append(total)
        query, key, value = streams
        mixed = (key * value).astype(jnp.bfloat16)
        grad_conv = (cot * query).astype(jnp.bfloat16)
        earlier = jnp.concatenate(
            [mixed] + [rows_down(mixed, o * UNIT) for o in range(1, reach)], axis=1
        )
        later = jnp.concatenate(
            [grad_conv] + [rows_up(grad_conv, o * UNIT) for o in range(1, reach)], axis=1
        )
        spread = spreads[g]
        stacked = jnp.concatenate(
            [spread[:, o * PANEL : (o + 1) * PANEL] for o in range(reach)], axis=0
        )
        conv = jnp.dot(earlier, stacked, preferred_element_type=jnp.float32)
        back = lax.dot_general(
            later, spread, (((1,), (1,)), ((), ())), preferred_element_type=jnp.float32
        )
        products = lax.dot_general(
            mixed, later, (((0,), (0,)), ((), ())), preferred_element_type=jnp.float32
        )
        lags = lag_sums(products)
        for o in range(reach):
            fg[o, pl.ds(pl.multiple_of(g * 8, 8), 8), :] = lags[:, o * PANEL : (o + 1) * PANEL]
        out_t[:, chan, :] = (query * conv).reshape(panels, UNIT, PANEL)
        grads = (cot * conv, back * value, back * key)
        grad_in = None
        for tap in range(TAPS):
            part = weigh(tap, grads[0]) + weigh(TAPS + tap, grads[1]) + weigh(2 * TAPS + tap, grads[2])
            if tap:
                turned = pltpu.roll(part, PANEL - tap, 1)
                part = jnp.where(lane >= PANEL - tap, rows_up(turned, UNIT), turned)
            grad_in = part if grad_in is None else grad_in + part
        in_t[:, chan, :] = grad_in.reshape(panels, UNIT, PANEL)
        small_lane = lax.broadcasted_iota(jnp.int32, (UNIT, PANEL), 1)
        parts = jnp.concatenate(
            [
                jnp.sum((grads[m] * feats[tap]).reshape(panels, UNIT, PANEL), axis=0)
                for m in range(3)
                for tap in range(TAPS)
            ],
            axis=0,
        )
        high = parts.astype(jnp.bfloat16)
        low = (parts - high.astype(jnp.float32)).astype(jnp.bfloat16)
        ones = jnp.ones((PANEL, PANEL), jnp.bfloat16)
        added = jnp.dot(high, ones, preferred_element_type=jnp.float32) + jnp.dot(
            low, ones, preferred_element_type=jnp.float32
        )
        sums = jnp.zeros((UNIT, PANEL), jnp.float32)
        for k in range(3 * TAPS):
            sums = jnp.where(small_lane == k, added[k * UNIT : (k + 1) * UNIT], sums)
        sg_t[chan, :] = sums
        return carry

    lax.fori_loop(0, TILE // UNIT, group, 0, unroll=UNROLL)


def layer_kernel(
    reach, ndp, nctx, f_hbm, c_hbm, sw_hbm, fl_hbm, rp_hbm, out_hbm, in_hbm, fg_hbm, sg_hbm,
    near, far, halves, tail, tail_all, zx_send, zx_recv, gl_send, gl_recv,
    every, fg_all, sg_all, last_sem, sw, fl, rp, wrow, wt, taps, small_sem, arrived, leaving, spreads, ft, ct, out_t, in_t, fg, sg_t, pay, parts, sums,
    own_sem, in_send, in_recv, out_send, out_recv, keep_sem,
    rs_send, rs_recv, gd_send, gd_recv, gc_send, gc_recv, pair_send, pair_recv,
):
    dp, me = lax.axis_index("dp"), lax.axis_index("ctx")
    width = arrived.shape[3]
    tiles = width // TILE
    chunk, filled = sums.shape[0], tail.shape[0]
    core, chip, chips = lax.rem(me, 2), me // 2, nctx // 2
    lag_count = reach * (TILE // UNIT)
    early = tiles - 1
    ins, outs = (f_hbm, c_hbm), (out_hbm, in_hbm)

    def ctx_peer(k):
        return turn(me + k, nctx)

    def ctx_from(k):
        return turn(me + nctx - k, nctx)

    def dp_peer(k):
        return turn(dp + k, ndp)

    def dp_from(k):
        return turn(dp + ndp - k, ndp)

    in_spans, out_spans = spans(tiles, IN_SIZES), spans(tiles, OUT_SIZES)

    def lanes(j, count=1):
        return pl.ds(pl.multiple_of(j * TILE, TILE), count * TILE)

    def cols(owner, j, count=1):
        return pl.ds(pl.multiple_of(owner * width + j * TILE, TILE), count * TILE)

    def copy(src, dst, send, recv, device):
        return pltpu.make_async_remote_copy(
            src_ref=src, dst_ref=dst, send_sem=send, recv_sem=recv, device_id=device, device_id_type=MESH
        )

    def in_copy(a, span, k, slot):
        j, count = span
        return copy(
            ins[a].at[:, cols(ctx_peer(k), j, count)],
            arrived.at[a, slot, :, lanes(j, count)],
            in_send.at[a, j, k],
            in_recv.at[a, j, k],
            (dp, ctx_peer(k)),
        )

    def in_own(a, j):
        return pltpu.make_async_copy(
            ins[a].at[:, cols(me, j)], arrived.at[a, me, :, lanes(j)], own_sem.at[a, j]
        )

    def out_copy(a, span, k, slot):
        j, count = span
        return copy(
            leaving.at[a, ctx_peer(k), :, lanes(j, count)],
            outs[a].at[:, cols(slot, j, count)],
            out_send.at[a, j, k],
            out_recv.at[a, j, k],
            (dp, ctx_peer(k)),
        )

    def out_own(a, j):
        return pltpu.make_async_copy(
            leaving.at[a, me, :, lanes(j)], outs[a].at[:, cols(me, j)], keep_sem.at[a, j]
        )

    def rs_copy(k):
        part = pl.ds(pl.multiple_of(dp_peer(k) * chunk, chunk), chunk)
        return copy(pay.at[part], parts.at[k], rs_send.at[k], rs_recv.at[k], (dp_peer(k), me))

    def gc_copy(k, slot):
        return copy(sums, every.at[core, dp, slot], gc_send.at[k], gc_recv.at[k], (dp, ctx_peer(2 * k)))

    def gd_copy(k, slot):
        return copy(
            every.at[core, dp], every.at[core, slot], gd_send.at[k], gd_recv.at[k], (dp_peer(k), me)
        )

    def zx_copy(k, slot):
        return copy(halves.at[dp], halves.at[slot], zx_send.at[k], zx_recv.at[k], (dp_peer(k), me))

    def gl_copy(k, slot):
        return copy(tail, tail_all.at[core, slot], gl_send.at[k], gl_recv.at[k], (dp, ctx_peer(2 * k)))

    def pair_copy(i, which):
        ref = (every, tail_all)[i]
        return copy(
            ref.at[which], ref.at[which], pair_send.at[i], pair_recv.at[i], (dp, me + 1 - 2 * core)
        )

    def each(count, body, unroll=1):
        if count < 1:
            return
        unroll = max(1, min(unroll, count))

        def step(i, carry):
            body(i)
            return carry

        lax.fori_loop(0, count, step, 0, unroll=unroll)

    small = [
        pltpu.make_async_copy(src, dst, small_sem.at[i])
        for i, (src, dst) in enumerate(((sw_hbm, sw), (fl_hbm, fl), (rp_hbm, rp)))
    ]
    for one in small:
        one.start()
    barrier = pltpu.get_barrier_semaphore()
    others = [ctx_peer(k) for k in range(1, nctx)]
    for other in others:

        @pl.when(other != 0)
        def _():
            pl.semaphore_signal(barrier, inc=1, device_id=(dp, other), device_id_type=MESH)

    for a in range(2):
        each(tiles, lambda j: in_own(a, j).start())

    @pl.when(me != 0)
    def _():
        pl.semaphore_wait(barrier, nctx - 1)
        pl.semaphore_signal(near, inc=1, device_id=(dp, 0), device_id_type=MESH)

    @pl.when(me == 0)
    def _():
        pl.semaphore_wait(near, nctx - 1)
        for k in range(1, ndp):
            pl.semaphore_signal(barrier, inc=1, device_id=(dp_peer(k), 0), device_id_type=MESH)

    for span in in_spans:
        for a in range(2):
            each(nctx - 1, unroll=AROUND, body=lambda i: in_copy(a, span, i + 1, me).start())
    for one in small:
        one.wait()
    units = taps.shape[0]
    group = me * units
    block = pl.ds(pl.multiple_of(group // PANEL * PANEL, PANEL), PANEL)
    lag_pos = lax.broadcasted_iota(jnp.int32, (fl.shape[0], PANEL), 0)
    masked = jnp.where(lag_pos < rp[:, block] * PANEL, fl[:, block].astype(jnp.float32), 0.0)
    masked = pltpu.roll(masked, lax.rem(PANEL - lax.rem(group, PANEL), PANEL), 1)
    for o in range(reach):
        taps[:, o * PANEL : (o + 1) * PANEL] = masked[o * PANEL : (o + 1) * PANEL].T[:units]
    wrow[...] = jnp.zeros_like(wrow)

    def turn_weights(j):
        for m in range(3):
            wrow[m * TAPS : (m + 1) * TAPS] = sw[m, :, cols(me, j)]
        wt[lanes(j), :] = wrow[...].T

    each(tiles, turn_weights)

    def build(g):
        spreads[g] = toeplitz(taps[pl.ds(g, 1), :])

    each(taps.shape[0], build, UNROLL)

    @pl.when(me == 0)
    def _():
        pl.semaphore_wait(barrier, ndp - 1)
        for other in others:
            pl.semaphore_signal(far, inc=1, device_id=(dp, other), device_id_type=MESH)

    @pl.when(me != 0)
    def _():
        pl.semaphore_wait(far, 1)

    def spread_ctx():
        each(ndp - 1, unroll=AROUND, body=lambda i: rs_copy(i + 1).wait_recv())
        total = pay[pl.ds(pl.multiple_of(dp * chunk, chunk), chunk)]
        for k in range(1, ndp):
            total = total + parts[k]
        sums[...] = total.astype(jnp.bfloat16)
        every[core, dp, chip] = sums[...]
        each(chips - 1, unroll=AROUND, body=lambda i: gc_copy(i + 1, chip).start())

    def spread_dp():
        each(chips - 1, unroll=AROUND, body=lambda i: gc_copy(i + 1, ctx_from(2 * i + 2) // 2).wait_recv())
        each(ndp - 1, unroll=AROUND, body=lambda i: gd_copy(i + 1, dp).start())

    def send_out(a, span):
        for j in range(span[0], span[0] + span[1]):
            out_own(a, j).start()
        each(nctx - 1, unroll=AROUND, body=lambda i: out_copy(a, span, i + 1, me).start())

    def one_tile(j):
        for a in range(2):
            in_own(a, j).wait()
        for span in in_spans:

            @pl.when(j == span[0])
            def _():
                for a in range(2):
                    each(
                        nctx - 1,
                        unroll=AROUND,
                        body=lambda i: in_copy(a, span, i + 1, ctx_from(i + 1)).wait_recv(),
                    )

        def turn_in(n):
            ft[n] = arrived[0, n, :, lanes(j)].astype(jnp.float32).T
            ct[n] = arrived[1, n, :, lanes(j)].astype(jnp.float32).T

        each(nctx, turn_in, UNROLL)
        units = TILE // UNIT
        tile_terms(
            reach, nctx, ft, ct, wt.at[lanes(j), :],
            spreads.at[pl.ds(j * units, units)], out_t, in_t, fg, sg_t,
        )

        def turn_out(n):
            leaving[0, n, :, lanes(j)] = out_t[n].T.astype(jnp.bfloat16)
            leaving[1, n, :, lanes(j)] = in_t[n].T.astype(jnp.bfloat16)

        each(nctx, turn_out, UNROLL)
        sums_now = row_sums(fg)
        lags = jnp.concatenate([sums_now[:, o * PANEL : (o + 1) * PANEL] for o in range(reach)], axis=0)
        shorts = sg_t[...].T[:UNIT]

        @pl.when(j < early)
        def _():
            pay[pl.ds(pl.multiple_of(j * lag_count, lag_count), lag_count)] = lags

        for place in range(early):

            @pl.when(j == place)
            def _():
                first = early * lag_count + place * 3 * TAPS
                pay[first : first + 3 * TAPS] = shorts[: 3 * TAPS]

        @pl.when(j == early - 1)
        def _():
            each(ndp - 1, unroll=AROUND, body=lambda i: rs_copy(i + 1).start())

        @pl.when(j == early)
        def _():
            halves[dp] = jnp.concatenate([lags, shorts], axis=0).astype(jnp.bfloat16)
            each(ndp - 1, unroll=AROUND, body=lambda i: zx_copy(i + 1, dp).start())

        for span in out_spans[:-1]:

            @pl.when(j == span[0] + span[1] - 1)
            def _():
                send_out(0, span)
                if span[0] + span[1] != early:
                    send_out(1, span)

        @pl.when(j == early)
        def _():
            if early:
                spread_ctx()
                if out_spans[-1][0] == early:
                    send_out(1, out_spans[-2])
            each(ndp - 1, unroll=AROUND, body=lambda i: zx_copy(i + 1, dp_from(i + 1)).wait_recv())
            total = halves[0].astype(jnp.float32)
            for k in range(1, ndp):
                total = total + halves[k].astype(jnp.float32)
            tail[...] = total.astype(jnp.bfloat16)
            tail_all[core, chip] = tail[...]
            each(chips - 1, unroll=AROUND, body=lambda i: gl_copy(i + 1, chip).start())
            send_out(0, out_spans[-1])
            if early:
                spread_dp()
            send_out(1, out_spans[-1])
            each(
                chips - 1,
                unroll=AROUND,
                body=lambda i: gl_copy(i + 1, ctx_from(2 * i + 2) // 2).wait_recv(),
            )
            pair_copy(1, core).start()

    if early:
        pay[early * (lag_count + 3 * TAPS) :] = jnp.zeros(
            (pay.shape[0] - early * (lag_count + 3 * TAPS), PANEL), jnp.float32
        )
    each(tiles, one_tile)
    if early:
        each(ndp - 1, unroll=AROUND, body=lambda i: gd_copy(i + 1, dp_from(i + 1)).wait_recv())
        pair_copy(0, core).start()
    pair_copy(1, 1 - core).wait_recv()
    if early:
        pair_copy(0, 1 - core).wait_recv()
    lag_rows = [[] for _ in range(reach)]
    width_units = TILE // UNIT
    for n in range(nctx):
        if early:
            before = every[n % 2, :, n // 2].astype(jnp.float32).reshape(-1, PANEL)
        for j in range(tiles):
            if j < early:
                lags = before[j * lag_count : (j + 1) * lag_count]
                row = early * lag_count + j * 3 * TAPS
                shorts = before[row : row + 3 * TAPS]
            else:
                terms = tail_all[n % 2, n // 2].astype(jnp.float32)
                lags, shorts = terms[:lag_count], terms[lag_count : lag_count + 3 * TAPS]
            for o in range(reach):
                lag_rows[o].append(lags[o * width_units : (o + 1) * width_units])
            first = (n * tiles + j) * TILE
            for m in range(3):
                sg_all[m, :, first : first + TILE] = shorts[m * TAPS : (m + 1) * TAPS]
    lag_pos = lax.broadcasted_iota(jnp.int32, (PANEL, fg_all.shape[1]), 0)
    for o in range(reach):
        lags = jnp.concatenate(lag_rows[o], axis=0).T
        fg_all[o * PANEL : (o + 1) * PANEL] = jnp.where(lag_pos + o * PANEL < rp[...] * PANEL, lags, 0.0)
    last = [
        pltpu.make_async_copy(src, dst, last_sem.at[i])
        for i, (src, dst) in enumerate(((fg_all, fg_hbm), (sg_all, sg_hbm)))
    ]
    for one in last:
        one.start()

    def finish():
        for a in range(2):
            for span in in_spans:
                each(nctx - 1, unroll=AROUND, body=lambda i: in_copy(a, span, i + 1, me).wait_send())
            each(tiles, lambda j: out_own(a, j).wait())
            for span in out_spans:
                each(nctx - 1, unroll=AROUND, body=lambda i: out_copy(a, span, i + 1, me).wait_send())
                each(
                    nctx - 1,
                    unroll=AROUND,
                    body=lambda i: out_copy(a, span, i + 1, ctx_from(i + 1)).wait_recv(),
                )

    if early:
        each(ndp - 1, unroll=AROUND, body=lambda i: rs_copy(i + 1).wait_send())
        each(chips - 1, unroll=AROUND, body=lambda i: gc_copy(i + 1, chip).wait_send())
        each(ndp - 1, unroll=AROUND, body=lambda i: gd_copy(i + 1, dp).wait_send())
        pair_copy(0, core).wait_send()
    each(ndp - 1, unroll=AROUND, body=lambda i: zx_copy(i + 1, dp).wait_send())
    each(chips - 1, unroll=AROUND, body=lambda i: gl_copy(i + 1, chip).wait_send())
    pair_copy(1, core).wait_send()
    finish()
    for one in last:
        one.wait()


def finish_kernel(*refs):
    sem = refs[-1]
    moves = [
        pltpu.make_async_copy(src, dst, sem.at[i]) for i, (src, dst) in enumerate(zip(refs[:4], refs[4:8]))
    ]
    for one in moves:
        one.start()
    for one in moves:
        one.wait()


def shards(ndp, nctx, features, short_weights, filters, reach_panels, cotangent):
    filter_len, groups = filters.shape
    channels = features.shape[2]
    reach = filter_len // PANEL
    rows = features.shape[1]
    assert rows == PANEL and features.shape[0] == 1
    width = channels // nctx
    tiles = width // TILE
    units = width // UNIT
    tile_units = TILE // UNIT
    reach_row = reach_panels.reshape(1, groups)
    filled = reach * tile_units + UNIT
    early_rows = max(tiles - 1, 1) * (reach * tile_units + 3 * TAPS)
    chunk = -(-early_rows // (UNIT * ndp)) * UNIT
    assert nctx % 2 == 0
    hbm = pl.BlockSpec(memory_space=pltpu.HBM)
    dma = pltpu.SemaphoreType.DMA
    turned = pltpu.VMEM((nctx, TILE, PANEL), jnp.float32)
    results = [
        jax.ShapeDtypeStruct((rows, channels), jnp.bfloat16),
        jax.ShapeDtypeStruct((rows, channels), jnp.bfloat16),
        jax.ShapeDtypeStruct((filter_len, groups), jnp.float32),
        jax.ShapeDtypeStruct((3, TAPS, channels), jnp.float32),
    ]
    held = pl.pallas_call(
        functools.partial(layer_kernel, reach, ndp, nctx),
        in_specs=[hbm] * 5,
        out_specs=[hbm] * 4,
        out_shape=results,
        scratch_shapes=[
            pltpu.SemaphoreType.REGULAR,
            pltpu.SemaphoreType.REGULAR,
            pltpu.VMEM((ndp, filled, PANEL), jnp.bfloat16),
            pltpu.VMEM((filled, PANEL), jnp.bfloat16),
            pltpu.VMEM((2, nctx // 2, filled, PANEL), jnp.bfloat16),
            dma((ndp,)),
            dma((ndp,)),
            dma((nctx // 2,)),
            dma((nctx // 2,)),
            pltpu.VMEM((2, ndp, nctx // 2, chunk, PANEL), jnp.bfloat16),
            pltpu.VMEM((filter_len, groups), jnp.float32),
            pltpu.VMEM((3, TAPS, channels), jnp.float32),
            dma((2,)),
            pltpu.VMEM((3, TAPS, channels), jnp.float32),
            pltpu.VMEM((filter_len, groups), jnp.bfloat16),
            pltpu.VMEM((1, groups), jnp.int32),
            pltpu.VMEM((UNIT, PANEL), jnp.float32),
            pltpu.VMEM((width, UNIT), jnp.float32),
            pltpu.VMEM((units, filter_len), jnp.float32),
            dma((3,)),
            pltpu.VMEM((2, nctx, PANEL, width), jnp.bfloat16),
            pltpu.VMEM((2, nctx, PANEL, width), jnp.bfloat16),
            pltpu.VMEM((units, PANEL, filter_len), jnp.bfloat16),
            turned,
            turned,
            turned,
            turned,
            pltpu.VMEM((reach, tile_units * 8, PANEL), jnp.float32),
            pltpu.VMEM((TILE, PANEL), jnp.float32),
            pltpu.VMEM((ndp * chunk, PANEL), jnp.float32),
            pltpu.VMEM((ndp, chunk, PANEL), jnp.float32),
            pltpu.VMEM((chunk, PANEL), jnp.bfloat16),
            dma((2, tiles)),
            dma((2, tiles, nctx)),
            dma((2, tiles, nctx)),
            dma((2, tiles, nctx)),
            dma((2, tiles, nctx)),
            dma((2, tiles)),
            dma((ndp,)),
            dma((ndp,)),
            dma((ndp,)),
            dma((ndp,)),
            dma((nctx // 2,)),
            dma((nctx // 2,)),
            dma((2,)),
            dma((2,)),
        ],
        compiler_params=pltpu.CompilerParams(
            collective_id=0, has_side_effects=True, vmem_limit_bytes=50 * 2**20
        ),
    )(*(pltpu.with_memory_space_constraint(one, pltpu.HBM) for one in (features[0], cotangent[0], short_weights, filters, reach_row)))
    layer_out, input_grad, filter_grad, short_grad = pl.pallas_call(
        finish_kernel,
        in_specs=[pl.BlockSpec(memory_space=pltpu.VMEM)] * 4,
        out_specs=[hbm] * 4,
        out_shape=results,
        scratch_shapes=[dma((4,))],
        compiler_params=pltpu.CompilerParams(vmem_limit_bytes=8 * 2**20),
    )(*held)
    return (layer_out[None], input_grad[None], filter_grad, short_grad)


def solution(mesh):
    return jax.shard_map(
        functools.partial(shards, mesh.shape["dp"], mesh.shape["ctx"]),
        mesh=mesh,
        in_specs=(P("dp", "ctx", None), P(), P(), P(), P("dp", "ctx", None)),
        out_specs=(P("dp", "ctx", None), P("dp", "ctx", None), P(), P()),
        check_vma=False,
    )
```

```python
import functools

import jax
import jax.numpy as jnp
from jax import lax
from jax.experimental import pallas as pl
from jax.experimental.pallas import tpu as pltpu
from jax.sharding import PartitionSpec as P

PANEL = 128
UNIT = 16
TILE = 128
TAPS = 3
UNROLL = 4
AROUND = 8
IN_SIZES = (1,)
OUT_SIZES = (1,)
MESH = pl.DeviceIdType.MESH


def rows_down(x, rows):
    return jnp.concatenate([jnp.zeros((rows, x.shape[1]), x.dtype), x[:-rows]], axis=0)


def rows_up(x, rows):
    return jnp.concatenate([x[rows:], jnp.zeros((rows, x.shape[1]), x.dtype)], axis=0)


def turn(place, count):
    return jnp.where(place >= count, place - count, place)


def spans(tiles, sizes):
    found, first = [], 0
    while first < tiles:
        count = min(sizes[min(len(found), len(sizes) - 1)], tiles - first)
        found.append((first, count))
        first += count
    return found


def causal():
    shape = (PANEL, PANEL)
    return lax.broadcasted_iota(jnp.int32, shape, 1) >= lax.broadcasted_iota(jnp.int32, shape, 0)


def toeplitz(taps):
    width = taps.shape[1]
    x = jnp.broadcast_to(taps, (8, width))
    row = lax.broadcasted_iota(jnp.int32, (8, width), 0)
    for bit in (1, 2, 4):
        x = jnp.where((row & bit) != 0, pltpu.roll(x, bit, 1), x)
    rows = 8
    while rows < PANEL:
        x = jnp.concatenate([x, pltpu.roll(x, rows, 1)], axis=0)
        rows *= 2
    first = jnp.where(causal(), x[:, :PANEL], 0.0)
    return jnp.concatenate([first, x[:, PANEL:]], axis=1).astype(jnp.bfloat16)


def lag_sums(products):
    width = products.shape[1]
    first = jnp.where(causal(), products[:, :PANEL], 0.0)
    x = jnp.concatenate([first, products[:, PANEL:]], axis=1)
    rows = PANEL // 2
    while rows >= 8:
        x = x[:rows] + pltpu.roll(x[rows:], width - rows, 1)
        rows //= 2
    return x


def row_sums(partial):
    reach = partial.shape[0]
    total = None
    for row in range(8):
        picked = pl.ds(row, TILE // UNIT, stride=8)
        x = jnp.concatenate([partial.at[o][picked, :] for o in range(reach)], axis=1)
        total = x if total is None else total + pltpu.roll(x, reach * PANEL - row, 1)
    return total


def tile_terms(reach, panels, ft, ct, wt, spreads, out_t, in_t, fg, sg_t):
    rows = panels * UNIT

    def group(g, carry):
        first = pl.multiple_of(g * UNIT, UNIT)
        lane = lax.broadcasted_iota(jnp.int32, (rows, PANEL), 1)
        chan = pl.ds(first, UNIT)
        feat = ft[:, chan, :].reshape(rows, PANEL)
        cot = ct[:, chan, :].reshape(rows, PANEL)
        w_all = wt[chan, :]

        def weigh(k, x):
            w = jnp.broadcast_to(w_all[:, k : k + 1], (UNIT, PANEL))
            return (x.reshape(panels, UNIT, PANEL) * w[None]).reshape(rows, PANEL)

        feats = [feat]
        for tap in range(1, TAPS):
            turned = pltpu.roll(feat, tap, 1)
            feats.append(jnp.where(lane < tap, rows_down(turned, UNIT), turned))
        streams = []
        for m in range(3):
            total = weigh(m * TAPS, feats[0])
            for tap in range(1, TAPS):
                total = total + weigh(m * TAPS + tap, feats[tap])
            streams.append(total)
        query, key, value = streams
        mixed = (key * value).astype(jnp.bfloat16)
        grad_conv = (cot * query).astype(jnp.bfloat16)
        earlier = jnp.concatenate(
            [mixed] + [rows_down(mixed, o * UNIT) for o in range(1, reach)], axis=1
        )
        later = jnp.concatenate(
            [grad_conv] + [rows_up(grad_conv, o * UNIT) for o in range(1, reach)], axis=1
        )
        spread = spreads[g]
        stacked = jnp.concatenate(
            [spread[:, o * PANEL : (o + 1) * PANEL] for o in range(reach)], axis=0
        )
        conv = jnp.dot(earlier, stacked, preferred_element_type=jnp.float32)
        back = lax.dot_general(
            later, spread, (((1,), (1,)), ((), ())), preferred_element_type=jnp.float32
        )
        products = lax.dot_general(
            mixed, later, (((0,), (0,)), ((), ())), preferred_element_type=jnp.float32
        )
        lags = lag_sums(products)
        for o in range(reach):
            fg[o, pl.ds(pl.multiple_of(g * 8, 8), 8), :] = lags[:, o * PANEL : (o + 1) * PANEL]
        out_t[:, chan, :] = (query * conv).reshape(panels, UNIT, PANEL)
        grads = (cot * conv, back * value, back * key)
        grad_in = None
        for tap in range(TAPS):
            part = weigh(tap, grads[0]) + weigh(TAPS + tap, grads[1]) + weigh(2 * TAPS + tap, grads[2])
            if tap:
                turned = pltpu.roll(part, PANEL - tap, 1)
                part = jnp.where(lane >= PANEL - tap, rows_up(turned, UNIT), turned)
            grad_in = part if grad_in is None else grad_in + part
        in_t[:, chan, :] = grad_in.reshape(panels, UNIT, PANEL)
        small_lane = lax.broadcasted_iota(jnp.int32, (UNIT, PANEL), 1)
        parts = jnp.concatenate(
            [
                jnp.sum((grads[m] * feats[tap]).reshape(panels, UNIT, PANEL), axis=0)
                for m in range(3)
                for tap in range(TAPS)
            ],
            axis=0,
        )
        high = parts.astype(jnp.bfloat16)
        low = (parts - high.astype(jnp.float32)).astype(jnp.bfloat16)
        ones = jnp.ones((PANEL, PANEL), jnp.bfloat16)
        added = jnp.dot(high, ones, preferred_element_type=jnp.float32) + jnp.dot(
            low, ones, preferred_element_type=jnp.float32
        )
        sums = jnp.zeros((UNIT, PANEL), jnp.float32)
        for k in range(3 * TAPS):
            sums = jnp.where(small_lane == k, added[k * UNIT : (k + 1) * UNIT], sums)
        sg_t[chan, :] = sums
        return carry

    lax.fori_loop(0, TILE // UNIT, group, 0, unroll=UNROLL)


def layer_kernel(
    reach, ndp, nctx, f_hbm, c_hbm, sw_hbm, fl_hbm, rp_hbm, out_hbm, in_hbm, fg_hbm, sg_hbm,
    near, far, halves, tail, tail_all, zx_send, zx_recv, gl_send, gl_recv,
    every, fg_all, sg_all, last_sem, sw, fl, rp, wrow, wt, taps, small_sem, arrived, leaving, spreads, ft, ct, out_t, in_t, fg, sg_t, pay, parts, sums,
    own_sem, in_send, in_recv, out_send, out_recv, keep_sem,
    rs_send, rs_recv, gd_send, gd_recv, gc_send, gc_recv, pair_send, pair_recv,
):
    dp, me = lax.axis_index("dp"), lax.axis_index("ctx")
    width = arrived.shape[3]
    tiles = width // TILE
    chunk, filled = sums.shape[0], tail.shape[0]
    core, chip, chips = lax.rem(me, 2), me // 2, nctx // 2
    lag_count = reach * (TILE // UNIT)
    early = tiles - 1
    ins, outs = (f_hbm, c_hbm), (out_hbm, in_hbm)

    def ctx_peer(k):
        return turn(me + k, nctx)

    def ctx_from(k):
        return turn(me + nctx - k, nctx)

    def dp_peer(k):
        return turn(dp + k, ndp)

    def dp_from(k):
        return turn(dp + ndp - k, ndp)

    in_spans, out_spans = spans(tiles, IN_SIZES), spans(tiles, OUT_SIZES)

    def lanes(j, count=1):
        return pl.ds(pl.multiple_of(j * TILE, TILE), count * TILE)

    def cols(owner, j, count=1):
        return pl.ds(pl.multiple_of(owner * width + j * TILE, TILE), count * TILE)

    def copy(src, dst, send, recv, device):
        return pltpu.make_async_remote_copy(
            src_ref=src, dst_ref=dst, send_sem=send, recv_sem=recv, device_id=device, device_id_type=MESH
        )

    def in_copy(a, span, k, slot):
        j, count = span
        return copy(
            ins[a].at[:, cols(ctx_peer(k), j, count)],
            arrived.at[a, slot, :, lanes(j, count)],
            in_send.at[a, j, k],
            in_recv.at[a, j, k],
            (dp, ctx_peer(k)),
        )

    def in_own(a, j):
        return pltpu.make_async_copy(
            ins[a].at[:, cols(me, j)], arrived.at[a, me, :, lanes(j)], own_sem.at[a, j]
        )

    def out_copy(a, span, k, slot):
        j, count = span
        return copy(
            leaving.at[a, ctx_peer(k), :, lanes(j, count)],
            outs[a].at[:, cols(slot, j, count)],
            out_send.at[a, j, k],
            out_recv.at[a, j, k],
            (dp, ctx_peer(k)),
        )

    def out_own(a, j):
        return pltpu.make_async_copy(
            leaving.at[a, me, :, lanes(j)], outs[a].at[:, cols(me, j)], keep_sem.at[a, j]
        )

    def rs_copy(k):
        part = pl.ds(pl.multiple_of(dp_peer(k) * chunk, chunk), chunk)
        return copy(pay.at[part], parts.at[k], rs_send.at[k], rs_recv.at[k], (dp_peer(k), me))

    def gc_copy(k, slot):
        return copy(sums, every.at[core, dp, slot], gc_send.at[k], gc_recv.at[k], (dp, ctx_peer(2 * k)))

    def gd_copy(k, slot):
        return copy(
            every.at[core, dp], every.at[core, slot], gd_send.at[k], gd_recv.at[k], (dp_peer(k), me)
        )

    def zx_copy(k, slot):
        return copy(halves.at[dp], halves.at[slot], zx_send.at[k], zx_recv.at[k], (dp_peer(k), me))

    def gl_copy(k, slot):
        return copy(tail, tail_all.at[core, slot], gl_send.at[k], gl_recv.at[k], (dp, ctx_peer(2 * k)))

    def pair_copy(i, which):
        ref = (every, tail_all)[i]
        return copy(
            ref.at[which], ref.at[which], pair_send.at[i], pair_recv.at[i], (dp, me + 1 - 2 * core)
        )

    def each(count, body, unroll=1):
        if count < 1:
            return
        unroll = max(1, min(unroll, count))

        def step(i, carry):
            body(i)
            return carry

        lax.fori_loop(0, count, step, 0, unroll=unroll)

    barrier = pltpu.get_barrier_semaphore()
    others = [ctx_peer(k) for k in range(1, nctx)]
    for other in others:

        @pl.when(other != 0)
        def _():
            pl.semaphore_signal(barrier, inc=1, device_id=(dp, other), device_id_type=MESH)

    small = [
        pltpu.make_async_copy(src, dst, small_sem.at[i])
        for i, (src, dst) in enumerate(((sw_hbm, sw), (fl_hbm, fl), (rp_hbm, rp)))
    ]
    for one in small:
        one.start()
    for a in range(2):
        each(tiles, lambda j: in_own(a, j).start())

    @pl.when(me != 0)
    def _():
        pl.semaphore_wait(barrier, nctx - 1)
        pl.semaphore_signal(near, inc=1, device_id=(dp, 0), device_id_type=MESH)

    @pl.when(me == 0)
    def _():
        pl.semaphore_wait(near, nctx - 1)
        for k in range(1, ndp):
            pl.semaphore_signal(barrier, inc=1, device_id=(dp_peer(k), 0), device_id_type=MESH)

    for span in in_spans:
        for a in range(2):
            each(nctx - 1, unroll=AROUND, body=lambda i: in_copy(a, span, i + 1, me).start())
    for one in small:
        one.wait()
    units = taps.shape[0]
    group = me * units
    block = pl.ds(pl.multiple_of(group // PANEL * PANEL, PANEL), PANEL)
    lag_pos = lax.broadcasted_iota(jnp.int32, (fl.shape[0], PANEL), 0)
    masked = jnp.where(lag_pos < rp[:, block] * PANEL, fl[:, block].astype(jnp.float32), 0.0)
    masked = pltpu.roll(masked, lax.rem(PANEL - lax.rem(group, PANEL), PANEL), 1)
    for o in range(reach):
        taps[:, o * PANEL : (o + 1) * PANEL] = masked[o * PANEL : (o + 1) * PANEL].T[:units]
    wrow[...] = jnp.zeros_like(wrow)

    def turn_weights(j):
        for m in range(3):
            wrow[m * TAPS : (m + 1) * TAPS] = sw[m, :, cols(me, j)]
        wt[lanes(j), :] = wrow[...].T

    each(tiles, turn_weights)

    def build(g):
        spreads[g] = toeplitz(taps[pl.ds(g, 1), :])

    each(taps.shape[0], build, UNROLL)

    @pl.when(me == 0)
    def _():
        pl.semaphore_wait(barrier, ndp - 1)
        for other in others:
            pl.semaphore_signal(far, inc=1, device_id=(dp, other), device_id_type=MESH)

    @pl.when(me != 0)
    def _():
        pl.semaphore_wait(far, 1)

    def spread_ctx():
        each(ndp - 1, unroll=AROUND, body=lambda i: rs_copy(i + 1).wait_recv())
        total = pay[pl.ds(pl.multiple_of(dp * chunk, chunk), chunk)]
        for k in range(1, ndp):
            total = total + parts[k]
        sums[...] = total.astype(jnp.bfloat16)
        every[core, dp, chip] = sums[...]
        each(chips - 1, unroll=AROUND, body=lambda i: gc_copy(i + 1, chip).start())

    def spread_dp():
        each(chips - 1, unroll=AROUND, body=lambda i: gc_copy(i + 1, ctx_from(2 * i + 2) // 2).wait_recv())
        each(ndp - 1, unroll=AROUND, body=lambda i: gd_copy(i + 1, dp).start())

    def send_out(a, span):
        for j in range(span[0], span[0] + span[1]):
            out_own(a, j).start()
        each(nctx - 1, unroll=AROUND, body=lambda i: out_copy(a, span, i + 1, me).start())

    def one_tile(j):
        for a in range(2):
            in_own(a, j).wait()
        for span in in_spans:

            @pl.when(j == span[0])
            def _():
                for a in range(2):
                    each(
                        nctx - 1,
                        unroll=AROUND,
                        body=lambda i: in_copy(a, span, i + 1, ctx_from(i + 1)).wait_recv(),
                    )

        def turn_in(n):
            ft[n] = arrived[0, n, :, lanes(j)].astype(jnp.float32).T
            ct[n] = arrived[1, n, :, lanes(j)].astype(jnp.float32).T

        each(nctx, turn_in, UNROLL)
        units = TILE // UNIT
        tile_terms(
            reach, nctx, ft, ct, wt.at[lanes(j), :],
            spreads.at[pl.ds(j * units, units)], out_t, in_t, fg, sg_t,
        )

        if early:

            @pl.when(j == early)
            def _():
                spread_ctx()

        def turn_out(n):
            leaving[0, n, :, lanes(j)] = out_t[n].T.astype(jnp.bfloat16)
            leaving[1, n, :, lanes(j)] = in_t[n].T.astype(jnp.bfloat16)

        each(nctx, turn_out, UNROLL)
        sums_now = row_sums(fg)
        lags = jnp.concatenate([sums_now[:, o * PANEL : (o + 1) * PANEL] for o in range(reach)], axis=0)
        shorts = sg_t[...].T[:UNIT]

        @pl.when(j < early)
        def _():
            pay[pl.ds(pl.multiple_of(j * lag_count, lag_count), lag_count)] = lags

        for place in range(early):

            @pl.when(j == place)
            def _():
                first = early * lag_count + place * 3 * TAPS
                pay[first : first + 3 * TAPS] = shorts[: 3 * TAPS]

        @pl.when(j == early - 1)
        def _():
            each(ndp - 1, unroll=AROUND, body=lambda i: rs_copy(i + 1).start())

        @pl.when(j == early)
        def _():
            halves[dp] = jnp.concatenate([lags, shorts], axis=0).astype(jnp.bfloat16)
            each(ndp - 1, unroll=AROUND, body=lambda i: zx_copy(i + 1, dp).start())

        for span in out_spans[:-1]:

            @pl.when(j == span[0] + span[1] - 1)
            def _():
                send_out(0, span)
                if span[0] + span[1] != early:
                    send_out(1, span)

        @pl.when(j == early)
        def _():
            if early:
                pass
                pass
            each(ndp - 1, unroll=AROUND, body=lambda i: zx_copy(i + 1, dp_from(i + 1)).wait_recv())
            total = halves[0].astype(jnp.float32)
            for k in range(1, ndp):
                total = total + halves[k].astype(jnp.float32)
            tail[...] = total.astype(jnp.bfloat16)
            tail_all[core, chip] = tail[...]
            each(chips - 1, unroll=AROUND, body=lambda i: gl_copy(i + 1, chip).start())
            if early:
                send_out(1, out_spans[-2])
            send_out(0, out_spans[-1])
            if early:
                spread_dp()
            send_out(1, out_spans[-1])
            each(
                chips - 1,
                unroll=AROUND,
                body=lambda i: gl_copy(i + 1, ctx_from(2 * i + 2) // 2).wait_recv(),
            )
            pair_copy(1, core).start()

    if early:
        pay[early * (lag_count + 3 * TAPS) :] = jnp.zeros(
            (pay.shape[0] - early * (lag_count + 3 * TAPS), PANEL), jnp.float32
        )
    each(tiles, one_tile)
    if early:
        each(ndp - 1, unroll=AROUND, body=lambda i: gd_copy(i + 1, dp_from(i + 1)).wait_recv())
        pair_copy(0, core).start()
    pair_copy(1, 1 - core).wait_recv()
    if early:
        pair_copy(0, 1 - core).wait_recv()
    lag_rows = [[] for _ in range(reach)]
    width_units = TILE // UNIT
    for n in range(nctx):
        if early:
            before = every[n % 2, :, n // 2].astype(jnp.float32).reshape(-1, PANEL)
        for j in range(tiles):
            if j < early:
                lags = before[j * lag_count : (j + 1) * lag_count]
                row = early * lag_count + j * 3 * TAPS
                shorts = before[row : row + 3 * TAPS]
            else:
                terms = tail_all[n % 2, n // 2].astype(jnp.float32)
                lags, shorts = terms[:lag_count], terms[lag_count : lag_count + 3 * TAPS]
            for o in range(reach):
                lag_rows[o].append(lags[o * width_units : (o + 1) * width_units])
            first = (n * tiles + j) * TILE
            for m in range(3):
                sg_all[m, :, first : first + TILE] = shorts[m * TAPS : (m + 1) * TAPS]
    lag_pos = lax.broadcasted_iota(jnp.int32, (PANEL, fg_all.shape[1]), 0)
    for o in range(reach):
        lags = jnp.concatenate(lag_rows[o], axis=0).T
        fg_all[o * PANEL : (o + 1) * PANEL] = jnp.where(lag_pos + o * PANEL < rp[...] * PANEL, lags, 0.0)
    last = [
        pltpu.make_async_copy(src, dst, last_sem.at[i])
        for i, (src, dst) in enumerate(((fg_all, fg_hbm), (sg_all, sg_hbm)))
    ]
    for one in last:
        one.start()

    def finish():
        for a in range(2):
            for span in in_spans:
                each(nctx - 1, unroll=AROUND, body=lambda i: in_copy(a, span, i + 1, me).wait_send())
            each(tiles, lambda j: out_own(a, j).wait())
            for span in out_spans:
                each(nctx - 1, unroll=AROUND, body=lambda i: out_copy(a, span, i + 1, me).wait_send())
                each(
                    nctx - 1,
                    unroll=AROUND,
                    body=lambda i: out_copy(a, span, i + 1, ctx_from(i + 1)).wait_recv(),
                )

    if early:
        each(ndp - 1, unroll=AROUND, body=lambda i: rs_copy(i + 1).wait_send())
        each(chips - 1, unroll=AROUND, body=lambda i: gc_copy(i + 1, chip).wait_send())
        each(ndp - 1, unroll=AROUND, body=lambda i: gd_copy(i + 1, dp).wait_send())
        pair_copy(0, core).wait_send()
    each(ndp - 1, unroll=AROUND, body=lambda i: zx_copy(i + 1, dp).wait_send())
    each(chips - 1, unroll=AROUND, body=lambda i: gl_copy(i + 1, chip).wait_send())
    pair_copy(1, core).wait_send()
    finish()
    for one in last:
        one.wait()


def finish_kernel(*refs):
    sem = refs[-1]
    moves = [
        pltpu.make_async_copy(src, dst, sem.at[i]) for i, (src, dst) in enumerate(zip(refs[:4], refs[4:8]))
    ]
    for one in moves:
        one.start()
    for one in moves:
        one.wait()


def shards(ndp, nctx, features, short_weights, filters, reach_panels, cotangent):
    filter_len, groups = filters.shape
    channels = features.shape[2]
    reach = filter_len // PANEL
    rows = features.shape[1]
    assert rows == PANEL and features.shape[0] == 1
    width = channels // nctx
    tiles = width // TILE
    units = width // UNIT
    tile_units = TILE // UNIT
    reach_row = reach_panels.reshape(1, groups)
    filled = reach * tile_units + UNIT
    early_rows = max(tiles - 1, 1) * (reach * tile_units + 3 * TAPS)
    chunk = -(-early_rows // (UNIT * ndp)) * UNIT
    assert nctx % 2 == 0
    hbm = pl.BlockSpec(memory_space=pltpu.HBM)
    dma = pltpu.SemaphoreType.DMA
    turned = pltpu.VMEM((nctx, TILE, PANEL), jnp.float32)
    results = [
        jax.ShapeDtypeStruct((rows, channels), jnp.bfloat16),
        jax.ShapeDtypeStruct((rows, channels), jnp.bfloat16),
        jax.ShapeDtypeStruct((filter_len, groups), jnp.float32),
        jax.ShapeDtypeStruct((3, TAPS, channels), jnp.float32),
    ]
    held = pl.pallas_call(
        functools.partial(layer_kernel, reach, ndp, nctx),
        in_specs=[hbm] * 5,
        out_specs=[hbm] * 4,
        out_shape=results,
        scratch_shapes=[
            pltpu.SemaphoreType.REGULAR,
            pltpu.SemaphoreType.REGULAR,
            pltpu.VMEM((ndp, filled, PANEL), jnp.bfloat16),
            pltpu.VMEM((filled, PANEL), jnp.bfloat16),
            pltpu.VMEM((2, nctx // 2, filled, PANEL), jnp.bfloat16),
            dma((ndp,)),
            dma((ndp,)),
            dma((nctx // 2,)),
            dma((nctx // 2,)),
            pltpu.VMEM((2, ndp, nctx // 2, chunk, PANEL), jnp.bfloat16),
            pltpu.VMEM((filter_len, groups), jnp.float32),
            pltpu.VMEM((3, TAPS, channels), jnp.float32),
            dma((2,)),
            pltpu.VMEM((3, TAPS, channels), jnp.float32),
            pltpu.VMEM((filter_len, groups), jnp.bfloat16),
            pltpu.VMEM((1, groups), jnp.int32),
            pltpu.VMEM((UNIT, PANEL), jnp.float32),
            pltpu.VMEM((width, UNIT), jnp.float32),
            pltpu.VMEM((units, filter_len), jnp.float32),
            dma((3,)),
            pltpu.VMEM((2, nctx, PANEL, width), jnp.bfloat16),
            pltpu.VMEM((2, nctx, PANEL, width), jnp.bfloat16),
            pltpu.VMEM((units, PANEL, filter_len), jnp.bfloat16),
            turned,
            turned,
            turned,
            turned,
            pltpu.VMEM((reach, tile_units * 8, PANEL), jnp.float32),
            pltpu.VMEM((TILE, PANEL), jnp.float32),
            pltpu.VMEM((ndp * chunk, PANEL), jnp.float32),
            pltpu.VMEM((ndp, chunk, PANEL), jnp.float32),
            pltpu.VMEM((chunk, PANEL), jnp.bfloat16),
            dma((2, tiles)),
            dma((2, tiles, nctx)),
            dma((2, tiles, nctx)),
            dma((2, tiles, nctx)),
            dma((2, tiles, nctx)),
            dma((2, tiles)),
            dma((ndp,)),
            dma((ndp,)),
            dma((ndp,)),
            dma((ndp,)),
            dma((nctx // 2,)),
            dma((nctx // 2,)),
            dma((2,)),
            dma((2,)),
        ],
        compiler_params=pltpu.CompilerParams(
            collective_id=0, has_side_effects=True, vmem_limit_bytes=50 * 2**20
        ),
    )(*(pltpu.with_memory_space_constraint(one, pltpu.HBM) for one in (features[0], cotangent[0], short_weights, filters, reach_row)))
    layer_out, input_grad, filter_grad, short_grad = pl.pallas_call(
        finish_kernel,
        in_specs=[pl.BlockSpec(memory_space=pltpu.VMEM)] * 4,
        out_specs=[hbm] * 4,
        out_shape=results,
        scratch_shapes=[dma((4,))],
        compiler_params=pltpu.CompilerParams(vmem_limit_bytes=8 * 2**20),
    )(*held)
    return (layer_out[None], input_grad[None], filter_grad, short_grad)


def solution(mesh):
    return jax.shard_map(
        functools.partial(shards, mesh.shape["dp"], mesh.shape["ctx"]),
        mesh=mesh,
        in_specs=(P("dp", "ctx", None), P(), P(), P(), P("dp", "ctx", None)),
        out_specs=(P("dp", "ctx", None), P("dp", "ctx", None), P(), P()),
        check_vma=False,
    )
```

```python
import functools

import jax
import jax.numpy as jnp
from jax import lax
from jax.experimental import pallas as pl
from jax.experimental.pallas import tpu as pltpu
from jax.sharding import PartitionSpec as P

PANEL = 128
UNIT = 16
TILE = 128
TAPS = 3
UNROLL = 4
AROUND = 8
IN_SIZES = (1,)
OUT_SIZES = (1,)
MESH = pl.DeviceIdType.MESH


def rows_down(x, rows):
    return jnp.concatenate([jnp.zeros((rows, x.shape[1]), x.dtype), x[:-rows]], axis=0)


def rows_up(x, rows):
    return jnp.concatenate([x[rows:], jnp.zeros((rows, x.shape[1]), x.dtype)], axis=0)


def turn(place, count):
    return jnp.where(place >= count, place - count, place)


def spans(tiles, sizes):
    found, first = [], 0
    while first < tiles:
        count = min(sizes[min(len(found), len(sizes) - 1)], tiles - first)
        found.append((first, count))
        first += count
    return found


def causal():
    shape = (PANEL, PANEL)
    return lax.broadcasted_iota(jnp.int32, shape, 1) >= lax.broadcasted_iota(jnp.int32, shape, 0)


def toeplitz(taps):
    width = taps.shape[1]
    x = jnp.broadcast_to(taps, (8, width))
    row = lax.broadcasted_iota(jnp.int32, (8, width), 0)
    for bit in (1, 2, 4):
        x = jnp.where((row & bit) != 0, pltpu.roll(x, bit, 1), x)
    rows = 8
    while rows < PANEL:
        x = jnp.concatenate([x, pltpu.roll(x, rows, 1)], axis=0)
        rows *= 2
    first = jnp.where(causal(), x[:, :PANEL], 0.0)
    return jnp.concatenate([first, x[:, PANEL:]], axis=1).astype(jnp.bfloat16)


def lag_sums(products):
    width = products.shape[1]
    first = jnp.where(causal(), products[:, :PANEL], 0.0)
    x = jnp.concatenate([first, products[:, PANEL:]], axis=1)
    rows = PANEL // 2
    while rows >= 8:
        x = x[:rows] + pltpu.roll(x[rows:], width - rows, 1)
        rows //= 2
    return x


def row_sums(partial):
    reach = partial.shape[0]
    total = None
    for row in range(8):
        picked = pl.ds(row, TILE // UNIT, stride=8)
        x = jnp.concatenate([partial.at[o][picked, :] for o in range(reach)], axis=1)
        total = x if total is None else total + pltpu.roll(x, reach * PANEL - row, 1)
    return total


def tile_terms(reach, panels, ft, ct, wt, spreads, out_t, in_t, fg, sg_t):
    rows = panels * UNIT

    def group(g, carry):
        first = pl.multiple_of(g * UNIT, UNIT)
        lane = lax.broadcasted_iota(jnp.int32, (rows, PANEL), 1)
        chan = pl.ds(first, UNIT)
        feat = ft[:, chan, :].reshape(rows, PANEL)
        cot = ct[:, chan, :].reshape(rows, PANEL)
        w_all = wt[chan, :]

        def weigh(k, x):
            w = jnp.broadcast_to(w_all[:, k : k + 1], (UNIT, PANEL))
            return (x.reshape(panels, UNIT, PANEL) * w[None]).reshape(rows, PANEL)

        feats = [feat]
        for tap in range(1, TAPS):
            turned = pltpu.roll(feat, tap, 1)
            feats.append(jnp.where(lane < tap, rows_down(turned, UNIT), turned))
        streams = []
        for m in range(3):
            total = weigh(m * TAPS, feats[0])
            for tap in range(1, TAPS):
                total = total + weigh(m * TAPS + tap, feats[tap])
            streams.append(total)
        query, key, value = streams
        mixed = (key * value).astype(jnp.bfloat16)
        grad_conv = (cot * query).astype(jnp.bfloat16)
        earlier = jnp.concatenate(
            [mixed] + [rows_down(mixed, o * UNIT) for o in range(1, reach)], axis=1
        )
        later = jnp.concatenate(
            [grad_conv] + [rows_up(grad_conv, o * UNIT) for o in range(1, reach)], axis=1
        )
        spread = spreads[g]
        stacked = jnp.concatenate(
            [spread[:, o * PANEL : (o + 1) * PANEL] for o in range(reach)], axis=0
        )
        conv = jnp.dot(earlier, stacked, preferred_element_type=jnp.float32)
        back = lax.dot_general(
            later, spread, (((1,), (1,)), ((), ())), preferred_element_type=jnp.float32
        )
        products = lax.dot_general(
            mixed, later, (((0,), (0,)), ((), ())), preferred_element_type=jnp.float32
        )
        lags = lag_sums(products)
        for o in range(reach):
            fg[o, pl.ds(pl.multiple_of(g * 8, 8), 8), :] = lags[:, o * PANEL : (o + 1) * PANEL]
        out_t[:, chan, :] = (query * conv).reshape(panels, UNIT, PANEL)
        grads = (cot * conv, back * value, back * key)
        grad_in = None
        for tap in range(TAPS):
            part = weigh(tap, grads[0]) + weigh(TAPS + tap, grads[1]) + weigh(2 * TAPS + tap, grads[2])
            if tap:
                turned = pltpu.roll(part, PANEL - tap, 1)
                part = jnp.where(lane >= PANEL - tap, rows_up(turned, UNIT), turned)
            grad_in = part if grad_in is None else grad_in + part
        in_t[:, chan, :] = grad_in.reshape(panels, UNIT, PANEL)
        small_lane = lax.broadcasted_iota(jnp.int32, (UNIT, PANEL), 1)
        parts = jnp.concatenate(
            [
                jnp.sum((grads[m] * feats[tap]).reshape(panels, UNIT, PANEL), axis=0)
                for m in range(3)
                for tap in range(TAPS)
            ],
            axis=0,
        )
        high = parts.astype(jnp.bfloat16)
        low = (parts - high.astype(jnp.float32)).astype(jnp.bfloat16)
        ones = jnp.ones((PANEL, PANEL), jnp.bfloat16)
        added = jnp.dot(high, ones, preferred_element_type=jnp.float32) + jnp.dot(
            low, ones, preferred_element_type=jnp.float32
        )
        sums = jnp.zeros((UNIT, PANEL), jnp.float32)
        for k in range(3 * TAPS):
            sums = jnp.where(small_lane == k, added[k * UNIT : (k + 1) * UNIT], sums)
        sg_t[chan, :] = sums
        return carry

    lax.fori_loop(0, TILE // UNIT, group, 0, unroll=UNROLL)


def layer_kernel(
    reach, ndp, nctx, f_hbm, c_hbm, sw_hbm, fl_hbm, rp_hbm, out_hbm, in_hbm, fg_hbm, sg_hbm,
    near, far, halves, tail, tail_all, zx_send, zx_recv, gl_send, gl_recv,
    every, fg_all, sg_all, last_sem, sw, fl, rp, wrow, wt, taps, small_sem, arrived, leaving, spreads, ft, ct, out_t, in_t, fg, sg_t, pay, parts, sums,
    own_sem, in_send, in_recv, out_send, out_recv, keep_sem,
    rs_send, rs_recv, gd_send, gd_recv, gc_send, gc_recv, pair_send, pair_recv,
):
    dp, me = lax.axis_index("dp"), lax.axis_index("ctx")
    width = arrived.shape[3]
    tiles = width // TILE
    chunk, filled = sums.shape[0], tail.shape[0]
    core, chip, chips = lax.rem(me, 2), me // 2, nctx // 2
    lag_count = reach * (TILE // UNIT)
    early = tiles - 1
    ins, outs = (f_hbm, c_hbm), (out_hbm, in_hbm)

    def ctx_peer(k):
        return turn(me + k, nctx)

    def ctx_from(k):
        return turn(me + nctx - k, nctx)

    def dp_peer(k):
        return turn(dp + k, ndp)

    def dp_from(k):
        return turn(dp + ndp - k, ndp)

    in_spans, out_spans = spans(tiles, IN_SIZES), spans(tiles, OUT_SIZES)

    def lanes(j, count=1):
        return pl.ds(pl.multiple_of(j * TILE, TILE), count * TILE)

    def cols(owner, j, count=1):
        return pl.ds(pl.multiple_of(owner * width + j * TILE, TILE), count * TILE)

    def copy(src, dst, send, recv, device):
        return pltpu.make_async_remote_copy(
            src_ref=src, dst_ref=dst, send_sem=send, recv_sem=recv, device_id=device, device_id_type=MESH
        )

    def in_copy(a, span, k, slot):
        j, count = span
        return copy(
            ins[a].at[:, cols(ctx_peer(k), j, count)],
            arrived.at[a, slot, :, lanes(j, count)],
            in_send.at[a, j, k],
            in_recv.at[a, j, k],
            (dp, ctx_peer(k)),
        )

    def in_own(a, j):
        return pltpu.make_async_copy(
            ins[a].at[:, cols(me, j)], arrived.at[a, me, :, lanes(j)], own_sem.at[a, j]
        )

    def out_copy(a, span, k, slot):
        j, count = span
        return copy(
            leaving.at[a, ctx_peer(k), :, lanes(j, count)],
            outs[a].at[:, cols(slot, j, count)],
            out_send.at[a, j, k],
            out_recv.at[a, j, k],
            (dp, ctx_peer(k)),
        )

    def out_own(a, j):
        return pltpu.make_async_copy(
            leaving.at[a, me, :, lanes(j)], outs[a].at[:, cols(me, j)], keep_sem.at[a, j]
        )

    def rs_copy(k):
        part = pl.ds(pl.multiple_of(dp_peer(k) * chunk, chunk), chunk)
        return copy(pay.at[part], parts.at[k], rs_send.at[k], rs_recv.at[k], (dp_peer(k), me))

    def gc_copy(k, slot):
        return copy(sums, every.at[core, dp, slot], gc_send.at[k], gc_recv.at[k], (dp, ctx_peer(2 * k)))

    def gd_copy(k, slot):
        return copy(
            every.at[core, dp], every.at[core, slot], gd_send.at[k], gd_recv.at[k], (dp_peer(k), me)
        )

    def zx_copy(k, slot):
        return copy(halves.at[dp], halves.at[slot], zx_send.at[k], zx_recv.at[k], (dp_peer(k), me))

    def gl_copy(k, slot):
        return copy(tail, tail_all.at[core, slot], gl_send.at[k], gl_recv.at[k], (dp, ctx_peer(2 * k)))

    def pair_copy(i, which):
        ref = (every, tail_all)[i]
        return copy(
            ref.at[which], ref.at[which], pair_send.at[i], pair_recv.at[i], (dp, me + 1 - 2 * core)
        )

    def each(count, body, unroll=1):
        if count < 1:
            return
        unroll = max(1, min(unroll, count))

        def step(i, carry):
            body(i)
            return carry

        lax.fori_loop(0, count, step, 0, unroll=unroll)

    barrier = pltpu.get_barrier_semaphore()
    others = [ctx_peer(k) for k in range(1, nctx)]
    for other in others:

        @pl.when(other != 0)
        def _():
            pl.semaphore_signal(barrier, inc=1, device_id=(dp, other), device_id_type=MESH)

    small = [
        pltpu.make_async_copy(src, dst, small_sem.at[i])
        for i, (src, dst) in enumerate(((sw_hbm, sw), (fl_hbm, fl), (rp_hbm, rp)))
    ]
    for one in small:
        one.start()
    for a in range(2):
        each(tiles, lambda j: in_own(a, j).start())

    @pl.when(me != 0)
    def _():
        pl.semaphore_wait(barrier, nctx - 1)
        pl.semaphore_signal(near, inc=1, device_id=(dp, 0), device_id_type=MESH)

    @pl.when(me == 0)
    def _():
        pl.semaphore_wait(near, nctx - 1)
        for k in range(1, ndp):
            pl.semaphore_signal(barrier, inc=1, device_id=(dp_peer(k), 0), device_id_type=MESH)

    for span in in_spans[:3]:
        for a in range(2):
            each(nctx - 1, unroll=AROUND, body=lambda i: in_copy(a, span, i + 1, me).start())
    for one in small:
        one.wait()
    units = taps.shape[0]
    group = me * units
    block = pl.ds(pl.multiple_of(group // PANEL * PANEL, PANEL), PANEL)
    lag_pos = lax.broadcasted_iota(jnp.int32, (fl.shape[0], PANEL), 0)
    masked = jnp.where(lag_pos < rp[:, block] * PANEL, fl[:, block].astype(jnp.float32), 0.0)
    masked = pltpu.roll(masked, lax.rem(PANEL - lax.rem(group, PANEL), PANEL), 1)
    for o in range(reach):
        taps[:, o * PANEL : (o + 1) * PANEL] = masked[o * PANEL : (o + 1) * PANEL].T[:units]
    wrow[...] = jnp.zeros_like(wrow)

    def turn_weights(j):
        for m in range(3):
            wrow[m * TAPS : (m + 1) * TAPS] = sw[m, :, cols(me, j)]
        wt[lanes(j), :] = wrow[...].T

    each(tiles, turn_weights)

    def build(g):
        spreads[g] = toeplitz(taps[pl.ds(g, 1), :])

    each(taps.shape[0], build, UNROLL)

    @pl.when(me == 0)
    def _():
        pl.semaphore_wait(barrier, ndp - 1)
        for other in others:
            pl.semaphore_signal(far, inc=1, device_id=(dp, other), device_id_type=MESH)

    @pl.when(me != 0)
    def _():
        pl.semaphore_wait(far, 1)

    def spread_ctx():
        each(ndp - 1, unroll=AROUND, body=lambda i: rs_copy(i + 1).wait_recv())
        total = pay[pl.ds(pl.multiple_of(dp * chunk, chunk), chunk)]
        for k in range(1, ndp):
            total = total + parts[k]
        sums[...] = total.astype(jnp.bfloat16)
        every[core, dp, chip] = sums[...]
        each(chips - 1, unroll=AROUND, body=lambda i: gc_copy(i + 1, chip).start())

    def spread_dp():
        each(chips - 1, unroll=AROUND, body=lambda i: gc_copy(i + 1, ctx_from(2 * i + 2) // 2).wait_recv())
        each(ndp - 1, unroll=AROUND, body=lambda i: gd_copy(i + 1, dp).start())

    def send_out(a, span):
        for j in range(span[0], span[0] + span[1]):
            out_own(a, j).start()
        each(nctx - 1, unroll=AROUND, body=lambda i: out_copy(a, span, i + 1, me).start())

    def one_tile(j):
        for a in range(2):
            in_own(a, j).wait()
        for span in in_spans:

            @pl.when(j == span[0])
            def _():
                for a in range(2):
                    each(
                        nctx - 1,
                        unroll=AROUND,
                        body=lambda i: in_copy(a, span, i + 1, ctx_from(i + 1)).wait_recv(),
                    )

        for span in in_spans[3:]:

            @pl.when(j == span[0] - 3)
            def _():
                for a in range(2):
                    each(nctx - 1, unroll=AROUND, body=lambda i: in_copy(a, span, i + 1, me).start())

        def turn_in(n):
            ft[n] = arrived[0, n, :, lanes(j)].astype(jnp.float32).T
            ct[n] = arrived[1, n, :, lanes(j)].astype(jnp.float32).T

        each(nctx, turn_in, UNROLL)
        units = TILE // UNIT
        tile_terms(
            reach, nctx, ft, ct, wt.at[lanes(j), :],
            spreads.at[pl.ds(j * units, units)], out_t, in_t, fg, sg_t,
        )

        def turn_out(n):
            leaving[0, n, :, lanes(j)] = out_t[n].T.astype(jnp.bfloat16)
            leaving[1, n, :, lanes(j)] = in_t[n].T.astype(jnp.bfloat16)

        each(nctx, turn_out, UNROLL)
        sums_now = row_sums(fg)
        lags = jnp.concatenate([sums_now[:, o * PANEL : (o + 1) * PANEL] for o in range(reach)], axis=0)
        shorts = sg_t[...].T[:UNIT]

        @pl.when(j < early)
        def _():
            pay[pl.ds(pl.multiple_of(j * lag_count, lag_count), lag_count)] = lags

        for place in range(early):

            @pl.when(j == place)
            def _():
                first = early * lag_count + place * 3 * TAPS
                pay[first : first + 3 * TAPS] = shorts[: 3 * TAPS]

        @pl.when(j == early - 1)
        def _():
            each(ndp - 1, unroll=AROUND, body=lambda i: rs_copy(i + 1).start())

        @pl.when(j == early)
        def _():
            halves[dp] = jnp.concatenate([lags, shorts], axis=0).astype(jnp.bfloat16)
            each(ndp - 1, unroll=AROUND, body=lambda i: zx_copy(i + 1, dp).start())

        for span in out_spans[:-1]:

            @pl.when(j == span[0] + span[1] - 1)
            def _():
                send_out(0, span)
                if span[0] + span[1] != early:
                    send_out(1, span)

        @pl.when(j == early)
        def _():
            if early:
                spread_ctx()
                if out_spans[-1][0] == early:
                    send_out(1, out_spans[-2])
            each(ndp - 1, unroll=AROUND, body=lambda i: zx_copy(i + 1, dp_from(i + 1)).wait_recv())
            total = halves[0].astype(jnp.float32)
            for k in range(1, ndp):
                total = total + halves[k].astype(jnp.float32)
            tail[...] = total.astype(jnp.bfloat16)
            tail_all[core, chip] = tail[...]
            each(chips - 1, unroll=AROUND, body=lambda i: gl_copy(i + 1, chip).start())
            send_out(0, out_spans[-1])
            if early:
                spread_dp()
            send_out(1, out_spans[-1])
            each(
                chips - 1,
                unroll=AROUND,
                body=lambda i: gl_copy(i + 1, ctx_from(2 * i + 2) // 2).wait_recv(),
            )
            pair_copy(1, core).start()

    if early:
        pay[early * (lag_count + 3 * TAPS) :] = jnp.zeros(
            (pay.shape[0] - early * (lag_count + 3 * TAPS), PANEL), jnp.float32
        )
    each(tiles, one_tile)
    if early:
        each(ndp - 1, unroll=AROUND, body=lambda i: gd_copy(i + 1, dp_from(i + 1)).wait_recv())
        pair_copy(0, core).start()
    pair_copy(1, 1 - core).wait_recv()
    if early:
        pair_copy(0, 1 - core).wait_recv()
    lag_rows = [[] for _ in range(reach)]
    width_units = TILE // UNIT
    for n in range(nctx):
        if early:
            before = every[n % 2, :, n // 2].astype(jnp.float32).reshape(-1, PANEL)
        for j in range(tiles):
            if j < early:
                lags = before[j * lag_count : (j + 1) * lag_count]
                row = early * lag_count + j * 3 * TAPS
                shorts = before[row : row + 3 * TAPS]
            else:
                terms = tail_all[n % 2, n // 2].astype(jnp.float32)
                lags, shorts = terms[:lag_count], terms[lag_count : lag_count + 3 * TAPS]
            for o in range(reach):
                lag_rows[o].append(lags[o * width_units : (o + 1) * width_units])
            first = (n * tiles + j) * TILE
            for m in range(3):
                sg_all[m, :, first : first + TILE] = shorts[m * TAPS : (m + 1) * TAPS]
    lag_pos = lax.broadcasted_iota(jnp.int32, (PANEL, fg_all.shape[1]), 0)
    for o in range(reach):
        lags = jnp.concatenate(lag_rows[o], axis=0).T
        fg_all[o * PANEL : (o + 1) * PANEL] = jnp.where(lag_pos + o * PANEL < rp[...] * PANEL, lags, 0.0)
    last = [
        pltpu.make_async_copy(src, dst, last_sem.at[i])
        for i, (src, dst) in enumerate(((fg_all, fg_hbm), (sg_all, sg_hbm)))
    ]
    for one in last:
        one.start()

    def finish():
        for a in range(2):
            for span in in_spans:
                each(nctx - 1, unroll=AROUND, body=lambda i: in_copy(a, span, i + 1, me).wait_send())
            each(tiles, lambda j: out_own(a, j).wait())
            for span in out_spans:
                each(nctx - 1, unroll=AROUND, body=lambda i: out_copy(a, span, i + 1, me).wait_send())
                each(
                    nctx - 1,
                    unroll=AROUND,
                    body=lambda i: out_copy(a, span, i + 1, ctx_from(i + 1)).wait_recv(),
                )

    if early:
        each(ndp - 1, unroll=AROUND, body=lambda i: rs_copy(i + 1).wait_send())
        each(chips - 1, unroll=AROUND, body=lambda i: gc_copy(i + 1, chip).wait_send())
        each(ndp - 1, unroll=AROUND, body=lambda i: gd_copy(i + 1, dp).wait_send())
        pair_copy(0, core).wait_send()
    each(ndp - 1, unroll=AROUND, body=lambda i: zx_copy(i + 1, dp).wait_send())
    each(chips - 1, unroll=AROUND, body=lambda i: gl_copy(i + 1, chip).wait_send())
    pair_copy(1, core).wait_send()
    finish()
    for one in last:
        one.wait()


def finish_kernel(*refs):
    sem = refs[-1]
    moves = [
        pltpu.make_async_copy(src, dst, sem.at[i]) for i, (src, dst) in enumerate(zip(refs[:4], refs[4:8]))
    ]
    for one in moves:
        one.start()
    for one in moves:
        one.wait()


def shards(ndp, nctx, features, short_weights, filters, reach_panels, cotangent):
    filter_len, groups = filters.shape
    channels = features.shape[2]
    reach = filter_len // PANEL
    rows = features.shape[1]
    assert rows == PANEL and features.shape[0] == 1
    width = channels // nctx
    tiles = width // TILE
    units = width // UNIT
    tile_units = TILE // UNIT
    reach_row = reach_panels.reshape(1, groups)
    filled = reach * tile_units + UNIT
    early_rows = max(tiles - 1, 1) * (reach * tile_units + 3 * TAPS)
    chunk = -(-early_rows // (UNIT * ndp)) * UNIT
    assert nctx % 2 == 0
    hbm = pl.BlockSpec(memory_space=pltpu.HBM)
    dma = pltpu.SemaphoreType.DMA
    turned = pltpu.VMEM((nctx, TILE, PANEL), jnp.float32)
    results = [
        jax.ShapeDtypeStruct((rows, channels), jnp.bfloat16),
        jax.ShapeDtypeStruct((rows, channels), jnp.bfloat16),
        jax.ShapeDtypeStruct((filter_len, groups), jnp.float32),
        jax.ShapeDtypeStruct((3, TAPS, channels), jnp.float32),
    ]
    held = pl.pallas_call(
        functools.partial(layer_kernel, reach, ndp, nctx),
        in_specs=[hbm] * 5,
        out_specs=[hbm] * 4,
        out_shape=results,
        scratch_shapes=[
            pltpu.SemaphoreType.REGULAR,
            pltpu.SemaphoreType.REGULAR,
            pltpu.VMEM((ndp, filled, PANEL), jnp.bfloat16),
            pltpu.VMEM((filled, PANEL), jnp.bfloat16),
            pltpu.VMEM((2, nctx // 2, filled, PANEL), jnp.bfloat16),
            dma((ndp,)),
            dma((ndp,)),
            dma((nctx // 2,)),
            dma((nctx // 2,)),
            pltpu.VMEM((2, ndp, nctx // 2, chunk, PANEL), jnp.bfloat16),
            pltpu.VMEM((filter_len, groups), jnp.float32),
            pltpu.VMEM((3, TAPS, channels), jnp.float32),
            dma((2,)),
            pltpu.VMEM((3, TAPS, channels), jnp.float32),
            pltpu.VMEM((filter_len, groups), jnp.bfloat16),
            pltpu.VMEM((1, groups), jnp.int32),
            pltpu.VMEM((UNIT, PANEL), jnp.float32),
            pltpu.VMEM((width, UNIT), jnp.float32),
            pltpu.VMEM((units, filter_len), jnp.float32),
            dma((3,)),
            pltpu.VMEM((2, nctx, PANEL, width), jnp.bfloat16),
            pltpu.VMEM((2, nctx, PANEL, width), jnp.bfloat16),
            pltpu.VMEM((units, PANEL, filter_len), jnp.bfloat16),
            turned,
            turned,
            turned,
            turned,
            pltpu.VMEM((reach, tile_units * 8, PANEL), jnp.float32),
            pltpu.VMEM((TILE, PANEL), jnp.float32),
            pltpu.VMEM((ndp * chunk, PANEL), jnp.float32),
            pltpu.VMEM((ndp, chunk, PANEL), jnp.float32),
            pltpu.VMEM((chunk, PANEL), jnp.bfloat16),
            dma((2, tiles)),
            dma((2, tiles, nctx)),
            dma((2, tiles, nctx)),
            dma((2, tiles, nctx)),
            dma((2, tiles, nctx)),
            dma((2, tiles)),
            dma((ndp,)),
            dma((ndp,)),
            dma((ndp,)),
            dma((ndp,)),
            dma((nctx // 2,)),
            dma((nctx // 2,)),
            dma((2,)),
            dma((2,)),
        ],
        compiler_params=pltpu.CompilerParams(
            collective_id=0, has_side_effects=True, vmem_limit_bytes=50 * 2**20
        ),
    )(*(pltpu.with_memory_space_constraint(one, pltpu.HBM) for one in (features[0], cotangent[0], short_weights, filters, reach_row)))
    layer_out, input_grad, filter_grad, short_grad = pl.pallas_call(
        finish_kernel,
        in_specs=[pl.BlockSpec(memory_space=pltpu.VMEM)] * 4,
        out_specs=[hbm] * 4,
        out_shape=results,
        scratch_shapes=[dma((4,))],
        compiler_params=pltpu.CompilerParams(vmem_limit_bytes=8 * 2**20),
    )(*held)
    return (layer_out[None], input_grad[None], filter_grad, short_grad)


def solution(mesh):
    return jax.shard_map(
        functools.partial(shards, mesh.shape["dp"], mesh.shape["ctx"]),
        mesh=mesh,
        in_specs=(P("dp", "ctx", None), P(), P(), P(), P("dp", "ctx", None)),
        out_specs=(P("dp", "ctx", None), P("dp", "ctx", None), P(), P()),
        check_vma=False,
    )
```
